32 devices in a mesh: fsdp: 2 (over x), ctx: 8 (over z, y), tp: 2 (over core).
Axes of the slice: x: 2, y: 2, z: 4, core: 2. Of those that a mesh axis runs over, the one named last changes fastest.
Arguments:
- tokens: bfloat16 [2, 2, 4096, 768], P(None, 'fsdp', 'ctx'), may hold values from -6 to 6
- segments: int32 [2, 2, 4096], P(None, 'fsdp', 'ctx'), may hold values from 0 to 23, never falling along the last dimension, each value on 1 to 2048 neighbouring positions
- query_weight: bfloat16 [768, 768], P(('fsdp', 'ctx'), 'tp'), may hold values from -0.21875 to 0.21875
- query_bias: float32 [768], P('tp'), may hold values from -3 to 3
- key_weight: bfloat16 [768, 64], P(('fsdp', 'ctx')), may hold values from -0.21875 to 0.21875
- key_bias: float32 [64], replicated, may hold values from -3 to 3
- value_weight: bfloat16 [768, 64], P(('fsdp', 'ctx')), may hold values from -0.21875 to 0.21875
- value_bias: float32 [64], replicated, may hold values from -3 to 3
- output_weight: bfloat16 [768, 768], P('tp', ('fsdp', 'ctx')), may hold values from -1.75 to 1.75
- output_bias: float32 [768], replicated, may hold values from -4 to 4
- upward_weight: bfloat16 [768, 3072], P(('fsdp', 'ctx'), 'tp'), may hold values from -0.21875 to 0.21875
- upward_bias: float32 [3072], P('tp'), may hold values from -3 to 3
- down_weight: bfloat16 [3072, 768], P('tp', ('fsdp', 'ctx')), may hold values from -0.109375 to 0.109375
- down_bias: float32 [768], replicated, may hold values from -4 to 4
- attend_gain: float32 [768], replicated, may hold values from 0.25 to 1.75
- attend_bias: float32 [768], replicated, may hold values from -2 to 2
- dense_gain: float32 [768], replicated, may hold values from 0.25 to 1.75
- dense_bias: float32 [768], replicated, may hold values from -2 to 2
- cotangent: bfloat16 [2, 2, 4096, 768], P(None, 'fsdp', 'ctx'), may hold values from -6 to 6
Outputs:
- result: bfloat16 [2, 2, 4096, 768], P(None, 'fsdp', 'ctx')
- tokens_grad: bfloat16 [2, 2, 4096, 768], P(None, 'fsdp', 'ctx')
- query_weight_grad: float32 [768, 768], P(('fsdp', 'ctx'), 'tp')
- query_bias_grad: float32 [768], P('tp')
- key_weight_grad: float32 [768, 64], P(('fsdp', 'ctx'))
- key_bias_grad: float32 [64], replicated
- value_weight_grad: float32 [768, 64], P(('fsdp', 'ctx'))
- value_bias_grad: float32 [64], replicated
- output_weight_grad: float32 [768, 768], P('tp', ('fsdp', 'ctx'))
- output_bias_grad: float32 [768], replicated
- upward_weight_grad: float32 [768, 3072], P(('fsdp', 'ctx'), 'tp')
- upward_bias_grad: float32 [3072], P('tp')
- down_weight_grad: float32 [3072, 768], P('tp', ('fsdp', 'ctx'))
- down_bias_grad: float32 [768], replicated
- attend_gain_grad: float32 [768], replicated
- attend_bias_grad: float32 [768], replicated
- dense_gain_grad: float32 [768], replicated
- dense_bias_grad: float32 [768], replicated
The draws below stay inside these ranges and needn't reach their ends.
Inputs may be any that keep to these rules, and one draw needn't show every extreme that they name: `segments`: within each sequence of 4096 tokens segment numbers never fall; each of the 24 numbers is used by 1 to 2048 tokens, one by exactly 2048.
All inputs are finite; a program needn't handle non-finite values.
Results may differ from the reference program's by a relative error of at most 0.04.
Values may be sent and summed in bfloat16 or wider, within the bound.
No kernel may reach another device: no remote copies, remote signals or barrier semaphores. Data moves between devices by JAX's collectives and lax.ppermute only.
A program may use at most 128 MiB of HBM per device.

```python
import math
import jax
import jax.numpy as jnp
import numpy as np
from jax import lax

D = 768
HEADS = 12
HEAD = 64
ROT = 16
FF = 3072
MICRO = 2
DOCS = 24
LEN = 4096
BATCH = 2


def raised(values, stream_key, source, target, shards_of, factor):
    owner, partner = [(jnp.arange(values.shape[axis_at]) // (values.shape[axis_at] // shards_of)).reshape([-1 if axis == axis_at else 1 for axis in range(values.ndim)]) for axis_at in (source, target)]
    chosen = jax.random.permutation(stream_key, shards_of)[partner]
    strong = (owner == chosen) | (owner == (partner + shards_of // 2) % shards_of)
    return jnp.where(strong, factor * values, values)


def block_levels(key, dims, cuts, least, largest):
    def one(axis_at, blocks):
        heights = jax.random.uniform(jax.random.fold_in(jax.random.fold_in(key, 6), axis_at), (blocks,), jnp.float32, least / len(cuts), largest / len(cuts))
        return jnp.repeat(jnp.exp(heights), dims[axis_at] // blocks).reshape((-1,) + (1,) * (len(dims) - axis_at - 1))

    loudness = one(*cuts[0])
    for cut in cuts[1:]:
        loudness = loudness * one(*cut)
    return loudness


def profile(amount, total, limit, slope):
    weights = [(1 << 20) // math.isqrt(rank ** slope) + 1 for rank in range(2, amount + 1)]
    spare, counts = total - limit - (amount - 1), [1] * (amount - 1)
    while spare > 0:
        candidates = [i for i in range(amount - 1) if counts[i] < limit]
        mass, budget = sum([weights[i] for i in candidates]), spare
        for i in candidates:
            extra = min(limit - counts[i], max(1, budget * weights[i] // mass), spare)
            counts[i] = counts[i] + extra
            spare = spare - extra
    return np.array([limit] + counts)


def uneven_parts(own_key, number_of, total, bound, lean):
    if number_of == 2:
        one = jax.random.randint(own_key, (), max(1, total - bound), min(bound, total - 1) + 1)
        return jnp.stack([one, total - one])
    tallies = jnp.asarray(profile(number_of, total, bound, lean), jnp.int32)
    couples = (number_of - 1) // 2
    giver, sink = tallies[1:1 + 2 * couples:2], tallies[2:2 + 2 * couples:2]
    room = jnp.minimum(giver - 1, bound - sink)
    moved = jax.random.randint(jax.random.fold_in(own_key, 1), (couples,), 0, 1 << 20) % (room + 1)
    tallies = tallies.at[1:1 + 2 * couples:2].set(giver - moved).at[2:2 + 2 * couples:2].set(sink + moved)
    return tallies[jax.random.permutation(jax.random.fold_in(own_key, 2), number_of)]


def scatter_about(own_key, extent, scale, most, cuts=(), held_as=jnp.bfloat16):
    level = block_levels(own_key, extent, cuts, -0.22, 0.18) if cuts else 1.0
    drawn = jax.random.normal(own_key, extent, jnp.float32) * scale * level
    return jnp.minimum(jnp.maximum(drawn, -most), most).astype(held_as)


def noise_with(key, shape, scale, limit, split, heavy, kind=jnp.bfloat16):
    result = scale * jax.random.normal(key, shape, jnp.float32)
    if split:
        result = result * block_levels(key, shape, split, -0.22, 0.18)
    return jnp.clip(raised(result, jax.random.fold_in(key, 3), *heavy), -limit, limit).astype(kind)


def setup_inputs(seed: int = 0) -> dict:
    splits = jax.random.split(jax.random.key(seed), 20)
    tokens = scatter_about(splits[0], (MICRO, BATCH, LEN, D), 1.0, 6.0, ((1, 2), (2, 8)))
    segments = jax.vmap(lambda own: jnp.searchsorted(jnp.cumsum(uneven_parts(own, DOCS, LEN, LEN // 2, 2)), jnp.arange(LEN), side="right"))(jax.random.split(splits[1], MICRO * BATCH)).reshape((MICRO, BATCH, LEN)).astype(jnp.int32)
    query_weight = scatter_about(splits[2], (D, HEADS * HEAD), D ** -0.5, 0.21875, ((0, 16), (1, 2)))
    query_bias = scatter_about(splits[3], (HEADS * HEAD,), 0.5, 3.0, ((0, 2),), jnp.float32)
    key_weight = scatter_about(splits[4], (D, HEAD), D ** -0.5, 0.21875, ((0, 16),))
    key_bias = scatter_about(splits[5], (HEAD,), 0.5, 3.0, (), jnp.float32)
    value_weight = scatter_about(splits[6], (D, HEAD), D ** -0.5, 0.21875, ((0, 16),))
    value_bias = scatter_about(splits[7], (HEAD,), 0.5, 3.0, (), jnp.float32)
    output_weight = scatter_about(splits[8], (HEADS * HEAD, D), (HEADS * HEAD // 64) ** -0.5, 1.75, ((0, 2), (1, 16)))
    output_bias = scatter_about(splits[9], (D,), 1.0, 4.0, (), jnp.float32)
    upward_weight = scatter_about(splits[10], (D, FF), D ** -0.5, 0.21875, ((0, 16), (1, 2)))
    upward_bias = scatter_about(splits[11], (FF,), 0.5, 3.0, ((0, 2),), jnp.float32)
    down_weight = scatter_about(splits[12], (FF, D), FF ** -0.5, 0.109375, ((0, 2), (1, 16)))
    down_bias = scatter_about(splits[13], (D,), 1.0, 4.0, (), jnp.float32)
    attend_gain = jnp.clip(1.0 + 0.15 * jax.random.normal(splits[14], (D,), jnp.float32), 0.25, 1.75)
    attend_bias = scatter_about(splits[15], (D,), 0.3, 2.0, (), jnp.float32)
    dense_gain = jnp.clip(1.0 + 0.15 * jax.random.normal(splits[16], (D,), jnp.float32), 0.25, 1.75)
    dense_bias = scatter_about(splits[17], (D,), 0.3, 2.0, (), jnp.float32)
    cotangent = noise_with(splits[18], (MICRO, BATCH, LEN, D), 1.0, 6.0, ((1, 2), (2, 8)), (2, 3, 8, 2.0))
    return {"tokens": tokens, "segments": segments, "query_weight": query_weight, "query_bias": query_bias, "key_weight": key_weight, "key_bias": key_bias, "value_weight": value_weight, "value_bias": value_bias, "output_weight": output_weight, "output_bias": output_bias, "upward_weight": upward_weight, "upward_bias": upward_bias, "down_weight": down_weight, "down_bias": down_bias, "attend_gain": attend_gain, "attend_bias": attend_bias, "dense_gain": dense_gain, "dense_bias": dense_bias, "cotangent": cotangent}


NEGATIVE = -1e+30
EPSILON = 1e-05

@jax.custom_vjp
def low(v):
    return lax.optimization_barrier(v.astype(jnp.bfloat16)).astype(jnp.float32)

@jax.custom_vjp
def low_back(v):
    return v

def low_keep(v):
    return (low(v), None)

def low_pass(kept, grad):
    return (grad,)

def back_keep(v):
    return (v, None)

def back_low(kept, grad):
    return (low(grad),)
low.defvjp(low_keep, low_pass)
low_back.defvjp(back_keep, back_low)

def matmul(left, right):
    return jnp.dot(left, right, precision=lax.Precision.HIGHEST, preferred_element_type=jnp.float32)

def layer_norm(values, gain, shift):
    centre = values - lax.optimization_barrier(jnp.mean(values, axis=-1, keepdims=True))
    spread = lax.rsqrt(lax.optimization_barrier(jnp.mean(centre * centre, axis=-1, keepdims=True)) + EPSILON)
    return centre * spread * gain + shift

def rotary_tables(positions):
    freqs = jnp.exp(jnp.arange(ROT // 2, dtype=jnp.float32) * (-2.0 * math.log(10000.0) / ROT))
    angle = positions.astype(jnp.float32)[:, None] * freqs[None, :]
    return (jnp.cos(angle), jnp.sin(angle))

def rotate(values, cosine, sine):
    half = ROT // 2
    first = values[..., :half]
    second = values[..., half:ROT]
    return jnp.concatenate([first * cosine - second * sine, second * cosine + first * sine, values[..., ROT:]], axis=-1)

def attend(query, keys, values, segment, index):
    length = query.shape[0]
    block = math.gcd(length, 256)
    starts = jnp.arange(length // block, dtype=jnp.int32) * block
    blocks = query.reshape(length // block, block, HEADS, HEAD)
    scale = HEAD ** (-0.5)

    def one_block(item):
        rows, begin = item
        row_index = begin + jnp.arange(block, dtype=jnp.int32)
        row_segment = lax.dynamic_slice_in_dim(segment, begin, block)
        scores = low_back(scale * jnp.einsum('qhd,kd->qhk', rows, keys, precision=lax.Precision.HIGHEST))
        allowed = ((row_segment[:, None] == segment[None, :]) & (index[None, :] <= row_index[:, None]))[:, None, :]
        probs = low(jax.nn.softmax(jnp.where(allowed, scores, NEGATIVE), axis=-1))
        return jnp.einsum('qhk,kd->qhd', probs, values, precision=lax.Precision.HIGHEST)
    return lax.map(jax.checkpoint(one_block), (blocks, starts)).reshape(length, HEADS, HEAD)

def layer(values, segment, params):
    query_weight, query_bias, key_weight, key_bias, value_weight, value_bias, output_weight, output_bias, upward_weight, upward_bias, down_weight, down_bias, attend_gain, attend_bias, dense_gain, dense_bias = params
    length = values.shape[0]
    index = jnp.arange(length, dtype=jnp.int32)
    positions = index - lax.optimization_barrier(jnp.sum((segment[None, :] < segment[:, None]).astype(jnp.int32), axis=1))
    cosine, sine = rotary_tables(positions)
    attend_in = low(layer_norm(values, attend_gain, attend_bias))
    dense_in = low(layer_norm(values, dense_gain, dense_bias))
    query = low_back(matmul(attend_in, query_weight) + query_bias).reshape(length, HEADS, HEAD)
    query = low(rotate(query, cosine[:, None, :], sine[:, None, :]))
    keys = low(rotate(low_back(matmul(attend_in, key_weight) + key_bias), cosine, sine))
    values_low = low(low_back(matmul(attend_in, value_weight) + value_bias))
    attended = attend(query, keys, values_low, segment, index)
    attended = low(low_back(attended)).reshape(length, HEADS * HEAD)
    branch = low_back(matmul(attended, output_weight))
    hidden_pre = low_back(matmul(dense_in, upward_weight) + upward_bias)
    hidden = low(jax.nn.gelu(hidden_pre, approximate=False))
    dense = low_back(matmul(hidden, down_weight))
    return values + branch + dense + output_bias + down_bias

def reference(tokens, segments, query_weight, query_bias, key_weight, key_bias, value_weight, value_bias, output_weight, output_bias, upward_weight, upward_bias, down_weight, down_bias, attend_gain, attend_bias, dense_gain, dense_bias, cotangent):
    params = tuple((p.astype(jnp.float32) for p in (query_weight, query_bias, key_weight, key_bias, value_weight, value_bias, output_weight, output_bias, upward_weight, upward_bias, down_weight, down_bias, attend_gain, attend_bias, dense_gain, dense_bias)))
    count = MICRO * BATCH
    inputs = tokens.astype(jnp.float32).reshape(count, LEN, D)
    seg_all = segments.reshape(count, LEN)
    grads_in = cotangent.astype(jnp.float32).reshape(count, LEN, D)
    zero = jax.tree.map(jnp.zeros_like, params)

    def one_sequence(total, item):
        values, segment, grad_out = item
        output, pull = jax.vjp(lambda inner, weights: layer(inner, segment, weights), values, params)
        grad_in, grad_params = pull(grad_out)
        return (jax.tree.map(jnp.add, total, grad_params), (output.astype(jnp.bfloat16), grad_in.astype(jnp.bfloat16)))
    total, (outputs, grads) = lax.scan(one_sequence, zero, (inputs, seg_all, grads_in))
    return (outputs.reshape(tokens.shape), grads.reshape(tokens.shape), total[0], total[1], total[2], total[3], total[4], total[5], total[6], total[7], total[8], total[9], total[10], total[11], total[12], total[13], total[14], total[15])
```

```python
import functools
import math

import jax
import jax.numpy as jnp
from jax import lax
from jax.experimental import pallas as pl
from jax.experimental.pallas import tpu as pltpu
from jax.sharding import PartitionSpec as P

ROT = 16
NEGATIVE = -1e30
EPSILON = 1e-05
LOG2E = math.log2(math.e)
LANES = 128
query_block = 256
key_block = 256
SHARDED = ("fsdp", "ctx")


def dot(left, right, left_dim, right_dim):
    return lax.dot_general(
        left,
        right,
        (((left_dim,), (right_dim,)), ((), ())),
        preferred_element_type=jnp.float32,
    )


def axis_bits(name):
    return [1 << b for b in reversed(range(lax.axis_size(name).bit_length() - 1))]


def all_bits():
    return [("fsdp", d) for d in axis_bits("fsdp")] + [("ctx", d) for d in axis_bits("ctx")]


def partner(values, stage):
    name, distance = stage
    pairs = [(i, i ^ distance) for i in range(lax.axis_size(name))]
    return lax.ppermute(values, name, pairs)


def own_bit(stage):
    name, distance = stage
    return (lax.axis_index(name) // distance) % 2 == 1


def gather_shards(piece, order):
    rank = {stage: i for i, stage in enumerate(all_bits())}
    held = piece[None]
    done = []
    for stage in order:
        low = 1 << sum(rank[other] > rank[stage] for other in done)
        split = held.reshape((held.shape[0] // low, 1, low) + piece.shape)
        other = partner(held, stage).reshape(split.shape)
        upper = own_bit(stage)
        held = jnp.concatenate(
            [jnp.where(upper, other, split), jnp.where(upper, split, other)], axis=1
        ).reshape((2 * held.shape[0],) + piece.shape)
        done.append(stage)
    return held


def scatter_sum(terms, order):
    rank = {stage: i for i, stage in enumerate(all_bits())}
    left = list(rank)
    held = terms
    for stage in order:
        left.remove(stage)
        low = 1 << sum(rank[other] > rank[stage] for other in left)
        split = held.reshape((held.shape[0] // (2 * low), 2, low) + terms.shape[1:])
        upper = own_bit(stage)
        shape = (held.shape[0] // 2,) + terms.shape[1:]
        send = jnp.where(upper, split[:, 0], split[:, 1]).reshape(shape)
        keep = jnp.where(upper, split[:, 1], split[:, 0]).reshape(shape)
        total = keep.astype(jnp.float32) + partner(send, stage).astype(jnp.float32)
        held = total.astype(jnp.bfloat16) if left else total
    return held[0]


def total_sum(values, stages):
    for stage in stages:
        values = values + partner(values, stage)
    return values


def norm_parts(values):
    centre = values - jnp.mean(values, axis=-1, keepdims=True)
    spread = lax.rsqrt(jnp.mean(centre * centre, axis=-1, keepdims=True) + EPSILON)
    return centre * spread, spread


def rotate(values, cosine, sine):
    half = ROT // 2
    first = values[..., :half, :]
    second = values[..., half:ROT, :]
    return jnp.concatenate(
        [first * cosine - second * sine, second * cosine + first * sine, values[..., ROT:, :]],
        axis=-2,
    )


def block_plan(start, before, micro, length):
    first = start[:, ::query_block]
    last = start[:, query_block - 1 :: query_block]
    begin = before + query_block * jnp.arange(length // query_block, dtype=jnp.int32)[None]
    lo = first // key_block
    hi = jnp.broadcast_to((begin + query_block - 1) // key_block + 1, lo.shape)
    a = jnp.clip((last + key_block - 1) // key_block, lo, hi)
    b = jnp.clip((begin + 1) // key_block, a, hi)
    return jnp.stack([lo, hi, a, b], axis=-1).reshape(-1)


def allowed_pairs(block, start, begin):
    shape = (key_block, query_block)
    key_index = block * key_block + lax.broadcasted_iota(jnp.int32, shape, 0)
    query_index = begin + lax.broadcasted_iota(jnp.int32, shape, 1)
    return (key_index >= start) & (key_index <= query_index)


def over_blocks(plan, at, body):
    lo, hi, a, b = plan[at], plan[at + 1], plan[at + 2], plan[at + 3]

    def step(block, carry):
        inside = (block >= a) & (block < b)

        @pl.when(inside)
        def _():
            body(block, False)

        @pl.when(jnp.logical_not(inside))
        def _():
            body(block, True)

        return carry

    lax.fori_loop(lo, hi, step, 0)


def forward_kernel(before, heads, head, plan, query, pair, start, out, out_low, logsum, best, total):
    at = pl.program_id(0) * pl.num_programs(1) + pl.program_id(1)
    begin = before + pl.program_id(1) * query_block
    factor = head**-0.5 * LOG2E
    best[...] = jnp.full(best.shape, NEGATIVE, jnp.float32)
    total[...] = jnp.zeros(total.shape, jnp.float32)
    out[...] = jnp.zeros(out.shape, jnp.float32)

    def body(block, masked):
        keys = pl.ds(pl.multiple_of(block * key_block, key_block), key_block)
        key = pair[0, :head, keys].T
        value = pair[0, head:, keys]
        if masked:
            allowed = allowed_pairs(block, start[...], begin)
        for h in range(heads):
            rows = pl.ds(h * head, head)
            scores = dot(key, query[rows, :], 1, 0) * factor
            if masked:
                scores = jnp.where(allowed, scores, NEGATIVE)
            old = best[pl.ds(h, 1), :]
            fresh = jnp.maximum(old, jnp.max(scores, axis=0, keepdims=True))
            weights = jnp.exp2(scores - fresh)
            shrink = jnp.exp2(old - fresh)
            best[pl.ds(h, 1), :] = fresh
            total[pl.ds(h, 1), :] = total[pl.ds(h, 1), :] * shrink + jnp.sum(
                weights, axis=0, keepdims=True
            )
            out[rows, :] = out[rows, :] * shrink + dot(value, weights.astype(jnp.bfloat16), 1, 0)

    over_blocks(plan, 4 * at, body)
    for h in range(heads):
        rows = pl.ds(h * head, head)
        value = out[rows, :] / total[pl.ds(h, 1), :]
        out[rows, :] = value
        out_low[rows, :] = value.astype(jnp.bfloat16)
    logsum[...] = best[...] + jnp.log(total[...]) * LOG2E


def backward_kernel(
    before, heads, head, plan, query, pair, start, grad, out, logsum, cosine, sine,
    query_grad, pair_grad, query_sum, pair_sum, delta,
):
    at = pl.program_id(0) * pl.num_programs(1) + pl.program_id(1)
    begin = before + pl.program_id(1) * query_block
    scale = head**-0.5

    @pl.when(pl.program_id(1) == 0)
    def _():
        pair_sum[...] = jnp.zeros(pair_sum.shape, jnp.float32)

    query_sum[...] = jnp.zeros(query_sum.shape, jnp.float32)
    for h in range(heads):
        rows = pl.ds(h * head, head)
        delta[pl.ds(h, 1), :] = jnp.sum(
            grad[rows, :].astype(jnp.float32) * out[rows, :], axis=0, keepdims=True
        )

    def body(block, masked):
        keys = pl.ds(pl.multiple_of(block * key_block, key_block), key_block)
        key_wide = pair[0, :head, keys]
        key = key_wide.T
        value = pair[0, head:, keys].T
        if masked:
            allowed = allowed_pairs(block, start[...], begin)
        key_grad = jnp.zeros((head, key_block), jnp.float32)
        value_grad = jnp.zeros((head, key_block), jnp.float32)
        for h in range(heads):
            rows = pl.ds(h * head, head)
            scores = dot(key, query[rows, :], 1, 0) * (scale * LOG2E)
            probs = jnp.exp2(scores - logsum[pl.ds(h, 1), :])
            if masked:
                probs = jnp.where(allowed, probs, 0.0)
            value_grad += dot(grad[rows, :], probs.astype(jnp.bfloat16), 1, 1)
            prob_grad = dot(value, grad[rows, :], 1, 0)
            score_grad = (probs * (prob_grad - delta[pl.ds(h, 1), :])).astype(jnp.bfloat16)
            query_sum[rows, :] += dot(key_wide, score_grad, 1, 0)
            key_grad += dot(query[rows, :], score_grad, 1, 1)
        pair_sum[:head, keys] += key_grad
        pair_sum[head:, keys] += value_grad

    over_blocks(plan, 4 * at, body)
    half = ROT // 2
    for h in range(heads):
        value = query_sum[pl.ds(h * head, head), :] * scale
        first, second = value[:half], value[half:ROT]
        turned = jnp.concatenate(
            [
                first * cosine[...] + second * sine[...],
                second * cosine[...] - first * sine[...],
                value[ROT:],
            ],
            axis=0,
        )
        query_grad[pl.ds(h * head, head), :] = turned.astype(jnp.bfloat16)

    @pl.when(pl.program_id(1) == pl.num_programs(1) - 1)
    def _():
        pair_grad[0, :head, :] = (pair_sum[:head, :] * scale).astype(jnp.bfloat16)
        pair_grad[0, head:, :] = pair_sum[head:, :].astype(jnp.bfloat16)


def attention_specs(heads, head, blocks, window):
    rows = heads * head
    query = pl.BlockSpec((rows, query_block), lambda m, i, plan: (0, m * blocks + i))
    pair = pl.BlockSpec((1, 2 * head, window), lambda m, i, plan: (m, 0, 0))
    single = pl.BlockSpec((1, query_block), lambda m, i, plan: (0, m * blocks + i))
    per_head = pl.BlockSpec((heads, query_block), lambda m, i, plan: (0, m * blocks + i))
    table = pl.BlockSpec((ROT // 2, query_block), lambda m, i, plan: (0, m * blocks + i))
    return query, pair, single, per_head, table


def attention_cost(micro, rows, length, products):
    pairs = micro * (rows // 64) * length * 2 * length
    return pl.CostEstimate(
        flops=2 * products * 64 * pairs, bytes_accessed=8 * micro * rows * length, transcendentals=pairs
    )


def attend_forward(plan, query, pair, start, before, heads, head):
    micro, _, window = pair.shape
    rows, count = query.shape
    blocks = count // micro // query_block
    q_spec, pair_spec, single, per_head, _ = attention_specs(heads, head, blocks, window)
    return pl.pallas_call(
        functools.partial(forward_kernel, before, heads, head),
        grid_spec=pltpu.PrefetchScalarGridSpec(
            num_scalar_prefetch=1,
            grid=(micro, blocks),
            in_specs=[q_spec, pair_spec, single],
            out_specs=[q_spec, q_spec, per_head],
            scratch_shapes=[
                pltpu.VMEM((heads, query_block), jnp.float32),
                pltpu.VMEM((heads, query_block), jnp.float32),
            ],
        ),
        out_shape=[
            jax.ShapeDtypeStruct((rows, count), jnp.float32),
            jax.ShapeDtypeStruct((rows, count), jnp.bfloat16),
            jax.ShapeDtypeStruct((heads, count), jnp.float32),
        ],
        compiler_params=pltpu.CompilerParams(vmem_limit_bytes=32 << 20),
        cost_estimate=attention_cost(micro, rows, count // micro, 2),
        name="attend_forward",
    )(plan, query, pair, start)


def attend_backward(plan, query, pair, start, grad, out, logsum, cosine, sine, before, heads, head):
    micro, _, window = pair.shape
    rows, count = query.shape
    blocks = count // micro // query_block
    q_spec, pair_spec, single, per_head, table = attention_specs(heads, head, blocks, window)
    return pl.pallas_call(
        functools.partial(backward_kernel, before, heads, head),
        grid_spec=pltpu.PrefetchScalarGridSpec(
            num_scalar_prefetch=1,
            grid=(micro, blocks),
            in_specs=[q_spec, pair_spec, single, q_spec, q_spec, per_head, table, table],
            out_specs=[q_spec, pair_spec],
            scratch_shapes=[
                pltpu.VMEM((rows, query_block), jnp.float32),
                pltpu.VMEM((2 * head, window), jnp.float32),
                pltpu.VMEM((heads, query_block), jnp.float32),
            ],
        ),
        out_shape=[
            jax.ShapeDtypeStruct((rows, count), jnp.bfloat16),
            jax.ShapeDtypeStruct((micro, 2 * head, window), jnp.bfloat16),
        ],
        compiler_params=pltpu.CompilerParams(vmem_limit_bytes=32 << 20),
        cost_estimate=attention_cost(micro, rows, count // micro, 5),
        name="attend_backward",
    )(plan, query, pair, start, grad, out, logsum, cosine, sine)


def shards(
    tokens,
    segments,
    query_weight,
    query_bias,
    key_weight,
    key_bias,
    value_weight,
    value_bias,
    output_weight,
    output_bias,
    upward_weight,
    upward_bias,
    down_weight,
    down_bias,
    attend_gain,
    attend_bias,
    dense_gain,
    dense_bias,
    cotangent,
):
    low = jnp.bfloat16
    micro, _, length, width = tokens.shape
    count = micro * length
    head = key_weight.shape[1]
    query_width = query_bias.shape[0]
    heads = query_width // head
    hidden_width = upward_bias.shape[0]
    devices = lax.axis_size("fsdp") * lax.axis_size("ctx")
    reach = lax.axis_size("ctx") // 2
    before = reach * length
    window = before + length
    core = lax.axis_index("tp")
    stages = all_bits()
    deep = [s for s in stages if s[0] == "ctx" and s[1] > 1]
    near = [s for s in stages if s[0] == "ctx" and s[1] == 1]
    side = [s for s in stages if s[0] == "fsdp"]

    shard_rows = key_weight.shape[0]
    pad_rows = -shard_rows % 16
    segment_rows = count // LANES
    seg_pad = -segment_rows % 16
    pair_piece = jnp.concatenate([key_weight, value_weight], axis=1)
    segment_piece = (segments + 1).astype(low).reshape(segment_rows, LANES)
    first_piece = jnp.concatenate(
        [
            jnp.pad(pair_piece, ((0, pad_rows), (0, 0))),
            jnp.pad(segment_piece, ((0, seg_pad), (0, 0))),
        ]
    )
    first_all = gather_shards(first_piece, side + deep + near)
    w_pair = first_all[:, :shard_rows].reshape(width, 2 * head)
    segment_all = first_all[:, shard_rows + pad_rows :][:, :segment_rows].reshape(
        lax.axis_size("fsdp"), lax.axis_size("ctx"), micro, length
    )
    bulk = lax.all_gather(
        jnp.concatenate([query_weight, output_weight.T, upward_weight, down_weight.T], axis=1),
        SHARDED,
        axis=0,
        tiled=True,
    )
    cuts = [query_width, 2 * query_width, 2 * query_width + hidden_width]
    w_query, w_output, w_upward, w_down = jnp.split(bulk, cuts, axis=1)

    mine = lax.dynamic_index_in_dim(segment_all, lax.axis_index("fsdp"), 0, keepdims=False)
    padded = jnp.concatenate([jnp.zeros((reach,) + mine.shape[1:], low), mine])
    seen = lax.dynamic_slice_in_dim(padded, lax.axis_index("ctx"), reach + 1)
    seen = jnp.transpose(seen, (1, 0, 2)).reshape(micro, window).astype(jnp.int32)
    local = segments[:, 0] + 1
    start = jnp.sum((seen[:, None, :] < local[:, :, None]).astype(jnp.int32), axis=2)
    positions = (before + jnp.arange(length, dtype=jnp.int32))[None] - start
    freqs = jnp.exp(
        jnp.arange(ROT // 2, dtype=jnp.float32) * (-2.0 * math.log(10000.0) / ROT)
    )
    angle = freqs[:, None] * positions.reshape(1, count).astype(jnp.float32)
    cosine, sine = jnp.cos(angle), jnp.sin(angle)
    plan = block_plan(start, before, micro, length)
    start = start.reshape(1, count)

    inputs = tokens.reshape(count, width).astype(jnp.float32)
    normed, spread = norm_parts(inputs)
    attend_in = (normed * attend_gain + attend_bias).astype(low)
    dense_in = (normed * dense_gain + dense_bias).astype(low)

    split = micro % lax.axis_size("tp") == 0 and lax.axis_size("tp") == 2 and micro == 2
    pair_lin = dot(w_pair, attend_in, 0, 1) + jnp.concatenate([key_bias, value_bias])[:, None]
    pair_all = jnp.concatenate(
        [rotate(pair_lin[:head], cosine, sine), pair_lin[head:]], axis=0
    ).astype(low)
    assert split
    pair_mine = jnp.where(core == 0, pair_all[:, :length], pair_all[:, length:])
    context = lax.axis_size("ctx")
    parts = [pair_mine]
    for d in range(1, reach + 1):
        parts.append(lax.ppermute(pair_mine, "ctx", [(i, i + d) for i in range(context - d)]))
    pair_half = jnp.concatenate(parts[::-1], axis=1)
    pair_other = partner(pair_half, ("tp", 1))
    pair = jnp.stack(
        [jnp.where(core == 0, pair_half, pair_other), jnp.where(core == 0, pair_other, pair_half)]
    )

    query_lin = dot(w_query, attend_in, 0, 1) + query_bias[:, None]
    query = (
        rotate(query_lin.reshape(heads, head, count), cosine, sine)
        .astype(low)
        .reshape(query_width, count)
    )
    attended, attended_low, logsum = attend_forward(plan, query, pair, start, before, heads, head)

    grad_low = cotangent.reshape(count, width)
    grad_full = grad_low.astype(jnp.float32)
    hidden_pre = dot(dense_in, w_upward, 1, 0) + upward_bias
    normal_cdf = 0.5 * (1.0 + lax.erf(hidden_pre * (1.0 / math.sqrt(2.0))))
    normal_pdf = jnp.exp(-0.5 * hidden_pre * hidden_pre) * (1.0 / math.sqrt(2.0 * math.pi))
    hidden = (hidden_pre * normal_cdf).astype(low)
    slope = normal_cdf + hidden_pre * normal_pdf
    pre_grad = (dot(grad_low, w_down, 1, 0) * slope).astype(low)
    dense_part = dot(pre_grad, w_upward, 1, 1)

    def by_device(values):
        return values.astype(low).reshape(devices, shard_rows, values.shape[1])

    grad_up = scatter_sum(by_device(dot(dense_in, pre_grad, 0, 0)), side + near + deep[::-1])
    grad_down = scatter_sum(by_device(dot(grad_low, hidden, 0, 0)), near + side + deep[::-1])

    attended_grad = dot(w_output, grad_low, 0, 1).astype(low)
    query_grad, pair_back = attend_backward(
        plan, query, pair, start, attended_grad, attended, logsum, cosine, sine, before, heads, head
    )

    send = jnp.where(core == 0, pair_back[1], pair_back[0])
    keep = jnp.where(core == 0, pair_back[0], pair_back[1])
    summed = (
        keep.astype(jnp.float32) + partner(send, ("tp", 1)).astype(jnp.float32)
    ).astype(low)
    pair_sum = summed[:, before:].astype(jnp.float32)
    for d in range(1, reach + 1):
        piece = summed[:, before - d * length : before - (d - 1) * length]
        pair_sum = pair_sum + lax.ppermute(
            piece, "ctx", [(i + d, i) for i in range(context - d)]
        ).astype(jnp.float32)
    pair_half = pair_sum.astype(low)
    pair_other = partner(pair_half, ("tp", 1))
    pair_grad = jnp.concatenate(
        [jnp.where(core == 0, pair_half, pair_other), jnp.where(core == 0, pair_other, pair_half)],
        axis=1,
    ).astype(jnp.float32)
    pair_low = jnp.concatenate(
        [rotate(pair_grad[:head], cosine, -sine), pair_grad[head:]], axis=0
    ).astype(low)

    pair_low_half = jnp.where(core == 0, pair_low[:head], pair_low[head:])
    w_pair_half = jnp.where(core == 0, w_pair[:, :head], w_pair[:, head:])
    attend_part = dot(query_grad, w_query, 0, 1) + dot(pair_low_half, w_pair_half, 0, 1)
    norm_part = (attend_part * attend_gain + dense_part * dense_gain).astype(low)
    norm_grad = norm_part.astype(jnp.float32) + partner(norm_part, ("tp", 1)).astype(jnp.float32)
    tokens_grad = (
        grad_full
        + spread
        * (
            norm_grad
            - jnp.mean(norm_grad, axis=-1, keepdims=True)
            - normed * jnp.mean(norm_grad * normed, axis=-1, keepdims=True)
        )
    ).astype(low)

    branches = (dot(attended_low, w_output, 0, 1) + dot(hidden, w_down, 1, 1)).astype(low)
    mixed = branches.astype(jnp.float32) + partner(branches, ("tp", 1)).astype(jnp.float32)
    result = (inputs + mixed + output_bias + down_bias).astype(low)

    grad_out = scatter_sum(
        by_device(dot(grad_low, attended_low, 0, 1)), side + near + deep[::-1]
    )
    grad_in = jnp.concatenate(
        [dot(attend_in, query_grad, 0, 1), dot(attend_in, pair_low, 0, 1)], axis=1
    )
    grad_in = scatter_sum(by_device(grad_in), near + side + deep[::-1])

    shared = jnp.concatenate(
        [
            jnp.sum(attend_part * normed, axis=0),
            jnp.sum(attend_part, axis=0),
            jnp.sum(dense_part * normed, axis=0),
            jnp.sum(dense_part, axis=0),
        ]
    )
    shared = shared + partner(shared, ("tp", 1))
    small = jnp.concatenate(
        [
            shared,
            jnp.sum(grad_full, axis=0),
            jnp.sum(pre_grad.astype(jnp.float32), axis=0),
            jnp.sum(query_grad.astype(jnp.float32), axis=1),
            jnp.sum(pair_low.astype(jnp.float32), axis=1),
        ]
    )
    small = total_sum(small.reshape(-1, LANES), stages).reshape(-1)
    sizes = [width] * 5 + [hidden_width, query_width, head, head]
    bounds = [sum(sizes[: i + 1]) for i in range(len(sizes) - 1)]
    g_gain, g_shift, d_gain, d_shift, out_b, up_b, q_b, k_b, v_b = jnp.split(small, bounds)
    shape = (micro, 1, length, width)
    return (
        result.reshape(shape),
        tokens_grad.reshape(shape),
        grad_in[:, :query_width],
        q_b,
        grad_in[:, query_width : query_width + head],
        k_b,
        grad_in[:, query_width + head :],
        v_b,
        grad_out.T,
        out_b,
        grad_up,
        up_b,
        grad_down.T,
        out_b,
        g_gain,
        g_shift,
        d_gain,
        d_shift,
    )


def solution(mesh):
    return jax.shard_map(
        shards,
        mesh=mesh,
        in_specs=(
            P(None, "fsdp", "ctx", None),
            P(None, "fsdp", "ctx"),
            P(("fsdp", "ctx"), "tp"),
            P("tp"),
            P(("fsdp", "ctx"), None),
            P(),
            P(("fsdp", "ctx"), None),
            P(),
            P("tp", ("fsdp", "ctx")),
            P(),
            P(("fsdp", "ctx"), "tp"),
            P("tp"),
            P("tp", ("fsdp", "ctx")),
            P(),
            P(),
            P(),
            P(),
            P(),
            P(None, "fsdp", "ctx", None),
        ),
        out_specs=(
            P(None, "fsdp", "ctx", None),
            P(None, "fsdp", "ctx", None),
            P(("fsdp", "ctx"), "tp"),
            P("tp"),
            P(("fsdp", "ctx"), None),
            P(),
            P(("fsdp", "ctx"), None),
            P(),
            P("tp", ("fsdp", "ctx")),
            P(),
            P(("fsdp", "ctx"), "tp"),
            P("tp"),
            P("tp", ("fsdp", "ctx")),
            P(),
            P(),
            P(),
            P(),
            P(),
        ),
        check_vma=False,
    )
```

```python
import functools
import math

import jax
import jax.numpy as jnp
from jax import lax
from jax.experimental import pallas as pl
from jax.experimental.pallas import tpu as pltpu
from jax.sharding import PartitionSpec as P

ROT = 16
NEGATIVE = -1e30
EPSILON = 1e-05
LOG2E = math.log2(math.e)
LANES = 128
forward_blocks = (512, 512)
backward_blocks = (256, 256)


def dot(left, right, left_dim, right_dim):
    return lax.dot_general(
        left,
        right,
        (((left_dim,), (right_dim,)), ((), ())),
        preferred_element_type=jnp.float32,
    )


def axis_bits(name):
    return [1 << b for b in reversed(range(lax.axis_size(name).bit_length() - 1))]


def all_bits():
    return [("fsdp", d) for d in axis_bits("fsdp")] + [("ctx", d) for d in axis_bits("ctx")]


def partner(values, stage):
    name, distance = stage
    pairs = [(i, i ^ distance) for i in range(lax.axis_size(name))]
    return lax.ppermute(values, name, pairs)


def own_bit(stage):
    name, distance = stage
    return (lax.axis_index(name) // distance) % 2 == 1


def gather_step(state, stage):
    held, done = state
    rank = {other: i for i, other in enumerate(all_bits())}
    low = 1 << sum(rank[other] > rank[stage] for other in done)
    piece = held.shape[1:]
    split = held.reshape((held.shape[0] // low, 1, low) + piece)
    other = partner(held, stage).reshape(split.shape)
    upper = own_bit(stage)
    held = jnp.concatenate(
        [jnp.where(upper, other, split), jnp.where(upper, split, other)], axis=1
    ).reshape((2 * held.shape[0],) + piece)
    return held, done + [stage]


def scatter_halves(held, left, stage):
    rank = {other: i for i, other in enumerate(all_bits())}
    low = 1 << sum(rank[other] > rank[stage] for other in left if other != stage)
    piece = held.shape[1:]
    split = held.reshape((held.shape[0] // (2 * low), 2, low) + piece)
    upper = own_bit(stage)
    shape = (held.shape[0] // 2,) + piece
    send = jnp.where(upper, split[:, 0], split[:, 1]).reshape(shape)
    keep = jnp.where(upper, split[:, 1], split[:, 0]).reshape(shape)
    return send, keep


def scatter_step(state, stage):
    held, left = state
    send, keep = scatter_halves(held, left, stage)
    left = [other for other in left if other != stage]
    total = keep.astype(jnp.float32) + partner(send, stage).astype(jnp.float32)
    return (total.astype(jnp.bfloat16) if left else total), left


def after(values, *others):
    return lax.optimization_barrier((values,) + others)[0]


def norm_parts(values):
    centre = values - jnp.mean(values, axis=-1, keepdims=True)
    spread = lax.rsqrt(jnp.mean(centre * centre, axis=-1, keepdims=True) + EPSILON)
    return centre * spread, spread


def rotate(values, cosine, sine):
    half = ROT // 2
    first = values[..., :half, :]
    second = values[..., half:ROT, :]
    return jnp.concatenate(
        [first * cosine - second * sine, second * cosine + first * sine, values[..., ROT:, :]],
        axis=-2,
    )


def block_plan(start, before, length, query_block, key_block):
    first = start[:, ::query_block]
    last = start[:, query_block - 1 :: query_block]
    begin = before + query_block * jnp.arange(length // query_block, dtype=jnp.int32)[None]
    lo = first // key_block
    hi = jnp.broadcast_to((begin + query_block - 1) // key_block + 1, lo.shape)
    a = jnp.clip((last + key_block - 1) // key_block, lo, hi)
    b = jnp.clip((begin + 1) // key_block, a, hi)
    return jnp.stack([lo, hi, a, b], axis=-1)


def allowed_pairs(block, key_block, start, last):
    key_index = block * key_block + lax.broadcasted_iota(
        jnp.int32, (key_block, start.shape[1]), 0
    )
    return (key_index >= start) & (key_index <= last)


def over_blocks(plan, at, body):
    lo, hi, a, b = plan[at], plan[at + 1], plan[at + 2], plan[at + 3]

    def step(block, carry):
        inside = (block >= a) & (block < b)

        @pl.when(inside)
        def _():
            body(block, False)

        @pl.when(jnp.logical_not(inside))
        def _():
            body(block, True)

        return carry

    lax.fori_loop(lo, hi, step, 0)


def spread_heads(pairs, heads, head, block):
    for h in range(heads):
        for wide, tall in pairs:
            wide[:, pl.ds(h * block, block)] = tall[pl.ds(h * head, head), :]


def forward_kernel(
    before, heads, head, key_block, plan, query, pair, start, out, out_low, logsum,
    wide, best, total, accum, first, last,
):
    block_rows = query.shape[1]
    at = pl.program_id(0) * pl.num_programs(1) + pl.program_id(1)
    begin = before + pl.program_id(1) * block_rows
    factor = head**-0.5 * LOG2E
    best[...] = jnp.full(best.shape, NEGATIVE, jnp.float32)
    total[...] = jnp.zeros(total.shape, jnp.float32)
    accum[...] = jnp.zeros(accum.shape, jnp.float32)
    spread_heads([(wide, query)], heads, head, block_rows)
    index = begin + lax.broadcasted_iota(jnp.int32, (1, block_rows), 1)
    for h in range(heads):
        first[:, pl.ds(h * block_rows, block_rows)] = start[...]
        last[:, pl.ds(h * block_rows, block_rows)] = index

    def body(block, masked):
        keys = pl.ds(pl.multiple_of(block * key_block, key_block), key_block)
        key = pair[0, :head, keys].T
        value = pair[0, head:, keys]
        value = jnp.concatenate([value, jnp.ones((8, key_block), jnp.bfloat16)], axis=0)
        scores = dot(key, wide[...], 1, 0) * factor
        if masked:
            allowed = allowed_pairs(block, key_block, first[...], last[...])
            scores = jnp.where(allowed, scores, NEGATIVE)
        old = best[...]
        fresh = jnp.maximum(old, jnp.max(scores, axis=0, keepdims=True))
        weights = jnp.exp2(scores - fresh).astype(jnp.bfloat16)
        shrink = jnp.exp2(old - fresh)
        best[...] = fresh
        product = dot(value, weights, 1, 0)
        accum[...] = accum[...] * shrink + product[:head]
        total[...] = total[...] * shrink + product[head : head + 1]

    over_blocks(plan, 4 * at, body)
    scaled = accum[...] / total[...]
    sums = best[...] + jnp.log(total[...]) * LOG2E
    for h in range(heads):
        columns = slice(h * block_rows, (h + 1) * block_rows)
        rows = pl.ds(h * head, head)
        out[rows, :] = scaled[:, columns]
        out_low[rows, :] = scaled[:, columns].astype(jnp.bfloat16)
        logsum[pl.ds(h, 1), :] = sums[:, columns]


def backward_kernel(
    before, heads, head, key_block, plan, query, pair, start, grad, out, logsum, cosine, sine,
    query_grad, pair_grad,
    wide, wide_grad, query_sum, pair_sum, sums, delta, first, last,
):
    block_rows = query.shape[1]
    begin = before + pl.program_id(0) * block_rows
    scale = head**-0.5

    @pl.when(pl.program_id(0) == 0)
    def _():
        pair_sum[...] = jnp.zeros(pair_sum.shape, jnp.float32)

    query_sum[...] = jnp.zeros(query_sum.shape, jnp.float32)
    spread_heads([(wide, query), (wide_grad, grad)], heads, head, block_rows)
    index = begin + lax.broadcasted_iota(jnp.int32, (1, block_rows), 1)
    for h in range(heads):
        rows = pl.ds(h * head, head)
        columns = pl.ds(h * block_rows, block_rows)
        first[:, columns] = start[...]
        last[:, columns] = index
        sums[:, columns] = logsum[pl.ds(h, 1), :]
        delta[:, columns] = jnp.sum(
            grad[rows, :].astype(jnp.float32) * out[rows, :], axis=0, keepdims=True
        )

    def body(block, masked):
        keys = pl.ds(pl.multiple_of(block * key_block, key_block), key_block)
        key_wide = pair[0, :head, keys]
        key = key_wide.T
        value = pair[0, head:, keys].T
        scores = dot(key, wide[...], 1, 0) * (scale * LOG2E)
        probs = jnp.exp2(scores - sums[...])
        if masked:
            allowed = allowed_pairs(block, key_block, first[...], last[...])
            probs = jnp.where(allowed, probs, 0.0)
        pair_sum[head:, keys] += dot(wide_grad[...], probs.astype(jnp.bfloat16), 1, 1)
        prob_grad = dot(value, wide_grad[...], 1, 0)
        score_grad = (probs * (prob_grad - delta[...])).astype(jnp.bfloat16)
        pair_sum[:head, keys] += dot(wide[...], score_grad, 1, 1)
        query_sum[...] += dot(key_wide, score_grad, 1, 0)

    over_blocks(plan, 4 * pl.program_id(0), body)
    half = ROT // 2
    for h in range(heads):
        value = query_sum[:, pl.ds(h * block_rows, block_rows)] * scale
        near, far = value[:half], value[half:ROT]
        turned = jnp.concatenate(
            [
                near * cosine[...] + far * sine[...],
                far * cosine[...] - near * sine[...],
                value[ROT:],
            ],
            axis=0,
        )
        query_grad[pl.ds(h * head, head), :] = turned.astype(jnp.bfloat16)

    @pl.when(pl.program_id(0) == pl.num_programs(0) - 1)
    def _():
        pair_grad[:head, :] = (pair_sum[:head, :] * scale).astype(jnp.bfloat16)
        pair_grad[head:, :] = pair_sum[head:, :].astype(jnp.bfloat16)


def attention_cost(micro, rows, length, products):
    pairs = micro * (rows // 64) * length * 2 * length
    return pl.CostEstimate(
        flops=2 * products * 64 * pairs, bytes_accessed=8 * micro * rows * length, transcendentals=pairs
    )


def attend_forward(start, query, pair, before, heads, head):
    micro, _, window = pair.shape
    rows, count = query.shape
    length = count // micro
    query_block, key_block = forward_blocks
    blocks = length // query_block
    spread = heads * query_block
    plan = block_plan(start, before, length, query_block, key_block).reshape(-1)
    column = lambda m, i, plan: (0, m * blocks + i)
    tall = pl.BlockSpec((rows, query_block), column)
    return pl.pallas_call(
        functools.partial(forward_kernel, before, heads, head, key_block),
        grid_spec=pltpu.PrefetchScalarGridSpec(
            num_scalar_prefetch=1,
            grid=(micro, blocks),
            in_specs=[
                tall,
                pl.BlockSpec((1, 2 * head, window), lambda m, i, plan: (m, 0, 0)),
                pl.BlockSpec((1, query_block), column),
            ],
            out_specs=[tall, tall, pl.BlockSpec((heads, query_block), column)],
            scratch_shapes=[
                pltpu.VMEM((head, spread), jnp.bfloat16),
                pltpu.VMEM((1, spread), jnp.float32),
                pltpu.VMEM((1, spread), jnp.float32),
                pltpu.VMEM((head, spread), jnp.float32),
                pltpu.VMEM((1, spread), jnp.int32),
                pltpu.VMEM((1, spread), jnp.int32),
            ],
        ),
        out_shape=[
            jax.ShapeDtypeStruct((rows, count), jnp.float32),
            jax.ShapeDtypeStruct((rows, count), jnp.bfloat16),
            jax.ShapeDtypeStruct((heads, count), jnp.float32),
        ],
        compiler_params=pltpu.CompilerParams(vmem_limit_bytes=40 << 20),
        cost_estimate=attention_cost(micro, rows, length, 2),
        name="attend_forward",
    )(plan, query, pair, start.reshape(1, count))


def attend_backward(at, start, query, pair, grad, out, logsum, cosine, sine, before, heads, head):
    micro, _, window = pair.shape
    rows, count = query.shape
    length = count // micro
    query_block, key_block = backward_blocks
    blocks = length // query_block
    spread = heads * query_block
    plan = block_plan(start, before, length, query_block, key_block)[at].reshape(-1)
    column = lambda i, plan: (0, at * blocks + i)
    tall = pl.BlockSpec((rows, query_block), column)
    table = pl.BlockSpec((ROT // 2, query_block), column)
    return pl.pallas_call(
        functools.partial(backward_kernel, before, heads, head, key_block),
        grid_spec=pltpu.PrefetchScalarGridSpec(
            num_scalar_prefetch=1,
            grid=(blocks,),
            in_specs=[
                tall,
                pl.BlockSpec((1, 2 * head, window), lambda i, plan: (at, 0, 0)),
                pl.BlockSpec((1, query_block), column),
                tall,
                tall,
                pl.BlockSpec((heads, query_block), column),
                table,
                table,
            ],
            out_specs=[
                pl.BlockSpec((rows, query_block), lambda i, plan: (0, i)),
                pl.BlockSpec((2 * head, window), lambda i, plan: (0, 0)),
            ],
            scratch_shapes=[
                pltpu.VMEM((head, spread), jnp.bfloat16),
                pltpu.VMEM((head, spread), jnp.bfloat16),
                pltpu.VMEM((head, spread), jnp.float32),
                pltpu.VMEM((2 * head, window), jnp.float32),
                pltpu.VMEM((1, spread), jnp.float32),
                pltpu.VMEM((1, spread), jnp.float32),
                pltpu.VMEM((1, spread), jnp.int32),
                pltpu.VMEM((1, spread), jnp.int32),
            ],
        ),
        out_shape=[
            jax.ShapeDtypeStruct((rows, length), jnp.bfloat16),
            jax.ShapeDtypeStruct((2 * head, window), jnp.bfloat16),
        ],
        compiler_params=pltpu.CompilerParams(vmem_limit_bytes=40 << 20),
        cost_estimate=attention_cost(1, rows, length, 5),
        name="attend_backward",
    )(plan, query, pair, start.reshape(1, count), grad, out, logsum, cosine, sine)


def shards(
    tokens,
    segments,
    query_weight,
    query_bias,
    key_weight,
    key_bias,
    value_weight,
    value_bias,
    output_weight,
    output_bias,
    upward_weight,
    upward_bias,
    down_weight,
    down_bias,
    attend_gain,
    attend_bias,
    dense_gain,
    dense_bias,
    cotangent,
):
    low = jnp.bfloat16
    micro, _, length, width = tokens.shape
    count = micro * length
    head = key_weight.shape[1]
    query_width = query_bias.shape[0]
    heads = query_width // head
    hidden_width = upward_bias.shape[0]
    devices = lax.axis_size("fsdp") * lax.axis_size("ctx")
    reach = lax.axis_size("ctx") // 2
    before = reach * length
    window = before + length
    core = lax.axis_index("tp")
    stages = all_bits()
    deep = [s for s in stages if s[0] == "ctx" and s[1] > 1]
    near = [s for s in stages if s[0] == "ctx" and s[1] == 1]
    side = [s for s in stages if s[0] == "fsdp"]

    first_half = core == 0

    def halves(own, other):
        return jnp.where(first_half, own, other), jnp.where(first_half, other, own)

    shard_rows = key_weight.shape[0]
    segment_piece = (segments + 1).astype(low).reshape(-1, head)
    piece_rows = max(shard_rows, segment_piece.shape[0])

    def padded(values):
        return jnp.pad(values, ((0, piece_rows - values.shape[0]), (0, 0)))

    pair_piece = jnp.concatenate(
        [padded(jnp.where(first_half, key_weight, value_weight)), padded(segment_piece)], axis=1
    )
    early = (pair_piece[None], [])
    asked = (query_weight[None], [])
    up = (upward_weight[None], [])
    down = (jnp.concatenate([down_weight.T, output_weight.T], axis=1)[None], [])
    up_order = deep + side + near
    down_order = deep + near + side
    for i, stage in enumerate(side + near + deep):
        early = gather_step(early, stage)
        if i < len(stages) - 2:
            up = gather_step(up, up_order[i])
            down = gather_step(down, down_order[i])
    for stage in near + side + deep:
        asked = gather_step(asked, stage)
    early_all = early[0]
    w_pair = early_all[:, :shard_rows, :head].reshape(width, head)
    w_query = asked[0].reshape(width, query_width)
    segment_all = early_all[:, : segment_piece.shape[0], head:].reshape(
        lax.axis_size("fsdp"), lax.axis_size("ctx"), micro, length
    )

    mine = lax.dynamic_index_in_dim(segment_all, lax.axis_index("fsdp"), 0, keepdims=False)
    reached = jnp.concatenate([jnp.zeros((reach,) + mine.shape[1:], low), mine])
    seen = lax.dynamic_slice_in_dim(reached, lax.axis_index("ctx"), reach + 1)
    seen = jnp.transpose(seen, (1, 0, 2)).reshape(micro, window).astype(jnp.int32)
    local = segments[:, 0] + 1
    start = jnp.sum((seen[:, None, :] < local[:, :, None]).astype(jnp.int32), axis=2)
    positions = (before + jnp.arange(length, dtype=jnp.int32))[None] - start
    freqs = jnp.exp(
        jnp.arange(ROT // 2, dtype=jnp.float32) * (-2.0 * math.log(10000.0) / ROT)
    )
    angle = freqs[:, None] * positions.reshape(1, count).astype(jnp.float32)
    cosine, sine = jnp.cos(angle), jnp.sin(angle)
    pair_cosine = jnp.where(first_half, cosine, 1.0)
    pair_sine = jnp.where(first_half, sine, 0.0)

    inputs = tokens.reshape(count, width).astype(jnp.float32)
    normed, spread = norm_parts(inputs)
    attend_in = (normed * attend_gain + attend_bias).astype(low)
    dense_in = (normed * dense_gain + dense_bias).astype(low)

    def by_micro(values):
        return jnp.transpose(values.reshape(head, micro, length), (1, 0, 2)).reshape(-1, length)

    def by_token(values):
        return jnp.transpose(values.reshape(micro, head, length), (1, 0, 2)).reshape(head, count)

    pair_lin = dot(w_pair, attend_in, 0, 1) + jnp.where(first_half, key_bias, value_bias)[:, None]
    pair_mine = by_micro(rotate(pair_lin, pair_cosine, pair_sine).astype(low))
    context = lax.axis_size("ctx")
    pair_mine = after(pair_mine, up[0], down[0])
    parts = [pair_mine]
    for d in range(1, reach + 1):
        parts.append(lax.ppermute(pair_mine, "ctx", [(i, i + d) for i in range(context - d)]))
    up = gather_step(up, up_order[-2])
    down = gather_step(down, down_order[-2])
    pair_half = jnp.concatenate(parts[::-1], axis=1)
    pair_other = partner(pair_half, ("tp", 1))
    pair = jnp.concatenate(
        [side_half.reshape(micro, head, window) for side_half in halves(pair_half, pair_other)],
        axis=1,
    )

    query_lin = dot(w_query, attend_in, 0, 1) + query_bias[:, None]
    query = (
        rotate(query_lin.reshape(heads, head, count), cosine, sine)
        .astype(low)
        .reshape(query_width, count)
    )
    query = after(query, up[0], down[0])
    attended, attended_low, logsum = attend_forward(start, query, pair, before, heads, head)
    w_upward = gather_step(up, up_order[-1])[0].reshape(width, hidden_width)
    w_down = gather_step(down, down_order[-1])[0].reshape(width, hidden_width + query_width)
    w_down, w_output = w_down[:, :hidden_width], w_down[:, hidden_width:]

    grad_low = cotangent.reshape(count, width)
    grad_full = grad_low.astype(jnp.float32)
    hidden_pre = dot(after(dense_in, attended_low), w_upward, 1, 0) + upward_bias
    normal_cdf = 0.5 * (1.0 + lax.erf(hidden_pre * (1.0 / math.sqrt(2.0))))
    normal_pdf = jnp.exp(-0.5 * hidden_pre * hidden_pre) * (1.0 / math.sqrt(2.0 * math.pi))
    hidden = (hidden_pre * normal_cdf).astype(low)
    slope = normal_cdf + hidden_pre * normal_pdf
    pre_grad = (dot(grad_low, w_down, 1, 0) * slope).astype(low)

    def by_device(values):
        return values.astype(low).reshape(devices, shard_rows, values.shape[1])

    up_order = side + near + deep[::-1]
    down_order = near + side + deep[::-1]
    up = (by_device(dot(dense_in, pre_grad, 0, 0)), stages)
    down = jnp.concatenate(
        [dot(grad_low, hidden, 0, 0).astype(low), dot(grad_low, attended_low, 0, 1).astype(low)],
        axis=1,
    )
    down = (by_device(down), stages)
    up = scatter_step(up, up_order[0])
    down = scatter_step(down, down_order[0])

    attended_grad = dot(w_output, grad_low, 0, 1).astype(low)
    query_grads, pair_grads = [], []
    for at in range(micro):
        if at == micro - 1:
            attended_grad = after(attended_grad, up[0], down[0])
            up = scatter_step(up, up_order[1])
            down = scatter_step(down, down_order[1])
        query_part, pair_part = attend_backward(
            at, start, query, pair, attended_grad, attended, logsum, cosine, sine, before, heads, head
        )
        query_grads.append(query_part)
        pair_grads.append(pair_part)
    query_grad = jnp.concatenate(query_grads, axis=1)
    pair_back = jnp.stack(pair_grads).reshape(micro, 2, head, window)

    keep, send = halves(pair_back[:, 0], pair_back[:, 1])
    summed = (keep.astype(jnp.float32) + partner(send, ("tp", 1)).astype(jnp.float32)).astype(low)
    summed = summed.reshape(micro * head, window)
    pair_sum = summed[:, before:].astype(jnp.float32)
    for d in range(1, reach + 1):
        piece = summed[:, before - d * length : before - (d - 1) * length]
        pair_sum = pair_sum + lax.ppermute(
            piece, "ctx", [(i + d, i) for i in range(context - d)]
        ).astype(jnp.float32)
    pair_low = rotate(by_token(pair_sum), pair_cosine, -pair_sine).astype(low)

    asked_order = side + near + deep[::-1]
    asked = (by_device(dot(attend_in, query_grad, 0, 1)), stages)
    for stage in asked_order:
        asked = scatter_step(asked, stage)
    for up_stage, down_stage in zip(up_order[2:], down_order[2:]):
        up = scatter_step(up, up_stage)
        down = scatter_step(down, down_stage)
    grad_query, grad_up, grad_down = asked[0][0], up[0][0], down[0][0]

    dense_part = dot(pre_grad, w_upward, 1, 1)
    attend_part = dot(query_grad, w_query, 0, 1) + dot(pair_low, w_pair, 0, 1)
    norm_part = (attend_part * attend_gain + dense_part * dense_gain).astype(low)
    norm_grad = norm_part.astype(jnp.float32) + partner(norm_part, ("tp", 1)).astype(jnp.float32)
    tokens_grad = (
        grad_full
        + spread
        * (
            norm_grad
            - jnp.mean(norm_grad, axis=-1, keepdims=True)
            - normed * jnp.mean(norm_grad * normed, axis=-1, keepdims=True)
        )
    ).astype(low)

    branches = (dot(attended_low, w_output, 0, 1) + dot(hidden, w_down, 1, 1)).astype(low)
    mixed = branches.astype(jnp.float32) + partner(branches, ("tp", 1)).astype(jnp.float32)
    result = (inputs + mixed + output_bias + down_bias).astype(low)

    small = jnp.concatenate(
        [
            jnp.sum(attend_part * normed, axis=0),
            jnp.sum(attend_part, axis=0),
            jnp.sum(dense_part * normed, axis=0),
            jnp.sum(dense_part, axis=0),
            jnp.pad(jnp.sum(pair_low.astype(jnp.float32), axis=1), (0, -head % LANES)),
            jnp.sum(grad_full, axis=0),
            jnp.sum(pre_grad.astype(jnp.float32), axis=0),
            jnp.sum(query_grad.astype(jnp.float32), axis=1),
        ]
    ).reshape(-1, LANES)
    shared_rows = 4 * width // LANES + 1
    piece_rows = shard_rows * head // LANES
    held = dot(attend_in, pair_low, 0, 1).reshape(devices, piece_rows, LANES)
    left = stages
    for stage in asked_order:
        send, keep = scatter_halves(held, left, stage)
        left = [other for other in left if other != stage]
        rows = send.shape[0] * piece_rows
        got = partner(jnp.concatenate([send.reshape(rows, LANES), small]), stage)
        held = keep + got[:rows].reshape(keep.shape)
        small = small + got[rows:]
    own = jnp.concatenate([held[0], small[:shared_rows]])
    got = partner(own, ("tp", 1))
    grad_key, grad_value = [
        values.reshape(shard_rows, head) for values in halves(held[0], got[:piece_rows])
    ]
    shared = small[: shared_rows - 1] + got[piece_rows : piece_rows + shared_rows - 1]
    g_gain, g_shift, d_gain, d_shift = jnp.split(shared.reshape(-1), 4)
    k_b, v_b = [values[:head] for values in halves(small[shared_rows - 1], got[-1])]
    rest = small[shared_rows:].reshape(-1)
    out_b, up_b, q_b = jnp.split(rest, [width, width + hidden_width])
    shape = (micro, 1, length, width)
    return (
        result.reshape(shape),
        tokens_grad.reshape(shape),
        grad_query,
        q_b,
        grad_key,
        k_b,
        grad_value,
        v_b,
        grad_down[:, hidden_width:].T,
        out_b,
        grad_up,
        up_b,
        grad_down[:, :hidden_width].T,
        out_b,
        g_gain,
        g_shift,
        d_gain,
        d_shift,
    )


def solution(mesh):
    return jax.shard_map(
        shards,
        mesh=mesh,
        in_specs=(
            P(None, "fsdp", "ctx", None),
            P(None, "fsdp", "ctx"),
            P(("fsdp", "ctx"), "tp"),
            P("tp"),
            P(("fsdp", "ctx"), None),
            P(),
            P(("fsdp", "ctx"), None),
            P(),
            P("tp", ("fsdp", "ctx")),
            P(),
            P(("fsdp", "ctx"), "tp"),
            P("tp"),
            P("tp", ("fsdp", "ctx")),
            P(),
            P(),
            P(),
            P(),
            P(),
            P(None, "fsdp", "ctx", None),
        ),
        out_specs=(
            P(None, "fsdp", "ctx", None),
            P(None, "fsdp", "ctx", None),
            P(("fsdp", "ctx"), "tp"),
            P("tp"),
            P(("fsdp", "ctx"), None),
            P(),
            P(("fsdp", "ctx"), None),
            P(),
            P("tp", ("fsdp", "ctx")),
            P(),
            P(("fsdp", "ctx"), "tp"),
            P("tp"),
            P("tp", ("fsdp", "ctx")),
            P(),
            P(),
            P(),
            P(),
            P(),
        ),
        check_vma=False,
    )
```

```python
import functools
import math

import jax
import jax.numpy as jnp
from jax import lax
from jax.experimental.layout import Layout, with_layout_constraint
from jax.experimental import pallas as pl
from jax.experimental.pallas import tpu as pltpu
from jax.sharding import PartitionSpec as P

ROT = 16
NEGATIVE = -1e30
EPSILON = 1e-05
LOG2E = math.log2(math.e)
LANES = 128
forward_blocks = (512, 512)
backward_blocks = (256, 256)


def dot(left, right, left_dim, right_dim):
    return lax.dot_general(
        left,
        right,
        (((left_dim,), (right_dim,)), ((), ())),
        preferred_element_type=jnp.float32,
    )


def axis_bits(name):
    return [1 << b for b in reversed(range(lax.axis_size(name).bit_length() - 1))]


def all_bits():
    return [("fsdp", d) for d in axis_bits("fsdp")] + [("ctx", d) for d in axis_bits("ctx")]


def partner(values, stage):
    name, distance = stage
    pairs = [(i, i ^ distance) for i in range(lax.axis_size(name))]
    return lax.ppermute(values, name, pairs)


def own_bit(stage):
    name, distance = stage
    return (lax.axis_index(name) // distance) % 2 == 1


def gather_step(state, stage):
    held, done = state
    rank = {other: i for i, other in enumerate(all_bits())}
    low = 1 << sum(rank[other] > rank[stage] for other in done)
    piece = held.shape[1:]
    split = held.reshape((held.shape[0] // low, 1, low) + piece)
    other = partner(held, stage).reshape(split.shape)
    upper = own_bit(stage)
    held = jnp.concatenate(
        [jnp.where(upper, other, split), jnp.where(upper, split, other)], axis=1
    ).reshape((2 * held.shape[0],) + piece)
    return held, done + [stage]


def scatter_halves(held, left, stage):
    rank = {other: i for i, other in enumerate(all_bits())}
    low = 1 << sum(rank[other] > rank[stage] for other in left if other != stage)
    piece = held.shape[1:]
    split = held.reshape((held.shape[0] // (2 * low), 2, low) + piece)
    upper = own_bit(stage).astype(jnp.int32)
    shape = (held.shape[0] // 2,) + piece
    send = lax.dynamic_index_in_dim(split, 1 - upper, 1, keepdims=False).reshape(shape)
    keep = lax.dynamic_index_in_dim(split, upper, 1, keepdims=False).reshape(shape)
    return send, keep


def scatter_step(state, stage):
    held, left = state
    send, keep = scatter_halves(held, left, stage)
    left = [other for other in left if other != stage]
    total = keep.astype(jnp.float32) + partner(send, stage).astype(jnp.float32)
    return (total.astype(jnp.bfloat16) if left else total), left


def after(values, *others):
    return lax.optimization_barrier((values,) + others)[0]


def norm_parts(values):
    centre = values - jnp.mean(values, axis=-1, keepdims=True)
    spread = lax.rsqrt(jnp.mean(centre * centre, axis=-1, keepdims=True) + EPSILON)
    return centre * spread, spread


def as_row(values):
    return values[...].reshape(1, values.shape[0])


def norm_kernel(
    tokens, attend_gain, attend_bias, dense_gain, dense_bias, attend_in, dense_in
):
    normed, _ = norm_parts(tokens[...].astype(jnp.float32))
    attend_in[...] = (normed * as_row(attend_gain) + as_row(attend_bias)).astype(jnp.bfloat16)
    dense_in[...] = (normed * as_row(dense_gain) + as_row(dense_bias)).astype(jnp.bfloat16)


def part_kernel(
    query_grad, pair_low, w_query, w_pair, dense_part, tokens, attend_gain, dense_gain,
    norm_part, sums,
):
    attend_part = dot(query_grad[...], w_query[...], 1, 1) + dot(pair_low[...].T, w_pair[...], 1, 1)
    dense = dense_part[...]
    normed, _ = norm_parts(tokens[...].astype(jnp.float32))
    norm_part[...] = (
        attend_part * as_row(attend_gain) + dense * as_row(dense_gain)
    ).astype(jnp.bfloat16)

    @pl.when(pl.program_id(0) == 0)
    def _():
        sums[...] = jnp.zeros(sums.shape, jnp.float32)

    rows = [attend_part * normed, attend_part, dense * normed, dense]
    sums[...] += jnp.concatenate([jnp.sum(row, axis=0, keepdims=True) for row in rows])


def back_kernel(own, other, cotangent, tokens, tokens_grad):
    grad = own[...].astype(jnp.float32) + other[...].astype(jnp.float32)
    normed, spread = norm_parts(tokens[...].astype(jnp.float32))
    inner = (
        grad
        - jnp.mean(grad, axis=-1, keepdims=True)
        - normed * jnp.mean(grad * normed, axis=-1, keepdims=True)
    )
    tokens_grad[...] = (cotangent[...].astype(jnp.float32) + spread * inner).astype(jnp.bfloat16)


def result_kernel(own, other, tokens, first_bias, second_bias, result):
    mixed = own[...].astype(jnp.float32) + other[...].astype(jnp.float32)
    result[...] = (
        tokens[...].astype(jnp.float32) + mixed + as_row(first_bias) + as_row(second_bias)
    ).astype(jnp.bfloat16)


def sum_kernel(
    shard_rows, shared_rows, small_rows, got, own, out_sum, up_sum, query_sum, out_again
):
    total = got[0].astype(jnp.float32)
    for device in range(1, got.shape[0]):
        total += got[device].astype(jnp.float32)
    high = total[shard_rows : shard_rows + small_rows]
    small = high + total[shard_rows + small_rows : shard_rows + 2 * small_rows]
    own[...] = jnp.concatenate([total[:shard_rows], small[:shared_rows]])
    at = shared_rows
    for out in (out_sum, up_sum, query_sum):
        out[...] = small[at : at + out.shape[0]]
        at += out.shape[0]
    out_again[...] = out_sum[...]


def last_kernel(shard_rows, head, core, own, other, key_grad, value_grad, key_sum, value_sum, *sums):
    first = core[0] == 0
    mine, theirs = own[...], other[...]
    keys = jnp.where(first, mine, theirs)
    values = jnp.where(first, theirs, mine)
    key_grad[...] = keys[:shard_rows, :head]
    value_grad[...] = values[:shard_rows, :head]
    key_sum[...] = keys[keys.shape[0] - 1 :, :head]
    value_sum[...] = values[keys.shape[0] - 1 :, :head]
    both = mine + theirs
    rows = sums[0].shape[0]
    for i, out in enumerate(sums):
        out[...] = both[shard_rows + i * rows : shard_rows + (i + 1) * rows]


def by_rows(kernel, name, rows, moving, fixed, outs, flops=0, grant=20):
    steps = moving[0][0].shape[moving[0][1]] // rows

    def spec(values, cut):
        if cut is None:
            return pl.BlockSpec(values.shape, lambda i: (0,) * len(values.shape))
        if cut == 0:
            return pl.BlockSpec((rows, values.shape[1]), lambda i: (i, 0))
        return pl.BlockSpec((values.shape[0], rows), lambda i: (0, i))

    arrays = [values for values, _ in moving] + fixed
    moved = sum(values.size * values.dtype.itemsize for values in arrays + [o for o, _ in outs])
    return pl.pallas_call(
        kernel,
        grid=(steps,),
        in_specs=[spec(*entry) for entry in moving] + [spec(values, None) for values in fixed],
        out_specs=[spec(*entry) for entry in outs],
        out_shape=[entry[0] for entry in outs],
        compiler_params=pltpu.CompilerParams(vmem_limit_bytes=grant << 20),
        cost_estimate=pl.CostEstimate(flops=flops, bytes_accessed=moved, transcendentals=0),
        name=name,
    )(*arrays)


def rotate(values, cosine, sine):
    half = ROT // 2
    first = values[..., :half, :]
    second = values[..., half:ROT, :]
    return jnp.concatenate(
        [first * cosine - second * sine, second * cosine + first * sine, values[..., ROT:, :]],
        axis=-2,
    )


def allowed_pairs(block, key_block, start, last):
    key_index = block * key_block + lax.broadcasted_iota(
        jnp.int32, (key_block, start.shape[1]), 0
    )
    return (key_index >= start) & (key_index <= last)


def over_blocks(starts, at, begin, block_rows, key_block, body):
    shift = key_block.bit_length() - 1
    lo = starts[at * block_rows] >> shift
    hi = (begin + (block_rows - 1) >> shift) + 1
    a = starts[at * block_rows + block_rows - 1] + (key_block - 1) >> shift
    b = begin + 1 >> shift

    def step(block, carry):
        inside = (block >= a) & (block < b)

        @pl.when(inside)
        def _():
            body(block, False)

        @pl.when(jnp.logical_not(inside))
        def _():
            body(block, True)

        return carry

    lax.fori_loop(lo, hi, step, 0)


def spread_heads(pairs, heads, head, block):
    for h in range(heads):
        for wide, tall in pairs:
            wide[:, pl.ds(h * block, block)] = tall[pl.ds(h * head, head), :]


def forward_kernel(
    before, heads, head, key_block, starts, query, pair, start, out, out_low, logsum,
    wide, best, total, accum, first, last,
):
    block_rows = query.shape[1]
    at = pl.program_id(0) * pl.num_programs(1) + pl.program_id(1)
    begin = before + pl.program_id(1) * block_rows
    factor = head**-0.5 * LOG2E
    best[...] = jnp.full(best.shape, NEGATIVE, jnp.float32)
    total[...] = jnp.zeros(total.shape, jnp.float32)
    accum[...] = jnp.zeros(accum.shape, jnp.float32)
    spread_heads([(wide, query)], heads, head, block_rows)
    index = begin + lax.broadcasted_iota(jnp.int32, (1, block_rows), 1)
    for h in range(heads):
        first[:, pl.ds(h * block_rows, block_rows)] = start[...]
        last[:, pl.ds(h * block_rows, block_rows)] = index

    def body(block, masked):
        keys = pl.ds(pl.multiple_of(block * key_block, key_block), key_block)
        key = pair[0, :head, keys].T
        value = pair[0, head:, keys]
        value = jnp.concatenate([value, jnp.ones((8, key_block), jnp.bfloat16)], axis=0)
        scores = dot(key, wide[...], 1, 0) * factor
        if masked:
            allowed = allowed_pairs(block, key_block, first[...], last[...])
            scores = jnp.where(allowed, scores, NEGATIVE)
        old = best[...]
        fresh = jnp.maximum(old, jnp.max(scores, axis=0, keepdims=True))
        weights = jnp.exp2(scores - fresh).astype(jnp.bfloat16)
        shrink = jnp.exp2(old - fresh)
        best[...] = fresh
        product = dot(value, weights, 1, 0)
        accum[...] = accum[...] * shrink + product[:head]
        total[...] = total[...] * shrink + product[head : head + 1]

    over_blocks(starts, at, begin, block_rows, key_block, body)
    scaled = accum[...] / total[...]
    sums = best[...] + jnp.log(total[...]) * LOG2E
    for h in range(heads):
        columns = slice(h * block_rows, (h + 1) * block_rows)
        rows = pl.ds(h * head, head)
        out[rows, :] = scaled[:, columns]
        logsum[pl.ds(h, 1), :] = sums[:, columns]
    out_low[...] = out[...].astype(jnp.bfloat16).T


def backward_kernel(
    before, heads, head, key_block, micro_at, starts, query, pair, start, grad, out, logsum, cosine, sine,
    query_grad, pair_grad,
    wide, wide_grad, query_sum, pair_sum, sums, delta, first, last,
):
    block_rows = query.shape[1]
    begin = before + pl.program_id(0) * block_rows
    scale = head**-0.5

    @pl.when(pl.program_id(0) == 0)
    def _():
        pair_sum[...] = jnp.zeros(pair_sum.shape, jnp.float32)

    query_sum[...] = jnp.zeros(query_sum.shape, jnp.float32)
    spread_heads([(wide, query), (wide_grad, grad)], heads, head, block_rows)
    index = begin + lax.broadcasted_iota(jnp.int32, (1, block_rows), 1)
    for h in range(heads):
        rows = pl.ds(h * head, head)
        columns = pl.ds(h * block_rows, block_rows)
        first[:, columns] = start[...]
        last[:, columns] = index
        sums[:, columns] = logsum[pl.ds(h, 1), :]
        delta[:, columns] = jnp.sum(
            grad[rows, :].astype(jnp.float32) * out[rows, :], axis=0, keepdims=True
        )

    def body(block, masked):
        keys = pl.ds(pl.multiple_of(block * key_block, key_block), key_block)
        key_wide = pair[0, :head, keys]
        key = key_wide.T
        value = pair[0, head:, keys].T
        scores = dot(key, wide[...], 1, 0) * (scale * LOG2E)
        probs = jnp.exp2(scores - sums[...])
        if masked:
            allowed = allowed_pairs(block, key_block, first[...], last[...])
            probs = jnp.where(allowed, probs, 0.0)
        pair_sum[head:, keys] += dot(wide_grad[...], probs.astype(jnp.bfloat16), 1, 1)
        prob_grad = dot(value, wide_grad[...], 1, 0)
        score_grad = (probs * (prob_grad - delta[...])).astype(jnp.bfloat16)
        pair_sum[:head, keys] += dot(wide[...], score_grad, 1, 1)
        query_sum[...] += dot(key_wide, score_grad, 1, 0)

    at = micro_at * pl.num_programs(0) + pl.program_id(0)
    over_blocks(starts, at, begin, block_rows, key_block, body)
    half = ROT // 2
    turned_heads = []
    for h in range(heads):
        value = query_sum[:, pl.ds(h * block_rows, block_rows)] * scale
        near, far = value[:half], value[half:ROT]
        turned = jnp.concatenate(
            [
                near * cosine[...] + far * sine[...],
                far * cosine[...] - near * sine[...],
                value[ROT:],
            ],
            axis=0,
        )
        turned_heads.append(turned.astype(jnp.bfloat16))
    query_grad[...] = jnp.concatenate(turned_heads, axis=0).T

    @pl.when(pl.program_id(0) == pl.num_programs(0) - 1)
    def _():
        pair_grad[:head, :] = (pair_sum[:head, :] * scale).astype(jnp.bfloat16)
        pair_grad[head:, :] = pair_sum[head:, :].astype(jnp.bfloat16)


def attention_cost(micro, rows, length, products):
    pairs = micro * (rows // 64) * length * 2 * length
    return pl.CostEstimate(
        flops=2 * products * 64 * pairs, bytes_accessed=8 * micro * rows * length, transcendentals=pairs
    )


def attend_forward(start, query, pair, before, heads, head):
    micro, _, window = pair.shape
    rows, count = query.shape
    length = count // micro
    query_block, key_block = forward_blocks
    blocks = length // query_block
    spread = heads * query_block
    column = lambda m, i, starts: (0, m * blocks + i)
    tall = pl.BlockSpec((rows, query_block), column)
    return pl.pallas_call(
        functools.partial(forward_kernel, before, heads, head, key_block),
        grid_spec=pltpu.PrefetchScalarGridSpec(
            num_scalar_prefetch=1,
            grid=(micro, blocks),
            in_specs=[
                tall,
                pl.BlockSpec((1, 2 * head, window), lambda m, i, starts: (m, 0, 0)),
                pl.BlockSpec((1, query_block), column),
            ],
            out_specs=[
                tall,
                pl.BlockSpec((query_block, rows), lambda m, i, starts: (m * blocks + i, 0)),
                pl.BlockSpec((heads, query_block), column),
            ],
            scratch_shapes=[
                pltpu.VMEM((head, spread), jnp.bfloat16),
                pltpu.VMEM((1, spread), jnp.float32),
                pltpu.VMEM((1, spread), jnp.float32),
                pltpu.VMEM((head, spread), jnp.float32),
                pltpu.VMEM((1, spread), jnp.int32),
                pltpu.VMEM((1, spread), jnp.int32),
            ],
        ),
        out_shape=[
            jax.ShapeDtypeStruct((rows, count), jnp.float32),
            jax.ShapeDtypeStruct((count, rows), jnp.bfloat16),
            jax.ShapeDtypeStruct((heads, count), jnp.float32),
        ],
        compiler_params=pltpu.CompilerParams(vmem_limit_bytes=40 << 20),
        cost_estimate=attention_cost(micro, rows, length, 2),
        name="attend_forward",
    )(start, query, pair, start.reshape(1, count))


def attend_backward(at, start, query, pair, grad, out, logsum, cosine, sine, before, heads, head):
    micro, _, window = pair.shape
    rows, count = query.shape
    length = count // micro
    query_block, key_block = backward_blocks
    blocks = length // query_block
    spread = heads * query_block
    column = lambda i, starts: (0, at * blocks + i)
    tall = pl.BlockSpec((rows, query_block), column)
    table = pl.BlockSpec((ROT // 2, query_block), column)
    return pl.pallas_call(
        functools.partial(backward_kernel, before, heads, head, key_block, at),
        grid_spec=pltpu.PrefetchScalarGridSpec(
            num_scalar_prefetch=1,
            grid=(blocks,),
            in_specs=[
                tall,
                pl.BlockSpec((1, 2 * head, window), lambda i, starts: (at, 0, 0)),
                pl.BlockSpec((1, query_block), column),
                tall,
                tall,
                pl.BlockSpec((heads, query_block), column),
                table,
                table,
            ],
            out_specs=[
                pl.BlockSpec((query_block, rows), lambda i, starts: (i, 0)),
                pl.BlockSpec((2 * head, window), lambda i, starts: (0, 0)),
            ],
            scratch_shapes=[
                pltpu.VMEM((head, spread), jnp.bfloat16),
                pltpu.VMEM((head, spread), jnp.bfloat16),
                pltpu.VMEM((head, spread), jnp.float32),
                pltpu.VMEM((2 * head, window), jnp.float32),
                pltpu.VMEM((1, spread), jnp.float32),
                pltpu.VMEM((1, spread), jnp.float32),
                pltpu.VMEM((1, spread), jnp.int32),
                pltpu.VMEM((1, spread), jnp.int32),
            ],
        ),
        out_shape=[
            jax.ShapeDtypeStruct((length, rows), jnp.bfloat16),
            jax.ShapeDtypeStruct((2 * head, window), jnp.bfloat16),
        ],
        compiler_params=pltpu.CompilerParams(vmem_limit_bytes=40 << 20),
        cost_estimate=attention_cost(1, rows, length, 5),
        name="attend_backward",
    )(start, query, pair, start.reshape(1, count), grad, out, logsum, cosine, sine)


def shards(
    tokens,
    segments,
    query_weight,
    query_bias,
    key_weight,
    key_bias,
    value_weight,
    value_bias,
    output_weight,
    output_bias,
    upward_weight,
    upward_bias,
    down_weight,
    down_bias,
    attend_gain,
    attend_bias,
    dense_gain,
    dense_bias,
    cotangent,
):
    low = jnp.bfloat16
    micro, _, length, width = tokens.shape
    count = micro * length
    head = key_weight.shape[1]
    query_width = query_bias.shape[0]
    heads = query_width // head
    hidden_width = upward_bias.shape[0]
    devices = lax.axis_size("fsdp") * lax.axis_size("ctx")
    reach = lax.axis_size("ctx") // 2
    before = reach * length
    window = before + length
    core = lax.axis_index("tp")
    stages = all_bits()
    deep = [s for s in stages if s[0] == "ctx" and s[1] > 1]
    near = [s for s in stages if s[0] == "ctx" and s[1] == 1]
    side = [s for s in stages if s[0] == "fsdp"]

    first_half = core == 0

    def halves(own, other):
        return jnp.where(first_half, own, other), jnp.where(first_half, other, own)

    shard_rows = key_weight.shape[0]
    segment_piece = (segments + 1).astype(low).reshape(-1, head)
    piece_rows = max(shard_rows, segment_piece.shape[0])

    def padded(values):
        return jnp.pad(values, ((0, piece_rows - values.shape[0]), (0, 0)))

    early_piece = jnp.concatenate(
        [
            padded(jnp.where(first_half, key_weight, value_weight)),
            padded(segment_piece),
            padded(query_weight),
        ],
        axis=1,
    )
    early = (early_piece[None], [])
    up = (upward_weight[None], [])
    down = (jnp.concatenate([down_weight.T, output_weight.T], axis=1)[None], [])
    up_order = deep + side + near
    down_order = deep + near + side
    early_order = deep + side + near
    for stage in early_order:
        if stage == early_order[-1]:
            early = (after(early[0], up[0], down[0]), early[1])
        early = gather_step(early, stage)
        if stage == early_order[0]:
            up = gather_step((after(up[0], early[0]), []), up_order[0])
            down = gather_step((after(down[0], early[0]), []), down_order[0])
    early_all = early[0]
    w_pair = early_all[:, :shard_rows, :head].reshape(width, head)
    w_query = early_all[:, :shard_rows, 2 * head :].reshape(width, query_width)
    segment_all = early_all[:, : segment_piece.shape[0], head : 2 * head].reshape(
        lax.axis_size("fsdp"), lax.axis_size("ctx"), micro, length
    )

    mine = lax.dynamic_index_in_dim(segment_all, lax.axis_index("fsdp"), 0, keepdims=False)
    reached = jnp.concatenate([jnp.zeros((reach,) + mine.shape[1:], low), mine])
    seen = lax.dynamic_slice_in_dim(reached, lax.axis_index("ctx"), reach + 1)
    seen = jnp.transpose(seen, (1, 0, 2)).reshape(micro, window).astype(jnp.int32)
    local = segments[:, 0] + 1
    start = jnp.sum((seen[:, None, :] < local[:, :, None]).astype(jnp.int32), axis=2).reshape(count)
    index = before + jnp.arange(length, dtype=jnp.int32)
    positions = jnp.tile(index, micro) - start
    freqs = jnp.exp(
        jnp.arange(ROT // 2, dtype=jnp.float32) * (-2.0 * math.log(10000.0) / ROT)
    )
    angle = freqs[:, None] * positions.reshape(1, count).astype(jnp.float32)
    cosine, sine = jnp.cos(angle), jnp.sin(angle)
    pair_cosine = jnp.where(first_half, cosine, 1.0)
    pair_sine = jnp.where(first_half, sine, 0.0)

    inputs = tokens.reshape(count, width)
    wide = jax.ShapeDtypeStruct((count, width), low)
    attend_in, dense_in = by_rows(
        norm_kernel,
        "norms",
        256,
        [(inputs, 0)],
        [attend_gain, attend_bias, dense_gain, dense_bias],
        [(wide, 0), (wide, 0)],
        grant=56,
    )

    def by_micro(values):
        return jnp.transpose(values.reshape(head, micro, length), (1, 0, 2)).reshape(-1, length)

    def by_token(values):
        return jnp.transpose(values.reshape(micro, head, length), (1, 0, 2)).reshape(head, count)

    pair_lin = dot(w_pair, attend_in, 0, 1) + jnp.where(first_half, key_bias, value_bias)[:, None]
    pair_mine = by_micro(rotate(pair_lin, pair_cosine, pair_sine).astype(low))
    context = lax.axis_size("ctx")
    for i in range(1, len(stages) - 2):
        up = gather_step(up, up_order[i])
        down = gather_step(down, down_order[i])

    def forward(values, d):
        return lax.ppermute(values, "ctx", [(i, i + d) for i in range(context - d)])

    farthest = forward(pair_mine, reach)
    held = pair_mine
    while held.shape[1] < before:
        held = jnp.concatenate([forward(held, held.shape[1] // length), held], axis=1)
    pair_half = jnp.concatenate([farthest, held], axis=1)
    pair_half = after(pair_half, up[0], down[0])
    up = gather_step(up, up_order[-2])
    down = gather_step(down, down_order[-2])
    pair_other = partner(pair_half, ("tp", 1))
    pair = jnp.concatenate(
        [side_half.reshape(micro, head, window) for side_half in halves(pair_half, pair_other)],
        axis=1,
    )

    query_lin = dot(w_query, attend_in, 0, 1) + query_bias[:, None]
    query = (
        rotate(query_lin.reshape(heads, head, count), cosine, sine)
        .astype(low)
        .reshape(query_width, count)
    )
    query = after(query, up[0], down[0])
    attended, attended_low, logsum = attend_forward(start, query, pair, before, heads, head)
    w_upward = gather_step(up, up_order[-1])[0].reshape(width, hidden_width)
    w_down = gather_step(down, down_order[-1])[0].reshape(width, hidden_width + query_width)
    w_down, w_output = w_down[:, :hidden_width], w_down[:, hidden_width:]

    grad_low = cotangent.reshape(count, width)
    hidden_pre = dot(after(dense_in, attended_low), w_upward, 1, 0) + upward_bias
    normal_cdf = 0.5 * (1.0 + lax.erf(hidden_pre * (1.0 / math.sqrt(2.0))))
    normal_pdf = jnp.exp(-0.5 * hidden_pre * hidden_pre) * (1.0 / math.sqrt(2.0 * math.pi))
    hidden = (hidden_pre * normal_cdf).astype(low)
    slope = normal_cdf + hidden_pre * normal_pdf
    pre_grad = (dot(grad_low, w_down, 1, 0) * slope).astype(low)

    def by_device(values):
        return values.astype(low).reshape(devices, shard_rows, values.shape[1])

    up_order = side + near + deep[::-1]
    down_order = near + side + deep[::-1]
    up = (by_device(dot(dense_in, pre_grad, 0, 0)), stages)
    row_major = Layout(major_to_minor=(0, 1))
    down = jnp.concatenate(
        [
            with_layout_constraint(dot(grad_low, values, 0, 0).astype(low), row_major)
            for values in (hidden, attended_low)
        ],
        axis=1,
    )
    down = (by_device(down), stages)
    up = scatter_step(up, up_order[0])
    down = scatter_step(down, down_order[0])

    attended_grad = dot(w_output, grad_low, 0, 1).astype(low)
    query_grads, pair_grads = [], []
    for at in range(micro):
        if at == micro - 1:
            attended_grad = after(attended_grad, up[0], down[0])
            up = scatter_step(up, up_order[1])
            down = scatter_step(down, down_order[1])
        query_part, pair_part = attend_backward(
            at, start, query, pair, attended_grad, attended, logsum, cosine, sine, before, heads, head
        )
        query_grads.append(query_part)
        pair_grads.append(pair_part)
    query_grad = jnp.concatenate(query_grads, axis=0)
    pair_back = jnp.stack(pair_grads).reshape(micro, 2, head, window)
    query_grad, pair_back, up_held, down_held = lax.optimization_barrier(
        (query_grad, pair_back, up[0], down[0])
    )

    keep, send = halves(pair_back[:, 0], pair_back[:, 1])
    summed = (keep.astype(jnp.float32) + partner(send, ("tp", 1)).astype(jnp.float32)).astype(low)
    summed = summed.reshape(micro * head, window)
    asked_order = side + near + deep[::-1]
    asked = by_device(dot(attend_in, query_grad, 0, 0))
    summed, asked, hidden_late, pre_grad_late, grad_late = lax.optimization_barrier(
        (summed, asked, hidden, pre_grad, grad_low)
    )
    asked = scatter_step((asked, stages), asked_order[0])

    def backward(values, d):
        return lax.ppermute(values.astype(low), "ctx", [(i + d, i) for i in range(context - d)])

    farthest = backward(summed[:, :length], reach)
    held = summed[:, length:].astype(jnp.float32)
    while held.shape[1] > length:
        half = held.shape[1] // 2
        got = backward(held[:, :half], half // length)
        held = held[:, half:] + got.astype(jnp.float32)
        if half == before // 2:
            up = scatter_step((after(up_held, held), up[1]), up_order[2])
            down = scatter_step((after(down_held, held), down[1]), down_order[2])
    pair_sum = held + farthest.astype(jnp.float32)
    asked = scatter_step(asked, asked_order[1])
    branches = (dot(attended_low, w_output, 1, 1) + dot(hidden_late, w_down, 1, 1)).astype(low)
    dense_part = dot(pre_grad_late, w_upward, 1, 1)
    early_sums = jnp.concatenate(
        [
            jnp.sum(grad_late.astype(jnp.float32), axis=0),
            jnp.sum(pre_grad.astype(jnp.float32), axis=0),
            jnp.sum(query_grad.astype(jnp.float32), axis=0),
        ]
    )
    pair_sum, asked_held, dense_part, branches, early_sums = lax.optimization_barrier(
        (pair_sum, asked[0], dense_part, branches, early_sums)
    )
    asked = scatter_step((asked_held, asked[1]), asked_order[2])
    branches_other = partner(branches, ("tp", 1))
    pair_low = rotate(by_token(pair_sum), pair_cosine, -pair_sine).astype(low)

    norm_part, sums = by_rows(
        part_kernel,
        "parts",
        256,
        [(query_grad, 0), (pair_low, 1), (w_query, None), (w_pair, None), (dense_part, 0), (inputs, 0)],
        [attend_gain, dense_gain],
        [(wide, 0), (jax.ShapeDtypeStruct((4, width), jnp.float32), None)],
        2 * count * width * (query_width + head),
    )
    pad_head = ((0, 0), (0, LANES - head))
    half_grad = jnp.pad(dot(attend_in, pair_low, 0, 1), pad_head).astype(low)
    small = jnp.concatenate(
        [
            sums.reshape(-1),
            jnp.pad(jnp.sum(pair_low.astype(jnp.float32), axis=1), (0, LANES - head)),
            early_sums,
        ]
    ).reshape(-1, LANES)
    small_rows = small.shape[0]
    small_high = lax.reduce_precision(small, 8, 7)
    fill = jnp.zeros((-(shard_rows + 2 * small_rows) % 16, LANES), low)
    every = jnp.concatenate([small_high.astype(low), (small - small_high).astype(low), fill])
    every = jnp.broadcast_to(every[None], (devices,) + every.shape)
    payload = jnp.concatenate([half_grad.reshape(devices, shard_rows, LANES), every], axis=1)
    payload, norm_part, asked_held, up_held, down_held, branches_other = lax.optimization_barrier(
        (payload, norm_part, asked[0], up[0], down[0], branches_other)
    )
    got = lax.all_to_all(payload, ("fsdp", "ctx"), 0, 0)
    norm_other = partner(norm_part, ("tp", 1))
    asked = (asked_held, asked[1])
    for i in range(3, len(stages)):
        asked = scatter_step(asked, asked_order[i])
    up, down = (up_held, up[1]), (down_held, down[1])
    for i in range(3, len(stages)):
        up = scatter_step(up, up_order[i])
        down = scatter_step(down, down_order[i])
    tokens_grad = by_rows(
        back_kernel,
        "back",
        256,
        [(norm_part, 0), (norm_other, 0), (grad_low, 0), (inputs, 0)],
        [],
        [(wide, 0)],
    )[0]
    result = by_rows(
        result_kernel,
        "results",
        256,
        [(branches, 0), (branches_other, 0), (inputs, 0)],
        [output_bias, down_bias],
        [(wide, 0)],
    )[0]
    got, tokens_grad, result, grad_query, grad_up, grad_down = lax.optimization_barrier(
        (got, tokens_grad, result, asked[0][0], up[0][0], down[0][0])
    )

    def rows_of(count):
        return jax.ShapeDtypeStruct((count, LANES), jnp.float32)

    shared_rows = 4 * width // LANES + 1
    sizes = [width // LANES, hidden_width // LANES, query_width // LANES, width // LANES]
    own, out_b, up_b, q_b, down_b = pl.pallas_call(
        functools.partial(sum_kernel, shard_rows, shared_rows, small_rows),
        out_shape=[rows_of(shard_rows + shared_rows)] + [rows_of(size) for size in sizes],
        name="sums",
    )(got)
    other = partner(own, ("tp", 1))
    outs = pl.pallas_call(
        functools.partial(last_kernel, shard_rows, head),
        out_shape=[jax.ShapeDtypeStruct((shard_rows, head), jnp.float32)] * 2
        + [jax.ShapeDtypeStruct((1, head), jnp.float32)] * 2
        + [rows_of(width // LANES)] * 4,
        in_specs=[pl.BlockSpec(memory_space=pltpu.SMEM)] + [pl.BlockSpec(memory_space=pltpu.VMEM)] * 2,
        name="last",
    )(core.astype(jnp.int32).reshape(1), own, other)
    grad_key, grad_value, k_b, v_b = outs[0], outs[1], outs[2].reshape(-1), outs[3].reshape(-1)
    g_gain, g_shift, d_gain, d_shift = [values.reshape(-1) for values in outs[4:]]
    out_b, up_b, q_b, down_b = [values.reshape(-1) for values in (out_b, up_b, q_b, down_b)]
    shape = (micro, 1, length, width)
    return (
        result.reshape(shape),
        tokens_grad.reshape(shape),
        grad_query,
        q_b,
        grad_key,
        k_b,
        grad_value,
        v_b,
        grad_down[:, hidden_width:].T,
        out_b,
        grad_up,
        up_b,
        grad_down[:, :hidden_width].T,
        down_b,
        g_gain,
        g_shift,
        d_gain,
        d_shift,
    )


def solution(mesh):
    return jax.shard_map(
        shards,
        mesh=mesh,
        in_specs=(
            P(None, "fsdp", "ctx", None),
            P(None, "fsdp", "ctx"),
            P(("fsdp", "ctx"), "tp"),
            P("tp"),
            P(("fsdp", "ctx"), None),
            P(),
            P(("fsdp", "ctx"), None),
            P(),
            P("tp", ("fsdp", "ctx")),
            P(),
            P(("fsdp", "ctx"), "tp"),
            P("tp"),
            P("tp", ("fsdp", "ctx")),
            P(),
            P(),
            P(),
            P(),
            P(),
            P(None, "fsdp", "ctx", None),
        ),
        out_specs=(
            P(None, "fsdp", "ctx", None),
            P(None, "fsdp", "ctx", None),
            P(("fsdp", "ctx"), "tp"),
            P("tp"),
            P(("fsdp", "ctx"), None),
            P(),
            P(("fsdp", "ctx"), None),
            P(),
            P("tp", ("fsdp", "ctx")),
            P(),
            P(("fsdp", "ctx"), "tp"),
            P("tp"),
            P("tp", ("fsdp", "ctx")),
            P(),
            P(),
            P(),
            P(),
            P(),
        ),
        check_vma=False,
    )
```

```python
import functools
import math

import jax
import jax.numpy as jnp
from jax import lax
from jax.experimental.layout import Layout, with_layout_constraint
from jax.experimental import pallas as pl
from jax.experimental.pallas import tpu as pltpu
from jax.sharding import PartitionSpec as P

ROT = 16
NEGATIVE = -1e30
EPSILON = 1e-05
LOG2E = math.log2(math.e)
LANES = 128
forward_blocks = (512, 512)
backward_blocks = (256, 256)


def dot(left, right, left_dim, right_dim):
    return lax.dot_general(
        left,
        right,
        (((left_dim,), (right_dim,)), ((), ())),
        preferred_element_type=jnp.float32,
    )


def axis_bits(name):
    return [1 << b for b in reversed(range(lax.axis_size(name).bit_length() - 1))]


def all_bits():
    return [("fsdp", d) for d in axis_bits("fsdp")] + [("ctx", d) for d in axis_bits("ctx")]


def partner(values, stage):
    name, distance = stage
    pairs = [(i, i ^ distance) for i in range(lax.axis_size(name))]
    return lax.ppermute(values, name, pairs)


def own_bit(stage):
    name, distance = stage
    return (lax.axis_index(name) // distance) % 2 == 1


def gather_join(state, stage, other):
    held, done = state
    rank = {other_stage: i for i, other_stage in enumerate(all_bits())}
    low = 1 << sum(rank[earlier] > rank[stage] for earlier in done)
    piece = held.shape[1:]
    split = held.reshape((held.shape[0] // low, 1, low) + piece)
    other = other.reshape(split.shape)
    upper = own_bit(stage)
    held = jnp.concatenate(
        [jnp.where(upper, other, split), jnp.where(upper, split, other)], axis=1
    ).reshape((2 * held.shape[0],) + piece)
    return held, done + [stage]


def scatter_send(state, stage):
    held, left = state
    rank = {other: i for i, other in enumerate(all_bits())}
    low = 1 << sum(rank[other] > rank[stage] for other in left if other != stage)
    piece = held.shape[1:]
    split = held.reshape((held.shape[0] // (2 * low), 2, low) + piece)
    upper = own_bit(stage).astype(jnp.int32)
    shape = (held.shape[0] // 2,) + piece
    send = lax.dynamic_index_in_dim(split, 1 - upper, 1, keepdims=False).reshape(shape)
    keep = lax.dynamic_index_in_dim(split, upper, 1, keepdims=False).reshape(shape)
    return (keep, [other for other in left if other != stage]), partner(send, stage)


def scatter_join(kept, other):
    keep, left = kept
    total = keep.astype(jnp.float32) + other.astype(jnp.float32)
    return (total.astype(jnp.bfloat16) if left else total), left


def scatter_rest(state, order):
    for stage in order:
        state = scatter_step(state, stage)
    return state


def gather_step(state, stage):
    return gather_join(state, stage, partner(state[0], stage))


def scatter_step(state, stage):
    return scatter_join(*scatter_send(state, stage))


def after(values, *others):
    return lax.optimization_barrier((values,) + others)[0]


def deep_rank():
    return lax.axis_index("ctx") // 2


def deep_send(terms, axis):
    size = terms.shape[axis]
    own, *others = [
        lax.dynamic_index_in_dim(terms, deep_rank() ^ mask, axis, keepdims=False)
        for mask in range(size)
    ]
    return own, [partner(values, ("ctx", 2 * mask + 2)) for mask, values in enumerate(others)]


def sum_all(values):
    return sum(other.astype(jnp.float32) for other in values)


def together(*values):
    return lax.optimization_barrier(values)


def norm_parts(values):
    centre = values - jnp.mean(values, axis=-1, keepdims=True)
    spread = lax.rsqrt(jnp.mean(centre * centre, axis=-1, keepdims=True) + EPSILON)
    return centre * spread, spread


def as_row(values):
    return values[...].reshape(1, values.shape[0])


def norm_kernel(
    tokens, attend_gain, attend_bias, dense_gain, dense_bias, attend_in, dense_in
):
    normed, _ = norm_parts(tokens[...].astype(jnp.float32))
    attend_in[...] = (normed * as_row(attend_gain) + as_row(attend_bias)).astype(jnp.bfloat16)
    dense_in[...] = (normed * as_row(dense_gain) + as_row(dense_bias)).astype(jnp.bfloat16)


def part_kernel(
    shard_rows, query_grad, pair_low, w_query, w_pair, dense_part, tokens, attend_gain, attend_bias,
    dense_gain, early, norm_part, payload, sums, pair_grad, pair_sum,
):
    step = pl.program_id(0)
    attend_part = dot(query_grad[...], w_query[...], 1, 1) + dot(pair_low[...].T, w_pair[...], 1, 1)
    dense = dense_part[...]
    normed, _ = norm_parts(tokens[...].astype(jnp.float32))
    norm_part[...] = (
        attend_part * as_row(attend_gain) + dense * as_row(dense_gain)
    ).astype(jnp.bfloat16)
    attend_in = (normed * as_row(attend_gain) + as_row(attend_bias)).astype(jnp.bfloat16)

    @pl.when(step == 0)
    def _():
        sums[...] = jnp.zeros(sums.shape, jnp.float32)
        pair_grad[...] = jnp.zeros(pair_grad.shape, jnp.float32)
        pair_sum[...] = jnp.zeros(pair_sum.shape, jnp.float32)

    rows = [attend_part * normed, attend_part, dense * normed, dense]
    sums[...] += jnp.concatenate([jnp.sum(row, axis=0, keepdims=True) for row in rows])
    pair_grad[...] += dot(pair_low[...], attend_in, 1, 0)
    pair_sum[...] += jnp.sum(pair_low[...].astype(jnp.float32), axis=1, keepdims=True)

    @pl.when(step == pl.num_programs(0) - 1)
    def _():
        head, width = pair_grad.shape
        fill = jnp.zeros((width, LANES - head), jnp.float32)
        grads = jnp.concatenate([pair_grad[...].T, fill], axis=1).astype(jnp.bfloat16)
        values = sums[...]
        small = [
            values[i : i + 1, j : j + LANES] for i in range(4) for j in range(0, width, LANES)
        ]
        pair_row = jnp.broadcast_to(pair_sum[...], (head, LANES)).T[:1]
        small.append(jnp.concatenate([pair_row, jnp.zeros((1, LANES - head), jnp.float32)], axis=1))
        small = jnp.concatenate(small + [early[...]])
        spare = payload.shape[1] - small.shape[0] - padded_rows(shard_rows)
        small = jnp.concatenate([small, jnp.zeros((spare, LANES), jnp.float32)]).astype(jnp.bfloat16)
        for device in range(payload.shape[0]):
            piece = grads[device * shard_rows : (device + 1) * shard_rows]
            payload[device, :shard_rows] = piece
            payload[device, padded_rows(shard_rows) :] = small


def padded_rows(rows):
    return rows + -rows % 16


def back_kernel(own, other, cotangent, tokens, tokens_grad):
    grad = own[...].astype(jnp.float32) + other[...].astype(jnp.float32)
    normed, spread = norm_parts(tokens[...].astype(jnp.float32))
    inner = (
        grad
        - jnp.mean(grad, axis=-1, keepdims=True)
        - normed * jnp.mean(grad * normed, axis=-1, keepdims=True)
    )
    tokens_grad[...] = (cotangent[...].astype(jnp.float32) + spread * inner).astype(jnp.bfloat16)


def result_kernel(own, other, tokens, first_bias, second_bias, result):
    mixed = own[...].astype(jnp.float32) + other[...].astype(jnp.float32)
    result[...] = (
        tokens[...].astype(jnp.float32) + mixed + as_row(first_bias) + as_row(second_bias)
    ).astype(jnp.bfloat16)


def sum_kernel(
    shard_rows, shared_rows, got, own, out_sum, up_sum, query_sum, out_again
):
    total = got[0].astype(jnp.float32)
    for device in range(1, got.shape[0]):
        total += got[device].astype(jnp.float32)
    small = total[padded_rows(shard_rows) :]
    own[...] = jnp.concatenate([total[:shard_rows], small[:shared_rows]])
    at = shared_rows
    for out in (out_sum, up_sum, query_sum):
        out[...] = small[at : at + out.shape[0]]
        at += out.shape[0]
    out_again[...] = out_sum[...]


def last_kernel(shard_rows, head, core, own, other, key_grad, value_grad, key_sum, value_sum, *sums):
    first = core[0] == 0
    mine, theirs = own[...], other[...]
    keys = jnp.where(first, mine, theirs)
    values = jnp.where(first, theirs, mine)
    key_grad[...] = keys[:shard_rows, :head]
    value_grad[...] = values[:shard_rows, :head]
    key_sum[...] = keys[keys.shape[0] - 1 :, :head]
    value_sum[...] = values[keys.shape[0] - 1 :, :head]
    both = mine + theirs
    rows = sums[0].shape[0]
    for i, out in enumerate(sums):
        out[...] = both[shard_rows + i * rows : shard_rows + (i + 1) * rows]


def by_rows(kernel, name, rows, moving, fixed, outs, flops=0, grant=20, scratch=()):
    steps = moving[0][0].shape[moving[0][1]] // rows

    def spec(values, cut):
        if cut is None:
            whole = (0,) * len(values.shape)
            return pl.BlockSpec(values.shape, lambda i: whole)
        if cut == 0:
            return pl.BlockSpec((rows, values.shape[1]), lambda i: (i, 0))
        return pl.BlockSpec((values.shape[0], rows), lambda i: (0, i))

    arrays = [values for values, _ in moving] + fixed
    moved = sum(values.size * values.dtype.itemsize for values in arrays + [o for o, _ in outs])
    return pl.pallas_call(
        kernel,
        grid=(steps,),
        in_specs=[spec(*entry) for entry in moving] + [spec(values, None) for values in fixed],
        out_specs=[spec(*entry) for entry in outs],
        out_shape=[entry[0] for entry in outs],
        scratch_shapes=list(scratch),
        compiler_params=pltpu.CompilerParams(vmem_limit_bytes=grant << 20),
        cost_estimate=pl.CostEstimate(flops=flops, bytes_accessed=moved, transcendentals=0),
        name=name,
    )(*arrays)


def rotate(values, cosine, sine):
    half = ROT // 2
    first = values[..., :half, :]
    second = values[..., half:ROT, :]
    return jnp.concatenate(
        [first * cosine - second * sine, second * cosine + first * sine, values[..., ROT:, :]],
        axis=-2,
    )


def allowed_pairs(block, key_block, start, last):
    key_index = block * key_block + lax.broadcasted_iota(
        jnp.int32, (key_block, start.shape[1]), 0
    )
    return (key_index >= start) & (key_index <= last)


def over_blocks(starts, at, begin, block_rows, key_block, body):
    shift = key_block.bit_length() - 1
    lo = starts[at * block_rows] >> shift
    hi = (begin + (block_rows - 1) >> shift) + 1
    a = starts[at * block_rows + block_rows - 1] + (key_block - 1) >> shift
    b = begin + 1 >> shift

    def step(block, carry):
        inside = (block >= a) & (block < b)

        @pl.when(inside)
        def _():
            body(block, False)

        @pl.when(jnp.logical_not(inside))
        def _():
            body(block, True)

        return carry

    lax.fori_loop(lo, hi, step, 0)


def spread_heads(pairs, heads, head, block):
    for h in range(heads):
        for wide, tall in pairs:
            wide[:, pl.ds(h * block, block)] = tall[pl.ds(h * head, head), :]


def forward_kernel(
    before, heads, head, key_block, starts, query, pair, start, out, out_low, logsum,
    wide, best, total, accum, first, last,
):
    block_rows = query.shape[1]
    at = pl.program_id(0) * pl.num_programs(1) + pl.program_id(1)
    begin = before + pl.program_id(1) * block_rows
    factor = head**-0.5 * LOG2E
    best[...] = jnp.full(best.shape, NEGATIVE, jnp.float32)
    total[...] = jnp.zeros(total.shape, jnp.float32)
    accum[...] = jnp.zeros(accum.shape, jnp.float32)
    spread_heads([(wide, query)], heads, head, block_rows)
    index = begin + lax.broadcasted_iota(jnp.int32, (1, block_rows), 1)
    for h in range(heads):
        first[:, pl.ds(h * block_rows, block_rows)] = start[...]
        last[:, pl.ds(h * block_rows, block_rows)] = index

    def body(block, masked):
        keys = pl.ds(pl.multiple_of(block * key_block, key_block), key_block)
        key = pair[0, :head, keys].T
        value = pair[0, head:, keys]
        value = jnp.concatenate([value, jnp.ones((8, key_block), jnp.bfloat16)], axis=0)
        scores = dot(key, wide[...], 1, 0) * factor
        if masked:
            allowed = allowed_pairs(block, key_block, first[...], last[...])
            scores = jnp.where(allowed, scores, NEGATIVE)
        old = best[...]
        fresh = jnp.maximum(old, jnp.max(scores, axis=0, keepdims=True))
        weights = jnp.exp2(scores - fresh).astype(jnp.bfloat16)
        shrink = jnp.exp2(old - fresh)
        best[...] = fresh
        product = dot(value, weights, 1, 0)
        accum[...] = accum[...] * shrink + product[:head]
        total[...] = total[...] * shrink + product[head : head + 1]

    over_blocks(starts, at, begin, block_rows, key_block, body)
    scaled = accum[...] / total[...]
    sums = best[...] + jnp.log(total[...]) * LOG2E
    for h in range(heads):
        columns = slice(h * block_rows, (h + 1) * block_rows)
        rows = pl.ds(h * head, head)
        out[rows, :] = scaled[:, columns]
        logsum[pl.ds(h, 1), :] = sums[:, columns]
    out_low[...] = out[...].astype(jnp.bfloat16).T


def backward_kernel(
    before, heads, head, key_block, starts, query, pair, start, grad, out, logsum, cosine, sine,
    query_grad, pair_grad,
    wide, wide_grad, query_sum, pair_sum, sums, delta, first, last,
):
    block_rows = query.shape[1]
    at = pl.program_id(0) * pl.num_programs(1) + pl.program_id(1)
    begin = before + pl.program_id(1) * block_rows
    scale = head**-0.5

    @pl.when(pl.program_id(1) == 0)
    def _():
        pair_sum[...] = jnp.zeros(pair_sum.shape, jnp.float32)

    query_sum[...] = jnp.zeros(query_sum.shape, jnp.float32)
    spread_heads([(wide, query), (wide_grad, grad)], heads, head, block_rows)
    index = begin + lax.broadcasted_iota(jnp.int32, (1, block_rows), 1)
    for h in range(heads):
        rows = pl.ds(h * head, head)
        columns = pl.ds(h * block_rows, block_rows)
        first[:, columns] = start[...]
        last[:, columns] = index
        sums[:, columns] = logsum[pl.ds(h, 1), :]
        delta[:, columns] = jnp.sum(
            grad[rows, :].astype(jnp.float32) * out[rows, :], axis=0, keepdims=True
        )

    def body(block, masked):
        keys = pl.ds(pl.multiple_of(block * key_block, key_block), key_block)
        key_wide = pair[0, :head, keys]
        key = key_wide.T
        value = pair[0, head:, keys].T
        scores = dot(key, wide[...], 1, 0) * (scale * LOG2E)
        probs = jnp.exp2(scores - sums[...])
        if masked:
            allowed = allowed_pairs(block, key_block, first[...], last[...])
            probs = jnp.where(allowed, probs, 0.0)
        pair_sum[head:, keys] += dot(wide_grad[...], probs.astype(jnp.bfloat16), 1, 1)
        prob_grad = dot(value, wide_grad[...], 1, 0)
        score_grad = (probs * (prob_grad - delta[...])).astype(jnp.bfloat16)
        pair_sum[:head, keys] += dot(wide[...], score_grad, 1, 1)
        query_sum[...] += dot(key_wide, score_grad, 1, 0)

    over_blocks(starts, at, begin, block_rows, key_block, body)
    half = ROT // 2
    turned_heads = []
    for h in range(heads):
        value = query_sum[:, pl.ds(h * block_rows, block_rows)] * scale
        near, far = value[:half], value[half:ROT]
        turned = jnp.concatenate(
            [
                near * cosine[...] + far * sine[...],
                far * cosine[...] - near * sine[...],
                value[ROT:],
            ],
            axis=0,
        )
        turned_heads.append(turned.astype(jnp.bfloat16))
    query_grad[...] = jnp.concatenate(turned_heads, axis=0).T

    @pl.when(pl.program_id(1) == pl.num_programs(1) - 1)
    def _():
        pair_grad[0, :head, :] = (pair_sum[:head, :] * scale).astype(jnp.bfloat16)
        pair_grad[0, head:, :] = pair_sum[head:, :].astype(jnp.bfloat16)


def attention_cost(micro, rows, length, products):
    pairs = micro * (rows // 64) * length * 2 * length
    return pl.CostEstimate(
        flops=2 * products * 64 * pairs, bytes_accessed=8 * micro * rows * length, transcendentals=pairs
    )


def attend_forward(start, query, pair, before, heads, head):
    micro, _, window = pair.shape
    rows, count = query.shape
    length = count // micro
    query_block, key_block = forward_blocks
    blocks = length // query_block
    spread = heads * query_block
    column = lambda m, i, starts: (0, m * blocks + i)
    tall = pl.BlockSpec((rows, query_block), column)
    return pl.pallas_call(
        functools.partial(forward_kernel, before, heads, head, key_block),
        grid_spec=pltpu.PrefetchScalarGridSpec(
            num_scalar_prefetch=1,
            grid=(micro, blocks),
            in_specs=[
                tall,
                pl.BlockSpec((1, 2 * head, window), lambda m, i, starts: (m, 0, 0)),
                pl.BlockSpec((1, query_block), column),
            ],
            out_specs=[
                tall,
                pl.BlockSpec((query_block, rows), lambda m, i, starts: (m * blocks + i, 0)),
                pl.BlockSpec((heads, query_block), column),
            ],
            scratch_shapes=[
                pltpu.VMEM((head, spread), jnp.bfloat16),
                pltpu.VMEM((1, spread), jnp.float32),
                pltpu.VMEM((1, spread), jnp.float32),
                pltpu.VMEM((head, spread), jnp.float32),
                pltpu.VMEM((1, spread), jnp.int32),
                pltpu.VMEM((1, spread), jnp.int32),
            ],
        ),
        out_shape=[
            jax.ShapeDtypeStruct((rows, count), jnp.float32),
            jax.ShapeDtypeStruct((count, rows), jnp.bfloat16),
            jax.ShapeDtypeStruct((heads, count), jnp.float32),
        ],
        compiler_params=pltpu.CompilerParams(vmem_limit_bytes=40 << 20),
        cost_estimate=attention_cost(micro, rows, length, 2),
        name="attend_forward",
    )(start, query, pair, start.reshape(1, count))


def attend_backward(start, query, pair, grad, out, logsum, cosine, sine, before, heads, head):
    micro, _, window = pair.shape
    rows, count = query.shape
    length = count // micro
    query_block, key_block = backward_blocks
    blocks = length // query_block
    spread = heads * query_block
    column = lambda m, i, starts: (0, m * blocks + i)
    tall = pl.BlockSpec((rows, query_block), column)
    table = pl.BlockSpec((ROT // 2, query_block), column)
    keys = pl.BlockSpec((1, 2 * head, window), lambda m, i, starts: (m, 0, 0))
    return pl.pallas_call(
        functools.partial(backward_kernel, before, heads, head, key_block),
        grid_spec=pltpu.PrefetchScalarGridSpec(
            num_scalar_prefetch=1,
            grid=(micro, blocks),
            in_specs=[
                tall,
                keys,
                pl.BlockSpec((1, query_block), column),
                tall,
                tall,
                pl.BlockSpec((heads, query_block), column),
                table,
                table,
            ],
            out_specs=[
                pl.BlockSpec((query_block, rows), lambda m, i, starts: (m * blocks + i, 0)),
                keys,
            ],
            scratch_shapes=[
                pltpu.VMEM((head, spread), jnp.bfloat16),
                pltpu.VMEM((head, spread), jnp.bfloat16),
                pltpu.VMEM((head, spread), jnp.float32),
                pltpu.VMEM((2 * head, window), jnp.float32),
                pltpu.VMEM((1, spread), jnp.float32),
                pltpu.VMEM((1, spread), jnp.float32),
                pltpu.VMEM((1, spread), jnp.int32),
                pltpu.VMEM((1, spread), jnp.int32),
            ],
        ),
        out_shape=[
            jax.ShapeDtypeStruct((count, rows), jnp.bfloat16),
            jax.ShapeDtypeStruct((micro, 2 * head, window), jnp.bfloat16),
        ],
        compiler_params=pltpu.CompilerParams(vmem_limit_bytes=32 << 20),
        cost_estimate=attention_cost(micro, rows, length, 5),
        name="attend_backward",
    )(start, query, pair, start.reshape(1, count), grad, out, logsum, cosine, sine)


def shards(
    tokens,
    segments,
    query_weight,
    query_bias,
    key_weight,
    key_bias,
    value_weight,
    value_bias,
    output_weight,
    output_bias,
    upward_weight,
    upward_bias,
    down_weight,
    down_bias,
    attend_gain,
    attend_bias,
    dense_gain,
    dense_bias,
    cotangent,
):
    low = jnp.bfloat16
    micro, _, length, width = tokens.shape
    count = micro * length
    head = key_weight.shape[1]
    query_width = query_bias.shape[0]
    heads = query_width // head
    hidden_width = upward_bias.shape[0]
    devices = lax.axis_size("fsdp") * lax.axis_size("ctx")
    reach = lax.axis_size("ctx") // 2
    before = reach * length
    window = before + length
    core = lax.axis_index("tp")
    stages = all_bits()
    deep = [s for s in stages if s[0] == "ctx" and s[1] > 1]
    near = [s for s in stages if s[0] == "ctx" and s[1] == 1]
    side = [s for s in stages if s[0] == "fsdp"]

    first_half = core == 0

    def halves(own, other):
        return jnp.where(first_half, own, other), jnp.where(first_half, other, own)

    shard_rows = key_weight.shape[0]
    segment_piece = (segments + 1).astype(low).reshape(-1, head)
    piece_rows = max(shard_rows, segment_piece.shape[0])

    def padded(values):
        return jnp.pad(values, ((0, piece_rows - values.shape[0]), (0, 0)))

    early_piece = jnp.concatenate(
        [
            padded(jnp.where(first_half, key_weight, value_weight)),
            padded(segment_piece),
            padded(query_weight),
        ],
        axis=1,
    )
    early = (early_piece[None], [])
    up = (upward_weight[None], [])
    down = (jnp.concatenate([down_weight.T, output_weight.T], axis=1)[None], [])
    up_order = deep + side + near
    down_order = deep + near + side
    early_order = deep + side + near
    for stage in early_order:
        early = gather_step(early, stage)
        if stage == early_order[0]:
            up = gather_step((after(up[0], early[0]), []), up_order[0])
            down = gather_step((after(down[0], early[0]), []), down_order[0])
    early_all = after(early[0], up[0], down[0])
    w_pair = early_all[:, :shard_rows, :head].reshape(width, head)
    w_query = early_all[:, :shard_rows, 2 * head :].reshape(width, query_width)
    segment_all = early_all[:, : segment_piece.shape[0], head : 2 * head].reshape(
        lax.axis_size("fsdp"), lax.axis_size("ctx"), micro, length
    )

    mine = lax.dynamic_index_in_dim(segment_all, lax.axis_index("fsdp"), 0, keepdims=False)
    reached = jnp.concatenate([jnp.zeros((reach,) + mine.shape[1:], low), mine])
    seen = lax.dynamic_slice_in_dim(reached, lax.axis_index("ctx"), reach + 1)
    seen = jnp.transpose(seen, (1, 0, 2)).reshape(micro, window).astype(jnp.int32)
    local = segments[:, 0] + 1
    start = jnp.sum((seen[:, None, :] < local[:, :, None]).astype(jnp.int32), axis=2).reshape(count)
    index = before + jnp.arange(length, dtype=jnp.int32)
    positions = jnp.tile(index, micro) - start
    freqs = jnp.exp(
        jnp.arange(ROT // 2, dtype=jnp.float32) * (-2.0 * math.log(10000.0) / ROT)
    )
    angle = freqs[:, None] * positions.reshape(1, count).astype(jnp.float32)
    cosine, sine = jnp.cos(angle), jnp.sin(angle)
    pair_cosine = jnp.where(first_half, cosine, 1.0)
    pair_sine = jnp.where(first_half, sine, 0.0)

    inputs = tokens.reshape(count, width)
    wide = jax.ShapeDtypeStruct((count, width), low)
    attend_in, dense_in = by_rows(
        norm_kernel,
        "norms",
        256,
        [(inputs, 0)],
        [attend_gain, attend_bias, dense_gain, dense_bias],
        [(wide, 0), (wide, 0)],
        grant=56,
    )

    def by_micro(values):
        return jnp.transpose(values.reshape(head, micro, length), (1, 0, 2)).reshape(-1, length)

    def by_token(values):
        return jnp.transpose(values.reshape(micro, head, length), (1, 0, 2)).reshape(head, count)

    pair_lin = dot(w_pair, attend_in, 0, 1) + jnp.where(first_half, key_bias, value_bias)[:, None]
    pair_mine = by_micro(rotate(pair_lin, pair_cosine, pair_sine).astype(low))
    context = lax.axis_size("ctx")
    for i in range(1, len(stages) - 2):
        up = gather_step(up, up_order[i])
        down = gather_step(down, down_order[i])

    def forward(values, d):
        return lax.ppermute(values, "ctx", [(i, i + d) for i in range(context - d)])

    farthest = forward(pair_mine, reach)
    held = pair_mine
    while held.shape[1] < before:
        held = jnp.concatenate([forward(held, held.shape[1] // length), held], axis=1)
    pair_half = jnp.concatenate([farthest, held], axis=1)
    pair_half = after(pair_half, up[0], down[0])
    up = gather_step((after(up[0], pair_mine), up[1]), up_order[-2])
    down = gather_step((after(down[0], pair_mine), down[1]), down_order[-2])
    pair_other = partner(pair_half, ("tp", 1))
    pair = jnp.concatenate(
        [side_half.reshape(micro, head, window) for side_half in halves(pair_half, pair_other)],
        axis=1,
    )

    query_lin = dot(w_query, attend_in, 0, 1) + query_bias[:, None]
    query = (
        rotate(query_lin.reshape(heads, head, count), cosine, sine)
        .astype(low)
        .reshape(query_width, count)
    )
    attended, attended_low, logsum = attend_forward(start, query, pair, before, heads, head)
    w_upward = gather_step(up, up_order[-1])[0].reshape(width, hidden_width)
    w_down = gather_step(down, down_order[-1])[0].reshape(width, hidden_width + query_width)
    w_down, w_output = w_down[:, :hidden_width], w_down[:, hidden_width:]

    grad_low = cotangent.reshape(count, width)
    hidden_pre = dot(after(dense_in, attended_low), w_upward, 1, 0) + upward_bias
    normal_cdf = 0.5 * (1.0 + lax.erf(hidden_pre * (1.0 / math.sqrt(2.0))))
    normal_pdf = jnp.exp(-0.5 * hidden_pre * hidden_pre) * (1.0 / math.sqrt(2.0 * math.pi))
    hidden = (hidden_pre * normal_cdf).astype(low)
    slope = normal_cdf + hidden_pre * normal_pdf
    pre_grad = (dot(grad_low, w_down, 1, 0) * slope).astype(low)

    def by_device(values):
        return values.astype(low).reshape(devices, shard_rows, values.shape[1])

    up_order = side + near + deep[::-1]
    down_order = near + side + deep[::-1]
    up = (by_device(dot(dense_in, pre_grad, 0, 0)), stages)
    row_major = Layout(major_to_minor=(0, 1))

    def term(left, right):
        return with_layout_constraint(dot(left, right, 0, 0).astype(low), row_major)

    cut = hidden_width // 2
    down_terms = term(grad_low, hidden)
    third = jnp.concatenate([down_terms[:, :cut], term(grad_low, attended_low)], axis=1)
    third = by_device(third)
    shape = (lax.axis_size("fsdp"), context // 2, 2) + third.shape[1:]
    third_own, third_gots = deep_send(third.reshape(shape), 1)
    down = (by_device(down_terms[:, cut:]), stages)
    attended_grad = dot(w_output, grad_low, 0, 1).astype(low)
    down, down_got = scatter_send(down, down_order[0])
    attended_grad, up_held = together(attended_grad, up[0])
    up, up_got = scatter_send((up_held, up[1]), up_order[0])
    query_grad, pair_back = attend_backward(
        start, query, pair, attended_grad, attended, logsum, cosine, sine, before, heads, head
    )
    query_grad, pair_back, hidden, pre_grad, grad_late, up_got, down_got, *third_gots = together(
        query_grad, pair_back, hidden, pre_grad, grad_low, up_got, down_got, *third_gots
    )
    third = sum_all([third_own] + third_gots).astype(low)
    third = (third.reshape((-1,) + third.shape[2:]), side + near)
    third, third_got = scatter_send(third, side[0])
    pair_back = pair_back.reshape(micro, 2, head, window)

    keep, send = halves(pair_back[:, 0], pair_back[:, 1])
    pair_other = partner(send, ("tp", 1))
    asked_order = near + side + deep[::-1]
    asked = by_device(dot(attend_in, query_grad, 0, 0))
    pair_other, asked, hidden, pre_grad, grad_late, third_got = together(
        pair_other, asked, hidden, pre_grad, grad_late, third_got
    )
    third = scatter_rest(scatter_join(third, third_got), side[1:])
    up, up_got = scatter_send(scatter_join(up, up_got), up_order[1])
    down, down_got = scatter_send(scatter_join(down, down_got), down_order[1])
    asked, asked_got = scatter_send((asked, stages), asked_order[0])
    branches = (dot(attended_low, w_output, 1, 1) + dot(hidden, w_down, 1, 1)).astype(low)
    dense_part = dot(pre_grad, w_upward, 1, 1)
    early_sums = jnp.concatenate(
        [
            jnp.sum(grad_late.astype(jnp.float32), axis=0),
            jnp.sum(pre_grad.astype(jnp.float32), axis=0),
            jnp.sum(query_grad.astype(jnp.float32), axis=0),
        ]
    )
    summed = (keep.astype(jnp.float32) + pair_other.astype(jnp.float32)).astype(low)
    summed = summed.reshape(micro * head, window)

    def backward(values, d):
        return lax.ppermute(values.astype(low), "ctx", [(i + d, i) for i in range(context - d)])

    farthest = backward(summed[:, :length], reach)
    held = summed[:, length:].astype(jnp.float32)
    rest = deep[::-1]
    step = reach // 2
    while step:
        got = backward(held[:, : step * length], step)
        if step == reach // 2:
            got, farthest, asked_got, branches, dense_part, early_sums, up_got, down_got = together(
                got, farthest, asked_got, branches, dense_part, early_sums, up_got, down_got
            )
            asked, asked_got = scatter_send(scatter_join(asked, asked_got), asked_order[1])
            up = scatter_rest(scatter_join(up, up_got), up_order[2 : -len(rest)])
            down = scatter_rest(scatter_join(down, down_got), down_order[2 : -len(rest)])
            bulk, bulk_gots = deep_send(jnp.concatenate([up[0], down[0]], axis=2), 0)
        if step == 1:
            third_held, got, asked_got, bulk_gots[0] = together(
                third[0], got, asked_got, bulk_gots[0]
            )
            third, third_got = scatter_send((third_held, near), near[0])
        held = held[:, step * length :] + got.astype(jnp.float32)
        step //= 2
    pair_sum = held + farthest.astype(jnp.float32)
    asked, asked_got = scatter_send(scatter_join(asked, asked_got), asked_order[2])
    branches_other = partner(branches, ("tp", 1))
    pair_low = rotate(by_token(pair_sum), pair_cosine, -pair_sine).astype(low)

    shared_rows = 4 * width // LANES + 1
    small_rows = shared_rows + early_sums.shape[0] // LANES
    payload_rows = padded_rows(shard_rows) + padded_rows(small_rows)
    norm_part, payload = by_rows(
        functools.partial(part_kernel, shard_rows),
        "parts",
        256,
        [
            (query_grad, 0),
            (pair_low, 1),
            (w_query, None),
            (w_pair, None),
            (dense_part, 0),
            (inputs, 0),
        ],
        [attend_gain, attend_bias, dense_gain, early_sums.reshape(-1, LANES)],
        [(wide, 0), (jax.ShapeDtypeStruct((devices, payload_rows, LANES), low), None)],
        2 * count * width * (query_width + head),
        scratch=[
            pltpu.VMEM((4, width), jnp.float32),
            pltpu.VMEM((head, width), jnp.float32),
            pltpu.VMEM((head, 1), jnp.float32),
        ],
    )
    payload, norm_part, branches_other, asked_got, bulk_gots[1] = together(
        payload, norm_part, branches_other, asked_got, bulk_gots[1]
    )
    got = lax.all_to_all(payload, ("fsdp", "ctx"), 0, 0)
    norm_other = partner(norm_part, ("tp", 1))
    asked = scatter_rest(scatter_join(asked, asked_got), asked_order[3:-1])
    asked, asked_got = scatter_send(asked, asked_order[-1])
    tokens_grad = by_rows(
        back_kernel,
        "back",
        256,
        [(norm_part, 0), (norm_other, 0), (grad_low, 0), (inputs, 0)],
        [],
        [(wide, 0)],
    )[0]
    result = by_rows(
        result_kernel,
        "results",
        256,
        [(branches, 0), (branches_other, 0), (inputs, 0)],
        [output_bias, down_bias],
        [(wide, 0)],
    )[0]
    got, asked_got, third_got, tokens_grad, result, *bulk_gots = together(
        got, asked_got, third_got, tokens_grad, result, *bulk_gots
    )
    grad_query = scatter_join(asked, asked_got)[0][0]
    grad_bulk = sum_all([bulk] + bulk_gots)
    grad_third = scatter_join(third, third_got)[0][0]
    grad_up = grad_bulk[:, :hidden_width]
    grad_down = jnp.concatenate([grad_third[:, :cut], grad_bulk[:, hidden_width:]], axis=1)

    def rows_of(count):
        return jax.ShapeDtypeStruct((count, LANES), jnp.float32)

    sizes = [width // LANES, hidden_width // LANES, query_width // LANES, width // LANES]
    own, out_b, up_b, q_b, down_b = pl.pallas_call(
        functools.partial(sum_kernel, shard_rows, shared_rows),
        out_shape=[rows_of(shard_rows + shared_rows)] + [rows_of(size) for size in sizes],
        name="sums",
    )(got)
    other = partner(own, ("tp", 1))
    outs = pl.pallas_call(
        functools.partial(last_kernel, shard_rows, head),
        out_shape=[jax.ShapeDtypeStruct((shard_rows, head), jnp.float32)] * 2
        + [jax.ShapeDtypeStruct((1, head), jnp.float32)] * 2
        + [rows_of(width // LANES)] * 4,
        in_specs=[pl.BlockSpec(memory_space=pltpu.SMEM)] + [pl.BlockSpec(memory_space=pltpu.VMEM)] * 2,
        name="last",
    )(core.astype(jnp.int32).reshape(1), own, other)
    grad_key, grad_value, k_b, v_b = outs[0], outs[1], outs[2].reshape(-1), outs[3].reshape(-1)
    g_gain, g_shift, d_gain, d_shift = [values.reshape(-1) for values in outs[4:]]
    out_b, up_b, q_b, down_b = [values.reshape(-1) for values in (out_b, up_b, q_b, down_b)]
    shape = (micro, 1, length, width)
    return (
        result.reshape(shape),
        tokens_grad.reshape(shape),
        grad_query,
        q_b,
        grad_key,
        k_b,
        grad_value,
        v_b,
        grad_third[:, cut:].T,
        out_b,
        grad_up,
        up_b,
        grad_down.T,
        down_b,
        g_gain,
        g_shift,
        d_gain,
        d_shift,
    )


def solution(mesh):
    return jax.shard_map(
        shards,
        mesh=mesh,
        in_specs=(
            P(None, "fsdp", "ctx", None),
            P(None, "fsdp", "ctx"),
            P(("fsdp", "ctx"), "tp"),
            P("tp"),
            P(("fsdp", "ctx"), None),
            P(),
            P(("fsdp", "ctx"), None),
            P(),
            P("tp", ("fsdp", "ctx")),
            P(),
            P(("fsdp", "ctx"), "tp"),
            P("tp"),
            P("tp", ("fsdp", "ctx")),
            P(),
            P(),
            P(),
            P(),
            P(),
            P(None, "fsdp", "ctx", None),
        ),
        out_specs=(
            P(None, "fsdp", "ctx", None),
            P(None, "fsdp", "ctx", None),
            P(("fsdp", "ctx"), "tp"),
            P("tp"),
            P(("fsdp", "ctx"), None),
            P(),
            P(("fsdp", "ctx"), None),
            P(),
            P("tp", ("fsdp", "ctx")),
            P(),
            P(("fsdp", "ctx"), "tp"),
            P("tp"),
            P("tp", ("fsdp", "ctx")),
            P(),
            P(),
            P(),
            P(),
            P(),
        ),
        check_vma=False,
    )
```

```python
import functools
import math

import jax
import jax.numpy as jnp
from jax import lax
from jax.experimental.layout import Layout, with_layout_constraint
from jax.experimental import pallas as pl
from jax.experimental.pallas import tpu as pltpu
from jax.sharding import PartitionSpec as P

ROT = 16
NEGATIVE = -1e30
EPSILON = 1e-05
LOG2E = math.log2(math.e)
LANES = 128
forward_blocks = (512, 512)
backward_blocks = (256, 256)


def dot(left, right, left_dim, right_dim):
    return lax.dot_general(
        left,
        right,
        (((left_dim,), (right_dim,)), ((), ())),
        preferred_element_type=jnp.float32,
    )


def axis_bits(name):
    return [1 << b for b in reversed(range(lax.axis_size(name).bit_length() - 1))]


def all_bits():
    return [("fsdp", d) for d in axis_bits("fsdp")] + [("ctx", d) for d in axis_bits("ctx")]


def partner(values, stage):
    name, distance = stage
    pairs = [(i, i ^ distance) for i in range(lax.axis_size(name))]
    return lax.ppermute(values, name, pairs)


def own_bit(stage):
    name, distance = stage
    return (lax.axis_index(name) // distance) % 2 == 1


def gather_join(state, stage, other):
    held, done = state
    rank = {other_stage: i for i, other_stage in enumerate(all_bits())}
    low = 1 << sum(rank[earlier] > rank[stage] for earlier in done)
    piece = held.shape[1:]
    split = held.reshape((held.shape[0] // low, 1, low) + piece)
    other = other.reshape(split.shape)
    upper = own_bit(stage)
    held = jnp.concatenate(
        [jnp.where(upper, other, split), jnp.where(upper, split, other)], axis=1
    ).reshape((2 * held.shape[0],) + piece)
    return held, done + [stage]


def scatter_send(state, stage):
    held, left = state
    rank = {other: i for i, other in enumerate(all_bits())}
    low = 1 << sum(rank[other] > rank[stage] for other in left if other != stage)
    piece = held.shape[1:]
    split = held.reshape((held.shape[0] // (2 * low), 2, low) + piece)
    upper = own_bit(stage).astype(jnp.int32)
    shape = (held.shape[0] // 2,) + piece
    send = lax.dynamic_index_in_dim(split, 1 - upper, 1, keepdims=False).reshape(shape)
    keep = lax.dynamic_index_in_dim(split, upper, 1, keepdims=False).reshape(shape)
    return (keep, [other for other in left if other != stage]), partner(send, stage)


def scatter_join(kept, other):
    keep, left = kept
    total = keep.astype(jnp.float32) + other.astype(jnp.float32)
    return (total.astype(jnp.bfloat16) if left else total), left


def scatter_rest(state, order):
    for stage in order:
        state = scatter_step(state, stage)
    return state


def gather_step(state, stage):
    return gather_join(state, stage, partner(state[0], stage))


def scatter_step(state, stage):
    return scatter_join(*scatter_send(state, stage))


def deep_rank():
    return lax.axis_index("ctx") // 2


def deep_send(terms, axis):
    size = terms.shape[axis]
    own, *others = [
        lax.dynamic_index_in_dim(terms, deep_rank() ^ mask, axis, keepdims=False)
        for mask in range(size)
    ]
    return own, [partner(values, ("ctx", 2 * mask + 2)) for mask, values in enumerate(others)]


def sum_all(values):
    return sum(other.astype(jnp.float32) for other in values)


def together(*values):
    return lax.optimization_barrier(values)


def norm_parts(values):
    centre = values - jnp.mean(values, axis=-1, keepdims=True)
    spread = lax.rsqrt(jnp.mean(centre * centre, axis=-1, keepdims=True) + EPSILON)
    return centre * spread, spread


def as_row(values):
    return values[...].reshape(1, values.shape[0])


def norm_kernel(
    tokens, attend_gain, attend_bias, dense_gain, dense_bias, attend_in, dense_in
):
    normed, _ = norm_parts(tokens[...].astype(jnp.float32))
    attend_in[...] = (normed * as_row(attend_gain) + as_row(attend_bias)).astype(jnp.bfloat16)
    dense_in[...] = (normed * as_row(dense_gain) + as_row(dense_bias)).astype(jnp.bfloat16)


def part_kernel(
    shard_rows, query_grad, pair_low, w_query, w_pair, dense_part, tokens, attend_gain, attend_bias,
    dense_gain, early, norm_part, payload, sums, pair_grad, pair_sum,
):
    step = pl.program_id(0)
    attend_part = dot(query_grad[...], w_query[...], 1, 1) + dot(pair_low[...].T, w_pair[...], 1, 1)
    dense = dense_part[...]
    normed, _ = norm_parts(tokens[...].astype(jnp.float32))
    norm_part[...] = (
        attend_part * as_row(attend_gain) + dense * as_row(dense_gain)
    ).astype(jnp.bfloat16)
    attend_in = (normed * as_row(attend_gain) + as_row(attend_bias)).astype(jnp.bfloat16)

    @pl.when(step == 0)
    def _():
        sums[...] = jnp.zeros(sums.shape, jnp.float32)
        pair_grad[...] = jnp.zeros(pair_grad.shape, jnp.float32)
        pair_sum[...] = jnp.zeros(pair_sum.shape, jnp.float32)

    rows = [attend_part * normed, attend_part, dense * normed, dense]
    sums[...] += jnp.concatenate([jnp.sum(row, axis=0, keepdims=True) for row in rows])
    pair_grad[...] += dot(pair_low[...], attend_in, 1, 0)
    pair_sum[...] += jnp.sum(pair_low[...].astype(jnp.float32), axis=1, keepdims=True)

    @pl.when(step == pl.num_programs(0) - 1)
    def _():
        head, width = pair_grad.shape
        fill = jnp.zeros((width, LANES - head), jnp.float32)
        grads = jnp.concatenate([pair_grad[...].T, fill], axis=1).astype(jnp.bfloat16)
        values = sums[...]
        small = [
            values[i : i + 1, j : j + LANES] for i in range(4) for j in range(0, width, LANES)
        ]
        pair_row = jnp.broadcast_to(pair_sum[...], (head, LANES)).T[:1]
        small.append(jnp.concatenate([pair_row, jnp.zeros((1, LANES - head), jnp.float32)], axis=1))
        small = jnp.concatenate(small + [early[...]])
        spare = payload.shape[1] - small.shape[0] - padded_rows(shard_rows)
        small = jnp.concatenate([small, jnp.zeros((spare, LANES), jnp.float32)]).astype(jnp.bfloat16)
        for device in range(payload.shape[0]):
            piece = grads[device * shard_rows : (device + 1) * shard_rows]
            payload[device, :shard_rows] = piece
            payload[device, padded_rows(shard_rows) :] = small


def padded_rows(rows):
    return rows + -rows % 16


def ends_kernel(
    own, other, cotangent, tokens, branch, other_branch, first_bias, second_bias, tokens_grad, result
):
    grad = own[...].astype(jnp.float32) + other[...].astype(jnp.float32)
    values = tokens[...].astype(jnp.float32)
    normed, spread = norm_parts(values)
    inner = (
        grad
        - jnp.mean(grad, axis=-1, keepdims=True)
        - normed * jnp.mean(grad * normed, axis=-1, keepdims=True)
    )
    tokens_grad[...] = (cotangent[...].astype(jnp.float32) + spread * inner).astype(jnp.bfloat16)
    mixed = branch[...].astype(jnp.float32) + other_branch[...].astype(jnp.float32)
    result[...] = (values + mixed + as_row(first_bias) + as_row(second_bias)).astype(jnp.bfloat16)


def sum_kernel(
    shard_rows, shared_rows, got, own, out_sum, up_sum, query_sum, out_again
):
    total = got[0].astype(jnp.float32)
    for device in range(1, got.shape[0]):
        total += got[device].astype(jnp.float32)
    small = total[padded_rows(shard_rows) :]
    own[...] = jnp.concatenate([total[:shard_rows], small[:shared_rows]])
    at = shared_rows
    for out in (out_sum, up_sum, query_sum):
        out[...] = small[at : at + out.shape[0]]
        at += out.shape[0]
    out_again[...] = out_sum[...]


def grads_kernel(cut, hidden_width, *refs):
    terms, (query_grad, out_grad, up_grad, down_grad) = refs[:-4], refs[-4:]
    values = [term[...].astype(jnp.float32) for term in terms]
    bulk = sum(values[1:-4], values[0])
    third = values[-4] + values[-3]
    query_grad[...] = values[-2] + values[-1]
    up_grad[...] = bulk[:, :hidden_width]
    out_grad[...] = third[:, cut:]
    down_grad[:, :cut] = third[:, :cut]
    down_grad[:, cut:] = bulk[:, hidden_width:]


def last_kernel(shard_rows, head, core, own, other, key_grad, value_grad, key_sum, value_sum, *sums):
    first = core[0] == 0
    mine, theirs = own[...], other[...]
    keys = jnp.where(first, mine, theirs)
    values = jnp.where(first, theirs, mine)
    key_grad[...] = keys[:shard_rows, :head]
    value_grad[...] = values[:shard_rows, :head]
    key_sum[...] = keys[keys.shape[0] - 1 :, :head]
    value_sum[...] = values[keys.shape[0] - 1 :, :head]
    both = mine + theirs
    rows = sums[0].shape[0]
    for i, out in enumerate(sums):
        out[...] = both[shard_rows + i * rows : shard_rows + (i + 1) * rows]


def by_rows(kernel, name, rows, moving, fixed, outs, flops=0, grant=20, scratch=()):
    steps = moving[0][0].shape[moving[0][1]] // rows

    def spec(values, cut):
        if cut is None:
            whole = (0,) * len(values.shape)
            return pl.BlockSpec(values.shape, lambda i: whole)
        if cut == 0:
            return pl.BlockSpec((rows, values.shape[1]), lambda i: (i, 0))
        return pl.BlockSpec((values.shape[0], rows), lambda i: (0, i))

    arrays = [values for values, _ in moving] + fixed
    moved = sum(values.size * values.dtype.itemsize for values in arrays + [o for o, _ in outs])
    return pl.pallas_call(
        kernel,
        grid=(steps,),
        in_specs=[spec(*entry) for entry in moving] + [spec(values, None) for values in fixed],
        out_specs=[spec(*entry) for entry in outs],
        out_shape=[entry[0] for entry in outs],
        scratch_shapes=list(scratch),
        compiler_params=pltpu.CompilerParams(vmem_limit_bytes=grant << 20),
        cost_estimate=pl.CostEstimate(flops=flops, bytes_accessed=moved, transcendentals=0),
        name=name,
    )(*arrays)


def rotate(values, cosine, sine):
    half = ROT // 2
    first = values[..., :half, :]
    second = values[..., half:ROT, :]
    return jnp.concatenate(
        [first * cosine - second * sine, second * cosine + first * sine, values[..., ROT:, :]],
        axis=-2,
    )


def allowed_pairs(block, key_block, start, last):
    key_index = block * key_block + lax.broadcasted_iota(
        jnp.int32, (key_block, start.shape[1]), 0
    )
    return (key_index >= start) & (key_index <= last)


def over_blocks(starts, at, begin, block_rows, key_block, body):
    shift = key_block.bit_length() - 1
    lo = starts[at * block_rows] >> shift
    hi = (begin + (block_rows - 1) >> shift) + 1
    a = starts[at * block_rows + block_rows - 1] + (key_block - 1) >> shift
    b = begin + 1 >> shift

    def step(block, carry):
        inside = (block >= a) & (block < b)

        @pl.when(inside)
        def _():
            body(block, False)

        @pl.when(jnp.logical_not(inside))
        def _():
            body(block, True)

        return carry

    lax.fori_loop(lo, hi, step, 0)


def spread_heads(pairs, heads, head, block):
    for h in range(heads):
        for wide, tall in pairs:
            wide[:, pl.ds(h * block, block)] = tall[pl.ds(h * head, head), :]


def forward_kernel(
    before, heads, head, key_block, starts, query, pair, start, out, out_low, logsum,
    wide, best, total, accum, first, last,
):
    block_rows = query.shape[1]
    at = pl.program_id(0) * pl.num_programs(1) + pl.program_id(1)
    begin = before + pl.program_id(1) * block_rows
    factor = head**-0.5 * LOG2E
    best[...] = jnp.full(best.shape, NEGATIVE, jnp.float32)
    total[...] = jnp.zeros(total.shape, jnp.float32)
    accum[...] = jnp.zeros(accum.shape, jnp.float32)
    spread_heads([(wide, query)], heads, head, block_rows)
    index = begin + lax.broadcasted_iota(jnp.int32, (1, block_rows), 1)
    for h in range(heads):
        first[:, pl.ds(h * block_rows, block_rows)] = start[...]
        last[:, pl.ds(h * block_rows, block_rows)] = index

    def body(block, masked):
        keys = pl.ds(pl.multiple_of(block * key_block, key_block), key_block)
        key = pair[0, :head, keys].T
        value = pair[0, head:, keys]
        value = jnp.concatenate([value, jnp.ones((8, key_block), jnp.bfloat16)], axis=0)
        scores = dot(key, wide[...], 1, 0) * factor
        if masked:
            allowed = allowed_pairs(block, key_block, first[...], last[...])
            scores = jnp.where(allowed, scores, NEGATIVE)
        old = best[...]
        fresh = jnp.maximum(old, jnp.max(scores, axis=0, keepdims=True))
        weights = jnp.exp2(scores - fresh).astype(jnp.bfloat16)
        shrink = jnp.exp2(old - fresh)
        best[...] = fresh
        product = dot(value, weights, 1, 0)
        accum[...] = accum[...] * shrink + product[:head]
        total[...] = total[...] * shrink + product[head : head + 1]

    over_blocks(starts, at, begin, block_rows, key_block, body)
    scaled = accum[...] / total[...]
    sums = best[...] + jnp.log(total[...]) * LOG2E
    for h in range(heads):
        columns = slice(h * block_rows, (h + 1) * block_rows)
        rows = pl.ds(h * head, head)
        out[rows, :] = scaled[:, columns]
        logsum[pl.ds(h, 1), :] = sums[:, columns]
    out_low[...] = out[...].astype(jnp.bfloat16).T


def backward_kernel(
    before, heads, head, key_block, starts, query, pair, start, grad, out, logsum, cosine, sine,
    query_grad, pair_grad,
    wide, wide_grad, query_sum, pair_sum, sums, delta, first, last,
):
    block_rows = query.shape[1]
    at = pl.program_id(0) * pl.num_programs(1) + pl.program_id(1)
    begin = before + pl.program_id(1) * block_rows
    scale = head**-0.5

    @pl.when(pl.program_id(1) == 0)
    def _():
        pair_sum[...] = jnp.zeros(pair_sum.shape, jnp.float32)

    query_sum[...] = jnp.zeros(query_sum.shape, jnp.float32)
    spread_heads([(wide, query), (wide_grad, grad)], heads, head, block_rows)
    index = begin + lax.broadcasted_iota(jnp.int32, (1, block_rows), 1)
    for h in range(heads):
        rows = pl.ds(h * head, head)
        columns = pl.ds(h * block_rows, block_rows)
        first[:, columns] = start[...]
        last[:, columns] = index
        sums[:, columns] = logsum[pl.ds(h, 1), :]
        delta[:, columns] = jnp.sum(
            grad[rows, :].astype(jnp.float32) * out[rows, :], axis=0, keepdims=True
        )

    def body(block, masked):
        keys = pl.ds(pl.multiple_of(block * key_block, key_block), key_block)
        key_wide = pair[0, :head, keys]
        key = key_wide.T
        value = pair[0, head:, keys].T
        scores = dot(key, wide[...], 1, 0) * (scale * LOG2E)
        probs = jnp.exp2(scores - sums[...])
        if masked:
            allowed = allowed_pairs(block, key_block, first[...], last[...])
            probs = jnp.where(allowed, probs, 0.0)
        pair_sum[head:, keys] += dot(wide_grad[...], probs.astype(jnp.bfloat16), 1, 1)
        prob_grad = dot(value, wide_grad[...], 1, 0)
        score_grad = (probs * (prob_grad - delta[...])).astype(jnp.bfloat16)
        pair_sum[:head, keys] += dot(wide[...], score_grad, 1, 1)
        query_sum[...] += dot(key_wide, score_grad, 1, 0)

    over_blocks(starts, at, begin, block_rows, key_block, body)
    half = ROT // 2
    turned_heads = []
    for h in range(heads):
        value = query_sum[:, pl.ds(h * block_rows, block_rows)] * scale
        near, far = value[:half], value[half:ROT]
        turned = jnp.concatenate(
            [
                near * cosine[...] + far * sine[...],
                far * cosine[...] - near * sine[...],
                value[ROT:],
            ],
            axis=0,
        )
        turned_heads.append(turned.astype(jnp.bfloat16))
    query_grad[...] = jnp.concatenate(turned_heads, axis=0).T

    @pl.when(pl.program_id(1) == pl.num_programs(1) - 1)
    def _():
        pair_grad[0, :head, :] = (pair_sum[:head, :] * scale).astype(jnp.bfloat16)
        pair_grad[0, head:, :] = pair_sum[head:, :].astype(jnp.bfloat16)


def attention_cost(micro, rows, length, products):
    pairs = micro * (rows // 64) * length * 2 * length
    return pl.CostEstimate(
        flops=2 * products * 64 * pairs, bytes_accessed=8 * micro * rows * length, transcendentals=pairs
    )


def attend_forward(start, query, pair, before, heads, head):
    micro, _, window = pair.shape
    rows, count = query.shape
    length = count // micro
    query_block, key_block = forward_blocks
    blocks = length // query_block
    spread = heads * query_block
    column = lambda m, i, starts: (0, m * blocks + i)
    tall = pl.BlockSpec((rows, query_block), column)
    return pl.pallas_call(
        functools.partial(forward_kernel, before, heads, head, key_block),
        grid_spec=pltpu.PrefetchScalarGridSpec(
            num_scalar_prefetch=1,
            grid=(micro, blocks),
            in_specs=[
                tall,
                pl.BlockSpec((1, 2 * head, window), lambda m, i, starts: (m, 0, 0)),
                pl.BlockSpec((1, query_block), column),
            ],
            out_specs=[
                tall,
                pl.BlockSpec((query_block, rows), lambda m, i, starts: (m * blocks + i, 0)),
                pl.BlockSpec((heads, query_block), column),
            ],
            scratch_shapes=[
                pltpu.VMEM((head, spread), jnp.bfloat16),
                pltpu.VMEM((1, spread), jnp.float32),
                pltpu.VMEM((1, spread), jnp.float32),
                pltpu.VMEM((head, spread), jnp.float32),
                pltpu.VMEM((1, spread), jnp.int32),
                pltpu.VMEM((1, spread), jnp.int32),
            ],
        ),
        out_shape=[
            jax.ShapeDtypeStruct((rows, count), jnp.float32),
            jax.ShapeDtypeStruct((count, rows), jnp.bfloat16),
            jax.ShapeDtypeStruct((heads, count), jnp.float32),
        ],
        compiler_params=pltpu.CompilerParams(vmem_limit_bytes=32 << 20),
        cost_estimate=attention_cost(micro, rows, length, 2),
        name="attend_forward",
    )(start, query, pair, start.reshape(1, count))


def attend_backward(start, query, pair, grad, out, logsum, cosine, sine, before, heads, head):
    micro, _, window = pair.shape
    rows, count = query.shape
    length = count // micro
    query_block, key_block = backward_blocks
    blocks = length // query_block
    spread = heads * query_block
    column = lambda m, i, starts: (0, m * blocks + i)
    tall = pl.BlockSpec((rows, query_block), column)
    table = pl.BlockSpec((ROT // 2, query_block), column)
    keys = pl.BlockSpec((1, 2 * head, window), lambda m, i, starts: (m, 0, 0))
    return pl.pallas_call(
        functools.partial(backward_kernel, before, heads, head, key_block),
        grid_spec=pltpu.PrefetchScalarGridSpec(
            num_scalar_prefetch=1,
            grid=(micro, blocks),
            in_specs=[
                tall,
                keys,
                pl.BlockSpec((1, query_block), column),
                tall,
                tall,
                pl.BlockSpec((heads, query_block), column),
                table,
                table,
            ],
            out_specs=[
                pl.BlockSpec((query_block, rows), lambda m, i, starts: (m * blocks + i, 0)),
                keys,
            ],
            scratch_shapes=[
                pltpu.VMEM((head, spread), jnp.bfloat16),
                pltpu.VMEM((head, spread), jnp.bfloat16),
                pltpu.VMEM((head, spread), jnp.float32),
                pltpu.VMEM((2 * head, window), jnp.float32),
                pltpu.VMEM((1, spread), jnp.float32),
                pltpu.VMEM((1, spread), jnp.float32),
                pltpu.VMEM((1, spread), jnp.int32),
                pltpu.VMEM((1, spread), jnp.int32),
            ],
        ),
        out_shape=[
            jax.ShapeDtypeStruct((count, rows), jnp.bfloat16),
            jax.ShapeDtypeStruct((micro, 2 * head, window), jnp.bfloat16),
        ],
        compiler_params=pltpu.CompilerParams(vmem_limit_bytes=24 << 20),
        cost_estimate=attention_cost(micro, rows, length, 5),
        name="attend_backward",
    )(start, query, pair, start.reshape(1, count), grad, out, logsum, cosine, sine)


def shards(
    tokens,
    segments,
    query_weight,
    query_bias,
    key_weight,
    key_bias,
    value_weight,
    value_bias,
    output_weight,
    output_bias,
    upward_weight,
    upward_bias,
    down_weight,
    down_bias,
    attend_gain,
    attend_bias,
    dense_gain,
    dense_bias,
    cotangent,
):
    low = jnp.bfloat16
    micro, _, length, width = tokens.shape
    count = micro * length
    head = key_weight.shape[1]
    query_width = query_bias.shape[0]
    heads = query_width // head
    hidden_width = upward_bias.shape[0]
    devices = lax.axis_size("fsdp") * lax.axis_size("ctx")
    reach = lax.axis_size("ctx") // 2
    before = reach * length
    window = before + length
    core = lax.axis_index("tp")
    stages = all_bits()
    deep = [s for s in stages if s[0] == "ctx" and s[1] > 1]
    near = [s for s in stages if s[0] == "ctx" and s[1] == 1]
    side = [s for s in stages if s[0] == "fsdp"]

    first_half = core == 0

    def halves(own, other):
        return jnp.where(first_half, own, other), jnp.where(first_half, other, own)

    shard_rows = key_weight.shape[0]
    segment_piece = (segments + 1).astype(low).reshape(-1, head)
    piece_rows = max(shard_rows, segment_piece.shape[0])

    def padded(values):
        return jnp.pad(values, ((0, piece_rows - values.shape[0]), (0, 0)))

    early_piece = jnp.concatenate(
        [
            padded(jnp.where(first_half, key_weight, value_weight)),
            padded(segment_piece),
            padded(query_weight),
        ],
        axis=1,
    )
    early = (early_piece[None], [])
    up = (upward_weight[None], [])
    down = (jnp.concatenate([down_weight.T, output_weight.T], axis=1)[None], [])
    up_order = deep + near + side
    down_order = deep + side + near
    early_order = deep + side + near
    inputs = tokens.reshape(count, width)
    for stage in early_order:
        got = partner(early[0], stage)
        if stage == early_order[-2]:
            got, norm_inputs = together(got, inputs)
        early = gather_join(early, stage, got)
    up = gather_step(up, up_order[0])
    down = gather_step(down, down_order[0])
    early_all = early[0]
    w_pair = early_all[:, :shard_rows, :head].reshape(width, head)
    w_query = early_all[:, :shard_rows, 2 * head :].reshape(width, query_width)
    segment_all = early_all[:, : segment_piece.shape[0], head : 2 * head].reshape(
        lax.axis_size("fsdp"), lax.axis_size("ctx"), micro, length
    )

    mine = lax.dynamic_index_in_dim(segment_all, lax.axis_index("fsdp"), 0, keepdims=False)
    reached = jnp.concatenate([jnp.zeros((reach,) + mine.shape[1:], low), mine])
    seen = lax.dynamic_slice_in_dim(reached, lax.axis_index("ctx"), reach + 1)
    seen = jnp.transpose(seen, (1, 0, 2)).reshape(micro, window).astype(jnp.int32)
    local = segments[:, 0] + 1
    start = jnp.sum((seen[:, None, :] < local[:, :, None]).astype(jnp.int32), axis=2).reshape(count)
    index = before + jnp.arange(length, dtype=jnp.int32)
    positions = jnp.tile(index, micro) - start
    freqs = jnp.exp(
        jnp.arange(ROT // 2, dtype=jnp.float32) * (-2.0 * math.log(10000.0) / ROT)
    )
    angle = freqs[:, None] * positions.reshape(1, count).astype(jnp.float32)
    cosine, sine = jnp.cos(angle), jnp.sin(angle)
    pair_cosine = jnp.where(first_half, cosine, 1.0)
    pair_sine = jnp.where(first_half, sine, 0.0)

    wide = jax.ShapeDtypeStruct((count, width), low)
    attend_in, dense_in = by_rows(
        norm_kernel,
        "norms",
        256,
        [(norm_inputs, 0)],
        [attend_gain, attend_bias, dense_gain, dense_bias],
        [(wide, 0), (wide, 0)],
        grant=56,
    )

    def by_micro(values):
        return jnp.transpose(values.reshape(head, micro, length), (1, 0, 2)).reshape(-1, length)

    def by_token(values):
        return jnp.transpose(values.reshape(micro, head, length), (1, 0, 2)).reshape(head, count)

    pair_lin = dot(w_pair, attend_in, 0, 1) + jnp.where(first_half, key_bias, value_bias)[:, None]
    pair_mine = by_micro(rotate(pair_lin, pair_cosine, pair_sine).astype(low))
    context = lax.axis_size("ctx")
    for i in range(1, len(stages) - 2):
        up = gather_step(up, up_order[i])
        down = gather_step(down, down_order[i])

    def forward(values, d):
        return lax.ppermute(values, "ctx", [(i, i + d) for i in range(context - d)])

    farthest = forward(pair_mine, reach)
    held = pair_mine
    while held.shape[1] < before:
        held = jnp.concatenate([forward(held, held.shape[1] // length), held], axis=1)
    pair_half = jnp.concatenate([farthest, held], axis=1)
    up = gather_step(up, up_order[-2])
    down = gather_step(down, down_order[-2])
    pair_other = partner(pair_half, ("tp", 1))
    pair = jnp.concatenate(
        [side_half.reshape(micro, head, window) for side_half in halves(pair_half, pair_other)],
        axis=1,
    )

    query_lin = dot(w_query, attend_in, 0, 1) + query_bias[:, None]
    query = (
        rotate(query_lin.reshape(heads, head, count), cosine, sine)
        .astype(low)
        .reshape(query_width, count)
    )
    attended, attended_low, logsum = attend_forward(start, query, pair, before, heads, head)
    w_upward = gather_step(up, up_order[-1])[0].reshape(width, hidden_width)
    w_down = gather_step(down, down_order[-1])[0].reshape(width, hidden_width + query_width)
    w_down, w_output = w_down[:, :hidden_width], w_down[:, hidden_width:]

    grad_low = cotangent.reshape(count, width)
    hidden_pre = dot(dense_in, w_upward, 1, 0) + upward_bias
    normal_cdf = 0.5 * (1.0 + lax.erf(hidden_pre * (1.0 / math.sqrt(2.0))))
    normal_pdf = jnp.exp(-0.5 * hidden_pre * hidden_pre) * (1.0 / math.sqrt(2.0 * math.pi))
    hidden = (hidden_pre * normal_cdf).astype(low)
    slope = normal_cdf + hidden_pre * normal_pdf
    hidden, slope = together(hidden, slope.astype(low))
    pre_grad = (dot(grad_low, w_down, 1, 0) * slope.astype(jnp.float32)).astype(low)

    def by_device(values):
        return values.astype(low).reshape(devices, shard_rows, values.shape[1])

    up_order = side + near + deep[::-1]
    down_order = near + side + deep[::-1]
    up = (by_device(dot(dense_in, pre_grad, 0, 0)), stages)
    row_major = Layout(major_to_minor=(0, 1))

    def term(left, right):
        return with_layout_constraint(dot(left, right, 0, 0).astype(low), row_major)

    cut = hidden_width // 2
    down_terms = term(grad_low, hidden)
    third = jnp.concatenate([down_terms[:, :cut], term(grad_low, attended_low)], axis=1)
    third = by_device(third)
    shape = (lax.axis_size("fsdp"), context // 2, 2) + third.shape[1:]
    third_own, third_gots = deep_send(third.reshape(shape), 1)
    down = (by_device(down_terms[:, cut:]), stages)
    attended_grad = dot(w_output, grad_low, 0, 1).astype(low)
    down, down_got = scatter_send(down, down_order[0])
    attended_grad, up_held = together(attended_grad, up[0])
    up, up_got = scatter_send((up_held, up[1]), up_order[0])
    query_grad, pair_back = attend_backward(
        start, query, pair, attended_grad, attended, logsum, cosine, sine, before, heads, head
    )
    query_grad, pair_back, hidden, pre_grad, grad_late, up_got, down_got, *third_gots = together(
        query_grad, pair_back, hidden, pre_grad, grad_low, up_got, down_got, *third_gots
    )
    third = sum_all([third_own] + third_gots).astype(low)
    third = third.reshape((-1,) + third.shape[2:])
    pair_back = pair_back.reshape(micro, 2, head, window)

    keep, send = halves(pair_back[:, 0], pair_back[:, 1])
    pair_other = partner(send, ("tp", 1))
    asked_order = side + near + deep[::-1]
    asked = by_device(dot(attend_in, query_grad, 0, 0))
    pair_other, asked, hidden, pre_grad, grad_late = together(
        pair_other, asked, hidden, pre_grad, grad_late
    )
    up, up_got = scatter_send(scatter_join(up, up_got), up_order[1])
    down, down_got = scatter_send(scatter_join(down, down_got), down_order[1])
    asked, asked_got = scatter_send((asked, stages), asked_order[0])
    branches = (dot(attended_low, w_output, 1, 1) + dot(hidden, w_down, 1, 1)).astype(low)
    dense_part = dot(pre_grad, w_upward, 1, 1)
    early_sums = jnp.concatenate(
        [
            jnp.sum(grad_late.astype(jnp.float32), axis=0),
            jnp.sum(pre_grad.astype(jnp.float32), axis=0),
            jnp.sum(query_grad.astype(jnp.float32), axis=0),
        ]
    )
    summed = (keep.astype(jnp.float32) + pair_other.astype(jnp.float32)).astype(low)
    summed = summed.reshape(micro * head, window)

    def backward(values, d):
        return lax.ppermute(values.astype(low), "ctx", [(i + d, i) for i in range(context - d)])

    farthest = backward(summed[:, :length], reach)
    held = summed[:, length:].astype(jnp.float32)
    rest = deep[::-1]
    step = reach // 2
    while step:
        got = backward(held[:, : step * length], step)
        if step == reach // 2:
            got, farthest, asked_got, branches, dense_part, early_sums, up_got, down_got = together(
                got, farthest, asked_got, branches, dense_part, early_sums, up_got, down_got
            )
            asked, asked_got = scatter_send(scatter_join(asked, asked_got), asked_order[1])
            branches_other = partner(branches, ("tp", 1))
            up = scatter_rest(scatter_join(up, up_got), up_order[2 : -len(rest)])
            down = scatter_rest(scatter_join(down, down_got), down_order[2 : -len(rest)])
            bulk, bulk_gots = deep_send(jnp.concatenate([up[0], down[0]], axis=2), 0)
        if step == 1:
            third, got, asked_got, branches_other = together(third, got, asked_got, branches_other)
            third, third_got = scatter_send((third, side + near), side[0])
        held = held[:, step * length :] + got.astype(jnp.float32)
        step //= 2
    pair_sum = held + farthest.astype(jnp.float32)
    asked, asked_got = scatter_send(scatter_join(asked, asked_got), asked_order[2])
    pair_low = rotate(by_token(pair_sum), pair_cosine, -pair_sine).astype(low)

    shared_rows = 4 * width // LANES + 1
    small_rows = shared_rows + early_sums.shape[0] // LANES
    payload_rows = padded_rows(shard_rows) + padded_rows(small_rows)
    norm_part, payload = by_rows(
        functools.partial(part_kernel, shard_rows),
        "parts",
        256,
        [
            (query_grad, 0),
            (pair_low, 1),
            (w_query, None),
            (w_pair, None),
            (dense_part, 0),
            (inputs, 0),
        ],
        [attend_gain, attend_bias, dense_gain, early_sums.reshape(-1, LANES)],
        [(wide, 0), (jax.ShapeDtypeStruct((devices, payload_rows, LANES), low), None)],
        2 * count * width * (query_width + head),
        scratch=[
            pltpu.VMEM((4, width), jnp.float32),
            pltpu.VMEM((head, width), jnp.float32),
            pltpu.VMEM((head, 1), jnp.float32),
        ],
    )
    payload, norm_part, asked_got, third_got, branches_other, *bulk_gots[:-1] = together(
        payload, norm_part, asked_got, third_got, branches_other, *bulk_gots[:-1]
    )
    third = scatter_rest(scatter_join(third, third_got), side[1:])
    third, third_got = scatter_send(third, near[0])
    got = lax.all_to_all(payload, ("fsdp", "ctx"), 0, 0)
    norm_other = partner(norm_part, ("tp", 1))
    asked = scatter_rest(scatter_join(asked, asked_got), asked_order[3:-1])
    asked, asked_got = scatter_send(asked, asked_order[-1])
    tokens_grad, result = by_rows(
        ends_kernel,
        "ends",
        128,
        [
            (norm_part, 0),
            (norm_other, 0),
            (grad_low, 0),
            (inputs, 0),
            (branches, 0),
            (branches_other, 0),
        ],
        [output_bias, down_bias],
        [(wide, 0), (wide, 0)],
        grant=56,
    )
    got, asked_got, third_got, tokens_grad, result, *bulk_gots = together(
        got, asked_got, third_got, tokens_grad, result, *bulk_gots
    )
    def rows_of(count):
        return jax.ShapeDtypeStruct((count, LANES), jnp.float32)

    sizes = [width // LANES, hidden_width // LANES, query_width // LANES, width // LANES]
    own, out_b, up_b, q_b, down_b = pl.pallas_call(
        functools.partial(sum_kernel, shard_rows, shared_rows),
        out_shape=[rows_of(shard_rows + shared_rows)] + [rows_of(size) for size in sizes],
        name="sums",
    )(got)
    other = partner(own, ("tp", 1))
    terms = [bulk] + bulk_gots + [third[0][0], third_got[0], asked[0][0], asked_got[0]]
    grad_query, grad_out, grad_up, grad_down = pl.pallas_call(
        functools.partial(grads_kernel, cut, hidden_width),
        out_shape=[
            jax.ShapeDtypeStruct((shard_rows, columns), jnp.float32)
            for columns in (query_width, query_width, hidden_width, hidden_width)
        ],
        name="grads",
    )(*terms)
    outs = pl.pallas_call(
        functools.partial(last_kernel, shard_rows, head),
        out_shape=[jax.ShapeDtypeStruct((shard_rows, head), jnp.float32)] * 2
        + [jax.ShapeDtypeStruct((1, head), jnp.float32)] * 2
        + [rows_of(width // LANES)] * 4,
        in_specs=[pl.BlockSpec(memory_space=pltpu.SMEM)] + [pl.BlockSpec(memory_space=pltpu.VMEM)] * 2,
        name="last",
    )(core.astype(jnp.int32).reshape(1), own, other)
    grad_key, grad_value, k_b, v_b = outs[0], outs[1], outs[2].reshape(-1), outs[3].reshape(-1)
    g_gain, g_shift, d_gain, d_shift = [values.reshape(-1) for values in outs[4:]]
    out_b, up_b, q_b, down_b = [values.reshape(-1) for values in (out_b, up_b, q_b, down_b)]
    shape = (micro, 1, length, width)
    return (
        result.reshape(shape),
        tokens_grad.reshape(shape),
        grad_query,
        q_b,
        grad_key,
        k_b,
        grad_value,
        v_b,
        grad_out.T,
        out_b,
        grad_up,
        up_b,
        grad_down.T,
        down_b,
        g_gain,
        g_shift,
        d_gain,
        d_shift,
    )


def solution(mesh):
    return jax.shard_map(
        shards,
        mesh=mesh,
        in_specs=(
            P(None, "fsdp", "ctx", None),
            P(None, "fsdp", "ctx"),
            P(("fsdp", "ctx"), "tp"),
            P("tp"),
            P(("fsdp", "ctx"), None),
            P(),
            P(("fsdp", "ctx"), None),
            P(),
            P("tp", ("fsdp", "ctx")),
            P(),
            P(("fsdp", "ctx"), "tp"),
            P("tp"),
            P("tp", ("fsdp", "ctx")),
            P(),
            P(),
            P(),
            P(),
            P(),
            P(None, "fsdp", "ctx", None),
        ),
        out_specs=(
            P(None, "fsdp", "ctx", None),
            P(None, "fsdp", "ctx", None),
            P(("fsdp", "ctx"), "tp"),
            P("tp"),
            P(("fsdp", "ctx"), None),
            P(),
            P(("fsdp", "ctx"), None),
            P(),
            P("tp", ("fsdp", "ctx")),
            P(),
            P(("fsdp", "ctx"), "tp"),
            P("tp"),
            P("tp", ("fsdp", "ctx")),
            P(),
            P(),
            P(),
            P(),
            P(),
        ),
        check_vma=False,
    )
```

```python
import functools
import math

import jax
import jax.numpy as jnp
from jax import lax
from jax.experimental.layout import Layout, with_layout_constraint
from jax.experimental import pallas as pl
from jax.experimental.pallas import tpu as pltpu
from jax.sharding import PartitionSpec as P

ROT = 16
NEGATIVE = -1e30
EPSILON = 1e-05
LOG2E = math.log2(math.e)
LANES = 128
forward_blocks = (512, 512)
backward_blocks = (256, 256)


def dot(left, right, left_dim, right_dim):
    return lax.dot_general(
        left,
        right,
        (((left_dim,), (right_dim,)), ((), ())),
        preferred_element_type=jnp.float32,
    )


def axis_bits(name):
    return [1 << b for b in reversed(range(lax.axis_size(name).bit_length() - 1))]


def all_bits():
    return [("fsdp", d) for d in axis_bits("fsdp")] + [("ctx", d) for d in axis_bits("ctx")]


def partner(values, stage):
    name, distance = stage
    pairs = [(i, i ^ distance) for i in range(lax.axis_size(name))]
    return lax.ppermute(values, name, pairs)


def own_bit(stage):
    name, distance = stage
    return (lax.axis_index(name) // distance) % 2 == 1


def gather_join(state, stage, other):
    held, done = state
    rank = {other_stage: i for i, other_stage in enumerate(all_bits())}
    low = 1 << sum(rank[earlier] > rank[stage] for earlier in done)
    piece = held.shape[1:]
    split = held.reshape((held.shape[0] // low, 1, low) + piece)
    other = other.reshape(split.shape)
    upper = own_bit(stage)
    held = jnp.concatenate(
        [jnp.where(upper, other, split), jnp.where(upper, split, other)], axis=1
    ).reshape((2 * held.shape[0],) + piece)
    return held, done + [stage]


def scatter_send(state, stage):
    held, left = state
    rank = {other: i for i, other in enumerate(all_bits())}
    low = 1 << sum(rank[other] > rank[stage] for other in left if other != stage)
    piece = held.shape[1:]
    split = held.reshape((held.shape[0] // (2 * low), 2, low) + piece)
    upper = own_bit(stage).astype(jnp.int32)
    shape = (held.shape[0] // 2,) + piece
    send = lax.dynamic_index_in_dim(split, 1 - upper, 1, keepdims=False).reshape(shape)
    keep = lax.dynamic_index_in_dim(split, upper, 1, keepdims=False).reshape(shape)
    return (keep, [other for other in left if other != stage]), partner(send, stage)


def scatter_join(kept, other):
    keep, left = kept
    total = keep.astype(jnp.float32) + other.astype(jnp.float32)
    return (total.astype(jnp.bfloat16) if left else total), left


def scatter_rest(state, order):
    for stage in order:
        state = scatter_step(state, stage)
    return state


def gather_step(state, stage):
    return gather_join(state, stage, partner(state[0], stage))


def scatter_step(state, stage):
    return scatter_join(*scatter_send(state, stage))


def deep_rank():
    return lax.axis_index("ctx") // 2


def deep_send(terms, axis):
    size = terms.shape[axis]
    own, *others = [
        lax.dynamic_index_in_dim(terms, deep_rank() ^ mask, axis, keepdims=False)
        for mask in range(size)
    ]
    return own, [partner(values, ("ctx", 2 * mask + 2)) for mask, values in enumerate(others)]


def sum_all(values):
    return sum(other.astype(jnp.float32) for other in values)


def together(*values):
    return lax.optimization_barrier(values)


def norm_parts(values):
    centre = values - jnp.mean(values, axis=-1, keepdims=True)
    spread = lax.rsqrt(jnp.mean(centre * centre, axis=-1, keepdims=True) + EPSILON)
    return centre * spread, spread


def as_row(values):
    return values[...].reshape(1, values.shape[0])


def norm_kernel(
    tokens, attend_gain, attend_bias, dense_gain, dense_bias, attend_in, dense_in
):
    normed, _ = norm_parts(tokens[...].astype(jnp.float32))
    attend_in[...] = (normed * as_row(attend_gain) + as_row(attend_bias)).astype(jnp.bfloat16)
    dense_in[...] = (normed * as_row(dense_gain) + as_row(dense_bias)).astype(jnp.bfloat16)


def part_kernel(
    shard_rows, query_grad, pair_low, w_query, w_pair, dense_part, tokens, attend_gain, attend_bias,
    dense_gain, early, norm_part, payload, sums, pair_grad, pair_sum,
):
    step = pl.program_id(0)
    attend_part = dot(query_grad[...], w_query[...], 1, 1) + dot(pair_low[...].T, w_pair[...], 1, 1)
    dense = dense_part[...].astype(jnp.float32)
    normed, _ = norm_parts(tokens[...].astype(jnp.float32))
    norm_part[...] = (
        attend_part * as_row(attend_gain) + dense * as_row(dense_gain)
    ).astype(jnp.bfloat16)
    attend_in = (normed * as_row(attend_gain) + as_row(attend_bias)).astype(jnp.bfloat16)

    @pl.when(step == 0)
    def _():
        sums[...] = jnp.zeros(sums.shape, jnp.float32)
        pair_grad[...] = jnp.zeros(pair_grad.shape, jnp.float32)
        pair_sum[...] = jnp.zeros(pair_sum.shape, jnp.float32)

    rows = [attend_part * normed, attend_part, dense * normed, dense]
    sums[...] += jnp.concatenate([jnp.sum(row, axis=0, keepdims=True) for row in rows])
    pair_grad[...] += dot(pair_low[...], attend_in, 1, 0)
    pair_sum[...] += jnp.sum(pair_low[...].astype(jnp.float32), axis=1, keepdims=True)

    @pl.when(step == pl.num_programs(0) - 1)
    def _():
        head, width = pair_grad.shape
        fill = jnp.zeros((width, LANES - head), jnp.float32)
        grads = jnp.concatenate([pair_grad[...].T, fill], axis=1).astype(jnp.bfloat16)
        values = sums[...]
        small = [
            values[i : i + 1, j : j + LANES] for i in range(4) for j in range(0, width, LANES)
        ]
        pair_row = jnp.broadcast_to(pair_sum[...], (head, LANES)).T[:1]
        small.append(jnp.concatenate([pair_row, jnp.zeros((1, LANES - head), jnp.float32)], axis=1))
        small = jnp.concatenate(small + [early[...]])
        spare = payload.shape[1] - small.shape[0] - padded_rows(shard_rows)
        small = jnp.concatenate([small, jnp.zeros((spare, LANES), jnp.float32)]).astype(jnp.bfloat16)
        for device in range(payload.shape[0]):
            piece = grads[device * shard_rows : (device + 1) * shard_rows]
            payload[device, :shard_rows] = piece
            payload[device, padded_rows(shard_rows) :] = small


def padded_rows(rows):
    return rows + -rows % 16


def ends_kernel(
    own, other, cotangent, tokens, branch, other_branch, first_bias, second_bias, tokens_grad, result
):
    grad = own[...].astype(jnp.float32) + other[...].astype(jnp.float32)
    values = tokens[...].astype(jnp.float32)
    normed, spread = norm_parts(values)
    inner = (
        grad
        - jnp.mean(grad, axis=-1, keepdims=True)
        - normed * jnp.mean(grad * normed, axis=-1, keepdims=True)
    )
    tokens_grad[...] = (cotangent[...].astype(jnp.float32) + spread * inner).astype(jnp.bfloat16)
    mixed = branch[...].astype(jnp.float32) + other_branch[...].astype(jnp.float32)
    result[...] = (values + mixed + as_row(first_bias) + as_row(second_bias)).astype(jnp.bfloat16)


def sum_kernel(
    shard_rows, shared_rows, got, own, out_sum, up_sum, query_sum, out_again
):
    total = got[0].astype(jnp.float32)
    for device in range(1, got.shape[0]):
        total += got[device].astype(jnp.float32)
    small = total[padded_rows(shard_rows) :]
    own[...] = jnp.concatenate([total[:shard_rows], small[:shared_rows]])
    at = shared_rows
    for out in (out_sum, up_sum, query_sum):
        out[...] = small[at : at + out.shape[0]]
        at += out.shape[0]
    out_again[...] = out_sum[...]


def grads_kernel(cut, hidden_width, *refs):
    terms, (query_grad, out_grad, up_grad, down_grad) = refs[:-4], refs[-4:]
    values = [term[...].astype(jnp.float32) for term in terms]
    bulk = sum(values[1:-4], values[0])
    third = values[-4] + values[-3]
    query_grad[...] = values[-2] + values[-1]
    up_grad[...] = bulk[:, :hidden_width]
    out_grad[...] = third[:, cut:]
    down_grad[:, :cut] = third[:, :cut]
    down_grad[:, cut:] = bulk[:, hidden_width:]


def last_kernel(shard_rows, head, core, own, other, key_grad, value_grad, key_sum, value_sum, *sums):
    first = core[0] == 0
    mine, theirs = own[...], other[...]
    keys = jnp.where(first, mine, theirs)
    values = jnp.where(first, theirs, mine)
    key_grad[...] = keys[:shard_rows, :head]
    value_grad[...] = values[:shard_rows, :head]
    key_sum[...] = keys[keys.shape[0] - 1 :, :head]
    value_sum[...] = values[keys.shape[0] - 1 :, :head]
    both = mine + theirs
    rows = sums[0].shape[0]
    for i, out in enumerate(sums):
        out[...] = both[shard_rows + i * rows : shard_rows + (i + 1) * rows]


def by_rows(kernel, name, rows, moving, fixed, outs, flops=0, grant=20, scratch=()):
    steps = moving[0][0].shape[moving[0][1]] // rows

    def spec(values, cut):
        if cut is None:
            whole = (0,) * len(values.shape)
            return pl.BlockSpec(values.shape, lambda i: whole)
        if cut == 0:
            return pl.BlockSpec((rows, values.shape[1]), lambda i: (i, 0))
        return pl.BlockSpec((values.shape[0], rows), lambda i: (0, i))

    arrays = [values for values, _ in moving] + fixed
    moved = sum(values.size * values.dtype.itemsize for values in arrays + [o for o, _ in outs])
    return pl.pallas_call(
        kernel,
        grid=(steps,),
        in_specs=[spec(*entry) for entry in moving] + [spec(values, None) for values in fixed],
        out_specs=[spec(*entry) for entry in outs],
        out_shape=[entry[0] for entry in outs],
        scratch_shapes=list(scratch),
        compiler_params=pltpu.CompilerParams(vmem_limit_bytes=grant << 20),
        cost_estimate=pl.CostEstimate(flops=flops, bytes_accessed=moved, transcendentals=0),
        name=name,
    )(*arrays)


def rotate(values, cosine, sine):
    half = ROT // 2
    first = values[..., :half, :]
    second = values[..., half:ROT, :]
    return jnp.concatenate(
        [first * cosine - second * sine, second * cosine + first * sine, values[..., ROT:, :]],
        axis=-2,
    )


def allowed_pairs(block, key_block, start, last):
    key_index = block * key_block + lax.broadcasted_iota(
        jnp.int32, (key_block, start.shape[1]), 0
    )
    return (key_index >= start) & (key_index <= last)


def over_blocks(starts, at, begin, block_rows, key_block, body):
    shift = key_block.bit_length() - 1
    lo = starts[at * block_rows] >> shift
    hi = (begin + (block_rows - 1) >> shift) + 1
    a = starts[at * block_rows + block_rows - 1] + (key_block - 1) >> shift
    b = begin + 1 >> shift

    def step(block, carry):
        inside = (block >= a) & (block < b)

        @pl.when(inside)
        def _():
            body(block, False)

        @pl.when(jnp.logical_not(inside))
        def _():
            body(block, True)

        return carry

    lax.fori_loop(lo, hi, step, 0)


def spread_heads(pairs, heads, head, block):
    for h in range(heads):
        for wide, tall in pairs:
            wide[:, pl.ds(h * block, block)] = tall[pl.ds(h * head, head), :]


def forward_kernel(
    before, heads, head, key_block, starts, query, pair, start, out, out_low, logsum,
    wide, best, total, accum, first, last,
):
    block_rows = query.shape[1]
    at = pl.program_id(0) * pl.num_programs(1) + pl.program_id(1)
    begin = before + pl.program_id(1) * block_rows
    factor = head**-0.5 * LOG2E
    best[...] = jnp.full(best.shape, NEGATIVE, jnp.float32)
    total[...] = jnp.zeros(total.shape, jnp.float32)
    accum[...] = jnp.zeros(accum.shape, jnp.float32)
    spread_heads([(wide, query)], heads, head, block_rows)
    index = begin + lax.broadcasted_iota(jnp.int32, (1, block_rows), 1)
    for h in range(heads):
        first[:, pl.ds(h * block_rows, block_rows)] = start[...]
        last[:, pl.ds(h * block_rows, block_rows)] = index

    def body(block, masked):
        keys = pl.ds(pl.multiple_of(block * key_block, key_block), key_block)
        key = pair[0, :head, keys].T
        value = pair[0, head:, keys]
        value = jnp.concatenate([value, jnp.ones((8, key_block), jnp.bfloat16)], axis=0)
        scores = dot(key, wide[...], 1, 0) * factor
        if masked:
            allowed = allowed_pairs(block, key_block, first[...], last[...])
            scores = jnp.where(allowed, scores, NEGATIVE)
        old = best[...]
        fresh = jnp.maximum(old, jnp.max(scores, axis=0, keepdims=True))
        weights = jnp.exp2(scores - fresh).astype(jnp.bfloat16)
        shrink = jnp.exp2(old - fresh)
        best[...] = fresh
        product = dot(value, weights, 1, 0)
        accum[...] = accum[...] * shrink + product[:head]
        total[...] = total[...] * shrink + product[head : head + 1]

    over_blocks(starts, at, begin, block_rows, key_block, body)
    scaled = accum[...] / total[...]
    sums = best[...] + jnp.log(total[...]) * LOG2E
    for h in range(heads):
        columns = slice(h * block_rows, (h + 1) * block_rows)
        rows = pl.ds(h * head, head)
        out[rows, :] = scaled[:, columns]
        logsum[pl.ds(h, 1), :] = sums[:, columns]
    out_low[...] = out[...].astype(jnp.bfloat16).T


def backward_kernel(
    before, heads, head, key_block, starts, query, pair, start, grad, out, logsum, cosine, sine,
    query_grad, pair_grad,
    wide, wide_grad, query_sum, pair_sum, sums, delta, first, last,
):
    block_rows = query.shape[1]
    at = pl.program_id(0) * pl.num_programs(1) + pl.program_id(1)
    begin = before + pl.program_id(1) * block_rows
    scale = head**-0.5

    @pl.when(pl.program_id(1) == 0)
    def _():
        pair_sum[...] = jnp.zeros(pair_sum.shape, jnp.float32)

    query_sum[...] = jnp.zeros(query_sum.shape, jnp.float32)
    spread_heads([(wide, query), (wide_grad, grad)], heads, head, block_rows)
    index = begin + lax.broadcasted_iota(jnp.int32, (1, block_rows), 1)
    for h in range(heads):
        rows = pl.ds(h * head, head)
        columns = pl.ds(h * block_rows, block_rows)
        first[:, columns] = start[...]
        last[:, columns] = index
        sums[:, columns] = logsum[pl.ds(h, 1), :]
        delta[:, columns] = jnp.sum(
            grad[rows, :].astype(jnp.float32) * out[rows, :], axis=0, keepdims=True
        )

    def body(block, masked):
        keys = pl.ds(pl.multiple_of(block * key_block, key_block), key_block)
        key_wide = pair[0, :head, keys]
        key = key_wide.T
        value = pair[0, head:, keys].T
        scores = dot(key, wide[...], 1, 0) * (scale * LOG2E)
        probs = jnp.exp2(scores - sums[...])
        if masked:
            allowed = allowed_pairs(block, key_block, first[...], last[...])
            probs = jnp.where(allowed, probs, 0.0)
        pair_sum[head:, keys] += dot(wide_grad[...], probs.astype(jnp.bfloat16), 1, 1)
        prob_grad = dot(value, wide_grad[...], 1, 0)
        score_grad = (probs * (prob_grad - delta[...])).astype(jnp.bfloat16)
        pair_sum[:head, keys] += dot(wide[...], score_grad, 1, 1)
        query_sum[...] += dot(key_wide, score_grad, 1, 0)

    over_blocks(starts, at, begin, block_rows, key_block, body)
    half = ROT // 2
    turned_heads = []
    for h in range(heads):
        value = query_sum[:, pl.ds(h * block_rows, block_rows)] * scale
        near, far = value[:half], value[half:ROT]
        turned = jnp.concatenate(
            [
                near * cosine[...] + far * sine[...],
                far * cosine[...] - near * sine[...],
                value[ROT:],
            ],
            axis=0,
        )
        turned_heads.append(turned.astype(jnp.bfloat16))
    query_grad[...] = jnp.concatenate(turned_heads, axis=0).T

    @pl.when(pl.program_id(1) == pl.num_programs(1) - 1)
    def _():
        pair_grad[0, :head, :] = (pair_sum[:head, :] * scale).astype(jnp.bfloat16)
        pair_grad[0, head:, :] = pair_sum[head:, :].astype(jnp.bfloat16)


def attention_cost(micro, rows, length, products):
    pairs = micro * (rows // 64) * length * 2 * length
    return pl.CostEstimate(
        flops=2 * products * 64 * pairs, bytes_accessed=8 * micro * rows * length, transcendentals=pairs
    )


def attend_forward(start, query, pair, before, heads, head):
    micro, _, window = pair.shape
    rows, count = query.shape
    length = count // micro
    query_block, key_block = forward_blocks
    blocks = length // query_block
    spread = heads * query_block
    column = lambda m, i, starts: (0, m * blocks + i)
    tall = pl.BlockSpec((rows, query_block), column)
    return pl.pallas_call(
        functools.partial(forward_kernel, before, heads, head, key_block),
        grid_spec=pltpu.PrefetchScalarGridSpec(
            num_scalar_prefetch=1,
            grid=(micro, blocks),
            in_specs=[
                tall,
                pl.BlockSpec((1, 2 * head, window), lambda m, i, starts: (m, 0, 0)),
                pl.BlockSpec((1, query_block), column),
            ],
            out_specs=[
                tall,
                pl.BlockSpec((query_block, rows), lambda m, i, starts: (m * blocks + i, 0)),
                pl.BlockSpec((heads, query_block), column),
            ],
            scratch_shapes=[
                pltpu.VMEM((head, spread), jnp.bfloat16),
                pltpu.VMEM((1, spread), jnp.float32),
                pltpu.VMEM((1, spread), jnp.float32),
                pltpu.VMEM((head, spread), jnp.float32),
                pltpu.VMEM((1, spread), jnp.int32),
                pltpu.VMEM((1, spread), jnp.int32),
            ],
        ),
        out_shape=[
            jax.ShapeDtypeStruct((rows, count), jnp.float32),
            jax.ShapeDtypeStruct((count, rows), jnp.bfloat16),
            jax.ShapeDtypeStruct((heads, count), jnp.float32),
        ],
        compiler_params=pltpu.CompilerParams(vmem_limit_bytes=32 << 20),
        cost_estimate=attention_cost(micro, rows, length, 2),
        name="attend_forward",
    )(start, query, pair, start.reshape(1, count))


def attend_backward(start, query, pair, grad, out, logsum, cosine, sine, before, heads, head):
    micro, _, window = pair.shape
    rows, count = query.shape
    length = count // micro
    query_block, key_block = backward_blocks
    blocks = length // query_block
    spread = heads * query_block
    column = lambda m, i, starts: (0, m * blocks + i)
    tall = pl.BlockSpec((rows, query_block), column)
    table = pl.BlockSpec((ROT // 2, query_block), column)
    keys = pl.BlockSpec((1, 2 * head, window), lambda m, i, starts: (m, 0, 0))
    return pl.pallas_call(
        functools.partial(backward_kernel, before, heads, head, key_block),
        grid_spec=pltpu.PrefetchScalarGridSpec(
            num_scalar_prefetch=1,
            grid=(micro, blocks),
            in_specs=[
                tall,
                keys,
                pl.BlockSpec((1, query_block), column),
                tall,
                tall,
                pl.BlockSpec((heads, query_block), column),
                table,
                table,
            ],
            out_specs=[
                pl.BlockSpec((query_block, rows), lambda m, i, starts: (m * blocks + i, 0)),
                keys,
            ],
            scratch_shapes=[
                pltpu.VMEM((head, spread), jnp.bfloat16),
                pltpu.VMEM((head, spread), jnp.bfloat16),
                pltpu.VMEM((head, spread), jnp.float32),
                pltpu.VMEM((2 * head, window), jnp.float32),
                pltpu.VMEM((1, spread), jnp.float32),
                pltpu.VMEM((1, spread), jnp.float32),
                pltpu.VMEM((1, spread), jnp.int32),
                pltpu.VMEM((1, spread), jnp.int32),
            ],
        ),
        out_shape=[
            jax.ShapeDtypeStruct((count, rows), jnp.bfloat16),
            jax.ShapeDtypeStruct((micro, 2 * head, window), jnp.bfloat16),
        ],
        compiler_params=pltpu.CompilerParams(vmem_limit_bytes=24 << 20),
        cost_estimate=attention_cost(micro, rows, length, 5),
        name="attend_backward",
    )(start, query, pair, start.reshape(1, count), grad, out, logsum, cosine, sine)


def shards(
    tokens,
    segments,
    query_weight,
    query_bias,
    key_weight,
    key_bias,
    value_weight,
    value_bias,
    output_weight,
    output_bias,
    upward_weight,
    upward_bias,
    down_weight,
    down_bias,
    attend_gain,
    attend_bias,
    dense_gain,
    dense_bias,
    cotangent,
):
    low = jnp.bfloat16
    micro, _, length, width = tokens.shape
    count = micro * length
    head = key_weight.shape[1]
    query_width = query_bias.shape[0]
    heads = query_width // head
    hidden_width = upward_bias.shape[0]
    devices = lax.axis_size("fsdp") * lax.axis_size("ctx")
    reach = lax.axis_size("ctx") // 2
    before = reach * length
    window = before + length
    core = lax.axis_index("tp")
    stages = all_bits()
    deep = [s for s in stages if s[0] == "ctx" and s[1] > 1]
    near = [s for s in stages if s[0] == "ctx" and s[1] == 1]
    side = [s for s in stages if s[0] == "fsdp"]

    first_half = core == 0

    def halves(own, other):
        return jnp.where(first_half, own, other), jnp.where(first_half, other, own)

    shard_rows = key_weight.shape[0]
    segment_piece = (segments + 1).astype(low).reshape(-1, head)
    piece_rows = max(shard_rows, segment_piece.shape[0])

    def padded(values):
        return jnp.pad(values, ((0, piece_rows - values.shape[0]), (0, 0)))

    early_piece = jnp.concatenate(
        [
            padded(jnp.where(first_half, key_weight, value_weight)),
            padded(segment_piece),
            padded(query_weight),
        ],
        axis=1,
    )
    early = (early_piece[None], [])
    up = (upward_weight[None], [])
    down = (jnp.concatenate([down_weight.T, output_weight.T], axis=1)[None], [])
    up_order = deep + near + side
    down_order = deep + side + near
    early_order = deep + side + near
    inputs = tokens.reshape(count, width)
    for stage in early_order:
        got = partner(early[0], stage)
        if stage == early_order[-2]:
            got, norm_inputs = together(got, inputs)
        early = gather_join(early, stage, got)
    up = gather_step(up, up_order[0])
    down = gather_step(down, down_order[0])
    early_all = early[0]
    w_pair = early_all[:, :shard_rows, :head].reshape(width, head)
    w_query = early_all[:, :shard_rows, 2 * head :].reshape(width, query_width)
    segment_all = early_all[:, : segment_piece.shape[0], head : 2 * head].reshape(
        lax.axis_size("fsdp"), lax.axis_size("ctx"), micro, length
    )

    mine = lax.dynamic_index_in_dim(segment_all, lax.axis_index("fsdp"), 0, keepdims=False)
    reached = jnp.concatenate([jnp.zeros((reach,) + mine.shape[1:], low), mine])
    seen = lax.dynamic_slice_in_dim(reached, lax.axis_index("ctx"), reach + 1)
    seen = jnp.transpose(seen, (1, 0, 2)).reshape(micro, window).astype(jnp.int32)
    local = segments[:, 0] + 1
    start = jnp.sum((seen[:, None, :] < local[:, :, None]).astype(jnp.int32), axis=2).reshape(count)
    index = before + jnp.arange(length, dtype=jnp.int32)
    positions = jnp.tile(index, micro) - start
    freqs = jnp.exp(
        jnp.arange(ROT // 2, dtype=jnp.float32) * (-2.0 * math.log(10000.0) / ROT)
    )
    angle = freqs[:, None] * positions.reshape(1, count).astype(jnp.float32)
    cosine, sine = jnp.cos(angle), jnp.sin(angle)
    pair_cosine = jnp.where(first_half, cosine, 1.0)
    pair_sine = jnp.where(first_half, sine, 0.0)

    wide = jax.ShapeDtypeStruct((count, width), low)
    attend_in, dense_in = by_rows(
        norm_kernel,
        "norms",
        256,
        [(norm_inputs, 0)],
        [attend_gain, attend_bias, dense_gain, dense_bias],
        [(wide, 0), (wide, 0)],
        grant=56,
    )

    def by_micro(values):
        return jnp.transpose(values.reshape(head, micro, length), (1, 0, 2)).reshape(-1, length)

    def by_token(values):
        return jnp.transpose(values.reshape(micro, head, length), (1, 0, 2)).reshape(head, count)

    pair_lin = dot(w_pair, attend_in, 0, 1) + jnp.where(first_half, key_bias, value_bias)[:, None]
    pair_mine = by_micro(rotate(pair_lin, pair_cosine, pair_sine).astype(low))
    context = lax.axis_size("ctx")
    for i in range(1, len(stages) - 2):
        up = gather_step(up, up_order[i])
        down = gather_step(down, down_order[i])

    def forward(values, d):
        return lax.ppermute(values, "ctx", [(i, i + d) for i in range(context - d)])

    farthest = forward(pair_mine, reach)
    held = pair_mine
    while held.shape[1] < before:
        held = jnp.concatenate([forward(held, held.shape[1] // length), held], axis=1)
    pair_half = jnp.concatenate([farthest, held], axis=1)
    up = gather_step(up, up_order[-2])
    down = gather_step(down, down_order[-2])
    pair_other = partner(pair_half, ("tp", 1))
    pair = jnp.concatenate(
        [side_half.reshape(micro, head, window) for side_half in halves(pair_half, pair_other)],
        axis=1,
    )

    query_lin = dot(w_query, attend_in, 0, 1) + query_bias[:, None]
    query = (
        rotate(query_lin.reshape(heads, head, count), cosine, sine)
        .astype(low)
        .reshape(query_width, count)
    )
    attended, attended_low, logsum = attend_forward(start, query, pair, before, heads, head)
    w_upward = gather_step(up, up_order[-1])[0].reshape(width, hidden_width)
    w_down = gather_step(down, down_order[-1])[0].reshape(width, hidden_width + query_width)
    w_down, w_output = w_down[:, :hidden_width], w_down[:, hidden_width:]

    grad_low = cotangent.reshape(count, width)
    hidden_pre = dot(dense_in, w_upward, 1, 0) + upward_bias
    normal_cdf = 0.5 * (1.0 + lax.erf(hidden_pre * (1.0 / math.sqrt(2.0))))
    normal_pdf = jnp.exp(-0.5 * hidden_pre * hidden_pre) * (1.0 / math.sqrt(2.0 * math.pi))
    hidden = (hidden_pre * normal_cdf).astype(low)
    slope = normal_cdf + hidden_pre * normal_pdf
    hidden, slope = together(hidden, slope.astype(low))
    pre_grad = (dot(grad_low, w_down, 1, 0) * slope.astype(jnp.float32)).astype(low)

    def by_device(values):
        return values.astype(low).reshape(devices, shard_rows, values.shape[1])

    up_order = side + near + deep[::-1]
    down_order = near + side + deep[::-1]
    up = (by_device(dot(dense_in, pre_grad, 0, 0)), stages)
    row_major = Layout(major_to_minor=(0, 1))

    def term(left, right):
        return with_layout_constraint(dot(left, right, 0, 0).astype(low), row_major)

    cut = hidden_width // 2
    down_terms = term(grad_low, hidden)
    third = jnp.concatenate([down_terms[:, :cut], term(grad_low, attended_low)], axis=1)
    third = by_device(third)
    shape = (lax.axis_size("fsdp"), context // 2, 2) + third.shape[1:]
    third_own, third_gots = deep_send(third.reshape(shape), 1)
    down = (by_device(down_terms[:, cut:]), stages)
    attended_grad = dot(w_output, grad_low, 0, 1).astype(low)
    down, down_got = scatter_send(down, down_order[0])
    attended_grad, up_held = together(attended_grad, up[0])
    up, up_got = scatter_send((up_held, up[1]), up_order[0])
    query_grad, pair_back = attend_backward(
        start, query, pair, attended_grad, attended, logsum, cosine, sine, before, heads, head
    )
    query_grad, pair_back, hidden, pre_grad, grad_late, up_got, down_got, *third_gots = together(
        query_grad, pair_back, hidden, pre_grad, grad_low, up_got, down_got, *third_gots
    )
    third = sum_all([third_own] + third_gots).astype(low)
    third = third.reshape((-1,) + third.shape[2:])
    pair_back = pair_back.reshape(micro, 2, head, window)

    keep, send = halves(pair_back[:, 0], pair_back[:, 1])
    pair_other = partner(send, ("tp", 1))
    asked_order = side + near + deep[::-1]
    asked = by_device(dot(attend_in, query_grad, 0, 0))
    pair_other, asked, hidden, pre_grad, grad_late = together(
        pair_other, asked, hidden, pre_grad, grad_late
    )
    up, up_got = scatter_send(scatter_join(up, up_got), up_order[1])
    down, down_got = scatter_send(scatter_join(down, down_got), down_order[1])
    asked, asked_got = scatter_send((asked, stages), asked_order[0])
    branches = (dot(attended_low, w_output, 1, 1) + dot(hidden, w_down, 1, 1)).astype(low)
    dense_part = dot(pre_grad, w_upward, 1, 1).astype(low)
    early_sums = jnp.concatenate(
        [
            jnp.sum(grad_late.astype(jnp.float32), axis=0),
            jnp.sum(pre_grad.astype(jnp.float32), axis=0),
            jnp.sum(query_grad.astype(jnp.float32), axis=0),
        ]
    )
    summed = (keep.astype(jnp.float32) + pair_other.astype(jnp.float32)).astype(low)
    summed = summed.reshape(micro * head, window)

    def backward(values, d):
        return lax.ppermute(values.astype(low), "ctx", [(i + d, i) for i in range(context - d)])

    held = summed.astype(jnp.float32)
    step = reach // 2
    while step > 1:
        got = backward(held[:, : step * length], step)
        if step == reach // 2:
            got, asked_got, branches, dense_part, early_sums, up_got, down_got = together(
                got, asked_got, branches, dense_part, early_sums, up_got, down_got
            )
        held = held[:, step * length :]
        held = jnp.concatenate(
            [held[:, : step * length] + got.astype(jnp.float32), held[:, step * length :]], axis=1
        )
        step //= 2
    asked, asked_got = scatter_send(scatter_join(asked, asked_got), asked_order[1])
    branches_other = partner(branches, ("tp", 1))
    up = scatter_rest(scatter_join(up, up_got), up_order[2 : -len(deep)])
    down = scatter_rest(scatter_join(down, down_got), down_order[2 : -len(deep)])
    bulk, bulk_gots = deep_send(jnp.concatenate([up[0], down[0]], axis=2), 0)
    gots = [backward(held[:, (2 - d) * length : (3 - d) * length], d) for d in (1, 2)]
    third, asked_got, branches_other, *gots = together(third, asked_got, branches_other, *gots)
    third, third_got = scatter_send((third, side + near), side[0])
    pair_sum = held[:, 2 * length :] + gots[0].astype(jnp.float32) + gots[1].astype(jnp.float32)
    asked, asked_got = scatter_send(scatter_join(asked, asked_got), asked_order[2])
    pair_low = rotate(by_token(pair_sum), pair_cosine, -pair_sine).astype(low)

    shared_rows = 4 * width // LANES + 1
    small_rows = shared_rows + early_sums.shape[0] // LANES
    payload_rows = padded_rows(shard_rows) + padded_rows(small_rows)
    norm_part, payload = by_rows(
        functools.partial(part_kernel, shard_rows),
        "parts",
        256,
        [
            (query_grad, 0),
            (pair_low, 1),
            (w_query, None),
            (w_pair, None),
            (dense_part, 0),
            (inputs, 0),
        ],
        [attend_gain, attend_bias, dense_gain, early_sums.reshape(-1, LANES)],
        [(wide, 0), (jax.ShapeDtypeStruct((devices, payload_rows, LANES), low), None)],
        2 * count * width * (query_width + head),
        scratch=[
            pltpu.VMEM((4, width), jnp.float32),
            pltpu.VMEM((head, width), jnp.float32),
            pltpu.VMEM((head, 1), jnp.float32),
        ],
    )
    payload, norm_part, asked_got, third_got, branches_other, *bulk_gots[:-1] = together(
        payload, norm_part, asked_got, third_got, branches_other, *bulk_gots[:-1]
    )
    third = scatter_rest(scatter_join(third, third_got), side[1:])
    third, third_got = scatter_send(third, near[0])
    got = lax.all_to_all(payload, ("fsdp", "ctx"), 0, 0)
    norm_other = partner(norm_part, ("tp", 1))
    asked = scatter_rest(scatter_join(asked, asked_got), asked_order[3:-1])
    asked, asked_got = scatter_send(asked, asked_order[-1])
    tokens_grad, result = by_rows(
        ends_kernel,
        "ends",
        128,
        [
            (norm_part, 0),
            (norm_other, 0),
            (grad_low, 0),
            (inputs, 0),
            (branches, 0),
            (branches_other, 0),
        ],
        [output_bias, down_bias],
        [(wide, 0), (wide, 0)],
        grant=56,
    )
    got, asked_got, third_got, tokens_grad, result, *bulk_gots = together(
        got, asked_got, third_got, tokens_grad, result, *bulk_gots
    )
    def rows_of(count):
        return jax.ShapeDtypeStruct((count, LANES), jnp.float32)

    sizes = [width // LANES, hidden_width // LANES, query_width // LANES, width // LANES]
    own, out_b, up_b, q_b, down_b = pl.pallas_call(
        functools.partial(sum_kernel, shard_rows, shared_rows),
        out_shape=[rows_of(shard_rows + shared_rows)] + [rows_of(size) for size in sizes],
        name="sums",
    )(got)
    other = partner(own, ("tp", 1))
    terms = [bulk] + bulk_gots + [third[0][0], third_got[0], asked[0][0], asked_got[0]]
    grad_query, grad_out, grad_up, grad_down = pl.pallas_call(
        functools.partial(grads_kernel, cut, hidden_width),
        out_shape=[
            jax.ShapeDtypeStruct((shard_rows, columns), jnp.float32)
            for columns in (query_width, query_width, hidden_width, hidden_width)
        ],
        name="grads",
    )(*terms)
    outs = pl.pallas_call(
        functools.partial(last_kernel, shard_rows, head),
        out_shape=[jax.ShapeDtypeStruct((shard_rows, head), jnp.float32)] * 2
        + [jax.ShapeDtypeStruct((1, head), jnp.float32)] * 2
        + [rows_of(width // LANES)] * 4,
        in_specs=[pl.BlockSpec(memory_space=pltpu.SMEM)] + [pl.BlockSpec(memory_space=pltpu.VMEM)] * 2,
        name="last",
    )(core.astype(jnp.int32).reshape(1), own, other)
    grad_key, grad_value, k_b, v_b = outs[0], outs[1], outs[2].reshape(-1), outs[3].reshape(-1)
    g_gain, g_shift, d_gain, d_shift = [values.reshape(-1) for values in outs[4:]]
    out_b, up_b, q_b, down_b = [values.reshape(-1) for values in (out_b, up_b, q_b, down_b)]
    shape = (micro, 1, length, width)
    return (
        result.reshape(shape),
        tokens_grad.reshape(shape),
        grad_query,
        q_b,
        grad_key,
        k_b,
        grad_value,
        v_b,
        grad_out.T,
        out_b,
        grad_up,
        up_b,
        grad_down.T,
        down_b,
        g_gain,
        g_shift,
        d_gain,
        d_shift,
    )


def solution(mesh):
    return jax.shard_map(
        shards,
        mesh=mesh,
        in_specs=(
            P(None, "fsdp", "ctx", None),
            P(None, "fsdp", "ctx"),
            P(("fsdp", "ctx"), "tp"),
            P("tp"),
            P(("fsdp", "ctx"), None),
            P(),
            P(("fsdp", "ctx"), None),
            P(),
            P("tp", ("fsdp", "ctx")),
            P(),
            P(("fsdp", "ctx"), "tp"),
            P("tp"),
            P("tp", ("fsdp", "ctx")),
            P(),
            P(),
            P(),
            P(),
            P(),
            P(None, "fsdp", "ctx", None),
        ),
        out_specs=(
            P(None, "fsdp", "ctx", None),
            P(None, "fsdp", "ctx", None),
            P(("fsdp", "ctx"), "tp"),
            P("tp"),
            P(("fsdp", "ctx"), None),
            P(),
            P(("fsdp", "ctx"), None),
            P(),
            P("tp", ("fsdp", "ctx")),
            P(),
            P(("fsdp", "ctx"), "tp"),
            P("tp"),
            P("tp", ("fsdp", "ctx")),
            P(),
            P(),
            P(),
            P(),
            P(),
        ),
        check_vma=False,
    )
```

```python
import functools
import math

import jax
import jax.numpy as jnp
from jax import lax
from jax.experimental.layout import Layout, with_layout_constraint
from jax.experimental import pallas as pl
from jax.experimental.pallas import tpu as pltpu
from jax.sharding import PartitionSpec as P

ROT = 16
NEGATIVE = -1e30
EPSILON = 1e-05
LOG2E = math.log2(math.e)
LANES = 128
forward_blocks = (512, 512)
backward_blocks = (256, 256)


def dot(left, right, left_dim, right_dim):
    return lax.dot_general(
        left,
        right,
        (((left_dim,), (right_dim,)), ((), ())),
        preferred_element_type=jnp.float32,
    )


def axis_bits(name):
    return [1 << b for b in reversed(range(lax.axis_size(name).bit_length() - 1))]


def all_bits():
    return [("fsdp", d) for d in axis_bits("fsdp")] + [("ctx", d) for d in axis_bits("ctx")]


def partner(values, stage):
    name, distance = stage
    pairs = [(i, i ^ distance) for i in range(lax.axis_size(name))]
    return lax.ppermute(values, name, pairs)


def own_bit(stage):
    name, distance = stage
    return (lax.axis_index(name) // distance) % 2 == 1


def gather_join(state, stage, other):
    held, done = state
    rank = {other_stage: i for i, other_stage in enumerate(all_bits())}
    low = 1 << sum(rank[earlier] > rank[stage] for earlier in done)
    piece = held.shape[1:]
    split = held.reshape((held.shape[0] // low, 1, low) + piece)
    other = other.reshape(split.shape)
    upper = own_bit(stage)
    held = jnp.concatenate(
        [jnp.where(upper, other, split), jnp.where(upper, split, other)], axis=1
    ).reshape((2 * held.shape[0],) + piece)
    return held, done + [stage]


def scatter_send(state, stage):
    held, left = state
    rank = {other: i for i, other in enumerate(all_bits())}
    low = 1 << sum(rank[other] > rank[stage] for other in left if other != stage)
    piece = held.shape[1:]
    split = held.reshape((held.shape[0] // (2 * low), 2, low) + piece)
    upper = own_bit(stage).astype(jnp.int32)
    shape = (held.shape[0] // 2,) + piece
    send = lax.dynamic_index_in_dim(split, 1 - upper, 1, keepdims=False).reshape(shape)
    keep = lax.dynamic_index_in_dim(split, upper, 1, keepdims=False).reshape(shape)
    return (keep, [other for other in left if other != stage]), partner(send, stage)


def scatter_join(kept, other):
    keep, left = kept
    total = keep.astype(jnp.float32) + other.astype(jnp.float32)
    return (total.astype(jnp.bfloat16) if left else total), left


def scatter_rest(state, order):
    for stage in order:
        state = scatter_step(state, stage)
    return state


def gather_step(state, stage):
    return gather_join(state, stage, partner(state[0], stage))


def scatter_step(state, stage):
    return scatter_join(*scatter_send(state, stage))


def deep_rank():
    return lax.axis_index("ctx") // 2


def deep_send(terms, axis):
    size = terms.shape[axis]
    own, *others = [
        lax.dynamic_index_in_dim(terms, deep_rank() ^ mask, axis, keepdims=False)
        for mask in range(size)
    ]
    return own, [partner(values, ("ctx", 2 * mask + 2)) for mask, values in enumerate(others)]


def sum_all(values):
    return sum(other.astype(jnp.float32) for other in values)


def together(*values):
    return lax.optimization_barrier(values)


def norm_parts(values):
    centre = values - jnp.mean(values, axis=-1, keepdims=True)
    spread = lax.rsqrt(jnp.mean(centre * centre, axis=-1, keepdims=True) + EPSILON)
    return centre * spread, spread


def as_row(values):
    return values[...].reshape(1, values.shape[0])


def norm_kernel(
    tokens, attend_gain, attend_bias, dense_gain, dense_bias, attend_in, dense_in
):
    normed, _ = norm_parts(tokens[...].astype(jnp.float32))
    attend_in[...] = (normed * as_row(attend_gain) + as_row(attend_bias)).astype(jnp.bfloat16)
    dense_in[...] = (normed * as_row(dense_gain) + as_row(dense_bias)).astype(jnp.bfloat16)


def part_kernel(
    shard_rows, query_grad, pair_low, w_query, w_pair, dense_part, tokens, attend_gain, attend_bias,
    dense_gain, early, norm_part, payload, sums, pair_grad, pair_sum,
):
    step = pl.program_id(0)
    attend_part = dot(query_grad[...], w_query[...], 1, 1) + dot(pair_low[...].T, w_pair[...], 1, 1)
    dense = dense_part[...].astype(jnp.float32)
    normed, _ = norm_parts(tokens[...].astype(jnp.float32))
    norm_part[...] = (
        attend_part * as_row(attend_gain) + dense * as_row(dense_gain)
    ).astype(jnp.bfloat16)
    attend_in = (normed * as_row(attend_gain) + as_row(attend_bias)).astype(jnp.bfloat16)

    @pl.when(step == 0)
    def _():
        sums[...] = jnp.zeros(sums.shape, jnp.float32)
        pair_grad[...] = jnp.zeros(pair_grad.shape, jnp.float32)
        pair_sum[...] = jnp.zeros(pair_sum.shape, jnp.float32)

    rows = [attend_part * normed, attend_part, dense * normed, dense]
    sums[...] += jnp.concatenate([jnp.sum(row, axis=0, keepdims=True) for row in rows])
    pair_grad[...] += dot(pair_low[...], attend_in, 1, 0)
    pair_sum[...] += jnp.sum(pair_low[...].astype(jnp.float32), axis=1, keepdims=True)

    @pl.when(step == pl.num_programs(0) - 1)
    def _():
        head, width = pair_grad.shape
        fill = jnp.zeros((width, LANES - head), jnp.float32)
        grads = jnp.concatenate([pair_grad[...].T, fill], axis=1).astype(jnp.bfloat16)
        values = sums[...]
        small = [
            values[i : i + 1, j : j + LANES] for i in range(4) for j in range(0, width, LANES)
        ]
        pair_row = jnp.broadcast_to(pair_sum[...], (head, LANES)).T[:1]
        small.append(jnp.concatenate([pair_row, jnp.zeros((1, LANES - head), jnp.float32)], axis=1))
        small = jnp.concatenate(small + [early[...]])
        spare = payload.shape[1] - small.shape[0] - padded_rows(shard_rows)
        small = jnp.concatenate([small, jnp.zeros((spare, LANES), jnp.float32)]).astype(jnp.bfloat16)
        for device in range(payload.shape[0]):
            piece = grads[device * shard_rows : (device + 1) * shard_rows]
            payload[device, :shard_rows] = piece
            payload[device, padded_rows(shard_rows) :] = small


def padded_rows(rows):
    return rows + -rows % 16


def ends_kernel(
    own, other, cotangent, tokens, branch, other_branch, first_bias, second_bias, tokens_grad, result
):
    grad = own[...].astype(jnp.float32) + other[...].astype(jnp.float32)
    values = tokens[...].astype(jnp.float32)
    normed, spread = norm_parts(values)
    inner = (
        grad
        - jnp.mean(grad, axis=-1, keepdims=True)
        - normed * jnp.mean(grad * normed, axis=-1, keepdims=True)
    )
    tokens_grad[...] = (cotangent[...].astype(jnp.float32) + spread * inner).astype(jnp.bfloat16)
    mixed = branch[...].astype(jnp.float32) + other_branch[...].astype(jnp.float32)
    result[...] = (values + mixed + as_row(first_bias) + as_row(second_bias)).astype(jnp.bfloat16)


def sum_kernel(
    shard_rows, shared_rows, got, own, out_sum, up_sum, query_sum, out_again
):
    total = got[0].astype(jnp.float32)
    for device in range(1, got.shape[0]):
        total += got[device].astype(jnp.float32)
    small = total[padded_rows(shard_rows) :]
    own[...] = jnp.concatenate([total[:shard_rows], small[:shared_rows]])
    at = shared_rows
    for out in (out_sum, up_sum, query_sum):
        out[...] = small[at : at + out.shape[0]]
        at += out.shape[0]
    out_again[...] = out_sum[...]


def grads_kernel(cut, hidden_width, *refs):
    terms, (query_grad, out_grad, up_grad, down_grad) = refs[:-4], refs[-4:]
    values = [term[...].astype(jnp.float32) for term in terms]
    bulk = sum(values[1:-4], values[0])
    third = values[-4] + values[-3]
    query_grad[...] = values[-2] + values[-1]
    up_grad[...] = bulk[:, :hidden_width]
    out_grad[...] = third[:, cut:]
    down_grad[:, :cut] = third[:, :cut]
    down_grad[:, cut:] = bulk[:, hidden_width:]


def last_kernel(shard_rows, head, core, own, other, key_grad, value_grad, key_sum, value_sum, *sums):
    first = core[0] == 0
    mine, theirs = own[...], other[...]
    keys = jnp.where(first, mine, theirs)
    values = jnp.where(first, theirs, mine)
    key_grad[...] = keys[:shard_rows, :head]
    value_grad[...] = values[:shard_rows, :head]
    key_sum[...] = keys[keys.shape[0] - 1 :, :head]
    value_sum[...] = values[keys.shape[0] - 1 :, :head]
    both = mine + theirs
    rows = sums[0].shape[0]
    for i, out in enumerate(sums):
        out[...] = both[shard_rows + i * rows : shard_rows + (i + 1) * rows]


def by_rows(kernel, name, rows, moving, fixed, outs, flops=0, grant=20, scratch=()):
    steps = moving[0][0].shape[moving[0][1]] // rows

    def spec(values, cut):
        if cut is None:
            whole = (0,) * len(values.shape)
            return pl.BlockSpec(values.shape, lambda i: whole)
        if cut == 0:
            return pl.BlockSpec((rows, values.shape[1]), lambda i: (i, 0))
        return pl.BlockSpec((values.shape[0], rows), lambda i: (0, i))

    arrays = [values for values, _ in moving] + fixed
    moved = sum(values.size * values.dtype.itemsize for values in arrays + [o for o, _ in outs])
    return pl.pallas_call(
        kernel,
        grid=(steps,),
        in_specs=[spec(*entry) for entry in moving] + [spec(values, None) for values in fixed],
        out_specs=[spec(*entry) for entry in outs],
        out_shape=[entry[0] for entry in outs],
        scratch_shapes=list(scratch),
        compiler_params=pltpu.CompilerParams(vmem_limit_bytes=grant << 20),
        cost_estimate=pl.CostEstimate(flops=flops, bytes_accessed=moved, transcendentals=0),
        name=name,
    )(*arrays)


def rotate(values, cosine, sine):
    half = ROT // 2
    first = values[..., :half, :]
    second = values[..., half:ROT, :]
    return jnp.concatenate(
        [first * cosine - second * sine, second * cosine + first * sine, values[..., ROT:, :]],
        axis=-2,
    )


def allowed_pairs(block, key_block, start, last):
    key_index = block * key_block + lax.broadcasted_iota(
        jnp.int32, (key_block, start.shape[1]), 0
    )
    return (key_index >= start) & (key_index <= last)


def over_blocks(starts, at, begin, block_rows, key_block, body):
    shift = key_block.bit_length() - 1
    lo = starts[at * block_rows] >> shift
    hi = (begin + (block_rows - 1) >> shift) + 1
    a = starts[at * block_rows + block_rows - 1] + (key_block - 1) >> shift
    b = begin + 1 >> shift

    def step(block, carry):
        inside = (block >= a) & (block < b)

        @pl.when(inside)
        def _():
            body(block, False)

        @pl.when(jnp.logical_not(inside))
        def _():
            body(block, True)

        return carry

    lax.fori_loop(lo, hi, step, 0)


def spread_heads(pairs, heads, head, block):
    for h in range(heads):
        for wide, tall in pairs:
            wide[:, pl.ds(h * block, block)] = tall[pl.ds(h * head, head), :]


def forward_kernel(
    before, heads, head, key_block, starts, query, pair, start, out, out_low, logsum,
    wide, best, total, accum, first, last,
):
    block_rows = query.shape[1]
    at = pl.program_id(0) * pl.num_programs(1) + pl.program_id(1)
    begin = before + pl.program_id(1) * block_rows
    factor = head**-0.5 * LOG2E
    best[...] = jnp.full(best.shape, NEGATIVE, jnp.float32)
    total[...] = jnp.zeros(total.shape, jnp.float32)
    accum[...] = jnp.zeros(accum.shape, jnp.float32)
    spread_heads([(wide, query)], heads, head, block_rows)
    index = begin + lax.broadcasted_iota(jnp.int32, (1, block_rows), 1)
    for h in range(heads):
        first[:, pl.ds(h * block_rows, block_rows)] = start[...]
        last[:, pl.ds(h * block_rows, block_rows)] = index

    def body(block, masked):
        keys = pl.ds(pl.multiple_of(block * key_block, key_block), key_block)
        key = pair[0, :head, keys].T
        value = pair[0, head:, keys]
        value = jnp.concatenate([value, jnp.ones((8, key_block), jnp.bfloat16)], axis=0)
        scores = dot(key, wide[...], 1, 0) * factor
        if masked:
            allowed = allowed_pairs(block, key_block, first[...], last[...])
            scores = jnp.where(allowed, scores, NEGATIVE)
        old = best[...]
        fresh = jnp.maximum(old, jnp.max(scores, axis=0, keepdims=True))
        weights = jnp.exp2(scores - fresh).astype(jnp.bfloat16)
        shrink = jnp.exp2(old - fresh)
        best[...] = fresh
        product = dot(value, weights, 1, 0)
        accum[...] = accum[...] * shrink + product[:head]
        total[...] = total[...] * shrink + product[head : head + 1]

    over_blocks(starts, at, begin, block_rows, key_block, body)
    scaled = accum[...] / total[...]
    sums = best[...] + jnp.log(total[...]) * LOG2E
    for h in range(heads):
        columns = slice(h * block_rows, (h + 1) * block_rows)
        rows = pl.ds(h * head, head)
        out[rows, :] = scaled[:, columns]
        logsum[pl.ds(h, 1), :] = sums[:, columns]
    out_low[...] = out[...].astype(jnp.bfloat16).T


def backward_kernel(
    before, heads, head, key_block, starts, query, pair, start, grad, out, logsum, cosine, sine,
    query_grad, pair_grad,
    wide, wide_grad, query_sum, pair_sum, sums, delta, first, last,
):
    block_rows = query.shape[1]
    at = pl.program_id(0) * pl.num_programs(1) + pl.program_id(1)
    begin = before + pl.program_id(1) * block_rows
    scale = head**-0.5

    @pl.when(pl.program_id(1) == 0)
    def _():
        pair_sum[...] = jnp.zeros(pair_sum.shape, jnp.float32)

    query_sum[...] = jnp.zeros(query_sum.shape, jnp.float32)
    spread_heads([(wide, query), (wide_grad, grad)], heads, head, block_rows)
    index = begin + lax.broadcasted_iota(jnp.int32, (1, block_rows), 1)
    for h in range(heads):
        rows = pl.ds(h * head, head)
        columns = pl.ds(h * block_rows, block_rows)
        first[:, columns] = start[...]
        last[:, columns] = index
        sums[:, columns] = logsum[pl.ds(h, 1), :]
        delta[:, columns] = jnp.sum(
            grad[rows, :].astype(jnp.float32) * out[rows, :], axis=0, keepdims=True
        )

    def body(block, masked):
        keys = pl.ds(pl.multiple_of(block * key_block, key_block), key_block)
        key_wide = pair[0, :head, keys]
        key = key_wide.T
        value = pair[0, head:, keys].T
        scores = dot(key, wide[...], 1, 0) * (scale * LOG2E)
        probs = jnp.exp2(scores - sums[...])
        if masked:
            allowed = allowed_pairs(block, key_block, first[...], last[...])
            probs = jnp.where(allowed, probs, 0.0)
        pair_sum[head:, keys] += dot(wide_grad[...], probs.astype(jnp.bfloat16), 1, 1)
        prob_grad = dot(value, wide_grad[...], 1, 0)
        score_grad = (probs * (prob_grad - delta[...])).astype(jnp.bfloat16)
        pair_sum[:head, keys] += dot(wide[...], score_grad, 1, 1)
        query_sum[...] += dot(key_wide, score_grad, 1, 0)

    over_blocks(starts, at, begin, block_rows, key_block, body)
    half = ROT // 2
    turned_heads = []
    for h in range(heads):
        value = query_sum[:, pl.ds(h * block_rows, block_rows)] * scale
        near, far = value[:half], value[half:ROT]
        turned = jnp.concatenate(
            [
                near * cosine[...] + far * sine[...],
                far * cosine[...] - near * sine[...],
                value[ROT:],
            ],
            axis=0,
        )
        turned_heads.append(turned.astype(jnp.bfloat16))
    query_grad[...] = jnp.concatenate(turned_heads, axis=0).T

    @pl.when(pl.program_id(1) == pl.num_programs(1) - 1)
    def _():
        pair_grad[0, :head, :] = (pair_sum[:head, :] * scale).astype(jnp.bfloat16)
        pair_grad[0, head:, :] = pair_sum[head:, :].astype(jnp.bfloat16)


def attention_cost(micro, rows, length, products):
    pairs = micro * (rows // 64) * length * 2 * length
    return pl.CostEstimate(
        flops=2 * products * 64 * pairs, bytes_accessed=8 * micro * rows * length, transcendentals=pairs
    )


def attend_forward(start, query, pair, before, heads, head):
    micro, _, window = pair.shape
    rows, count = query.shape
    length = count // micro
    query_block, key_block = forward_blocks
    blocks = length // query_block
    spread = heads * query_block
    column = lambda m, i, starts: (0, m * blocks + i)
    tall = pl.BlockSpec((rows, query_block), column)
    return pl.pallas_call(
        functools.partial(forward_kernel, before, heads, head, key_block),
        grid_spec=pltpu.PrefetchScalarGridSpec(
            num_scalar_prefetch=1,
            grid=(micro, blocks),
            in_specs=[
                tall,
                pl.BlockSpec((1, 2 * head, window), lambda m, i, starts: (m, 0, 0)),
                pl.BlockSpec((1, query_block), column),
            ],
            out_specs=[
                tall,
                pl.BlockSpec((query_block, rows), lambda m, i, starts: (m * blocks + i, 0)),
                pl.BlockSpec((heads, query_block), column),
            ],
            scratch_shapes=[
                pltpu.VMEM((head, spread), jnp.bfloat16),
                pltpu.VMEM((1, spread), jnp.float32),
                pltpu.VMEM((1, spread), jnp.float32),
                pltpu.VMEM((head, spread), jnp.float32),
                pltpu.VMEM((1, spread), jnp.int32),
                pltpu.VMEM((1, spread), jnp.int32),
            ],
        ),
        out_shape=[
            jax.ShapeDtypeStruct((rows, count), jnp.float32),
            jax.ShapeDtypeStruct((count, rows), jnp.bfloat16),
            jax.ShapeDtypeStruct((heads, count), jnp.float32),
        ],
        compiler_params=pltpu.CompilerParams(vmem_limit_bytes=32 << 20),
        cost_estimate=attention_cost(micro, rows, length, 2),
        name="attend_forward",
    )(start, query, pair, start.reshape(1, count))


def attend_backward(start, query, pair, grad, out, logsum, cosine, sine, before, heads, head):
    micro, _, window = pair.shape
    rows, count = query.shape
    length = count // micro
    query_block, key_block = backward_blocks
    blocks = length // query_block
    spread = heads * query_block
    column = lambda m, i, starts: (0, m * blocks + i)
    tall = pl.BlockSpec((rows, query_block), column)
    table = pl.BlockSpec((ROT // 2, query_block), column)
    keys = pl.BlockSpec((1, 2 * head, window), lambda m, i, starts: (m, 0, 0))
    return pl.pallas_call(
        functools.partial(backward_kernel, before, heads, head, key_block),
        grid_spec=pltpu.PrefetchScalarGridSpec(
            num_scalar_prefetch=1,
            grid=(micro, blocks),
            in_specs=[
                tall,
                keys,
                pl.BlockSpec((1, query_block), column),
                tall,
                tall,
                pl.BlockSpec((heads, query_block), column),
                table,
                table,
            ],
            out_specs=[
                pl.BlockSpec((query_block, rows), lambda m, i, starts: (m * blocks + i, 0)),
                keys,
            ],
            scratch_shapes=[
                pltpu.VMEM((head, spread), jnp.bfloat16),
                pltpu.VMEM((head, spread), jnp.bfloat16),
                pltpu.VMEM((head, spread), jnp.float32),
                pltpu.VMEM((2 * head, window), jnp.float32),
                pltpu.VMEM((1, spread), jnp.float32),
                pltpu.VMEM((1, spread), jnp.float32),
                pltpu.VMEM((1, spread), jnp.int32),
                pltpu.VMEM((1, spread), jnp.int32),
            ],
        ),
        out_shape=[
            jax.ShapeDtypeStruct((count, rows), jnp.bfloat16),
            jax.ShapeDtypeStruct((micro, 2 * head, window), jnp.bfloat16),
        ],
        compiler_params=pltpu.CompilerParams(vmem_limit_bytes=24 << 20),
        cost_estimate=attention_cost(micro, rows, length, 5),
        name="attend_backward",
    )(start, query, pair, start.reshape(1, count), grad, out, logsum, cosine, sine)


def shards(
    tokens,
    segments,
    query_weight,
    query_bias,
    key_weight,
    key_bias,
    value_weight,
    value_bias,
    output_weight,
    output_bias,
    upward_weight,
    upward_bias,
    down_weight,
    down_bias,
    attend_gain,
    attend_bias,
    dense_gain,
    dense_bias,
    cotangent,
):
    low = jnp.bfloat16
    micro, _, length, width = tokens.shape
    count = micro * length
    head = key_weight.shape[1]
    query_width = query_bias.shape[0]
    heads = query_width // head
    hidden_width = upward_bias.shape[0]
    devices = lax.axis_size("fsdp") * lax.axis_size("ctx")
    reach = lax.axis_size("ctx") // 2
    before = reach * length
    window = before + length
    core = lax.axis_index("tp")
    stages = all_bits()
    deep = [s for s in stages if s[0] == "ctx" and s[1] > 1]
    near = [s for s in stages if s[0] == "ctx" and s[1] == 1]
    side = [s for s in stages if s[0] == "fsdp"]

    first_half = core == 0

    def halves(own, other):
        return jnp.where(first_half, own, other), jnp.where(first_half, other, own)

    shard_rows = key_weight.shape[0]
    segment_piece = (segments + 1).astype(low).reshape(-1, head)
    piece_rows = max(shard_rows, segment_piece.shape[0])

    def padded(values):
        return jnp.pad(values, ((0, piece_rows - values.shape[0]), (0, 0)))

    early_piece = jnp.concatenate(
        [
            padded(jnp.where(first_half, key_weight, value_weight)),
            padded(segment_piece),
            padded(query_weight),
        ],
        axis=1,
    )
    early = (early_piece[None], [])
    up = (upward_weight[None], [])
    down = (jnp.concatenate([down_weight.T, output_weight.T], axis=1)[None], [])
    up_order = deep + near + side
    down_order = deep + side + near
    early_order = deep + side + near
    inputs = tokens.reshape(count, width)
    for stage in early_order:
        got = partner(early[0], stage)
        if stage == early_order[-2]:
            got, norm_inputs = together(got, inputs)
        early = gather_join(early, stage, got)
    up = gather_step(up, up_order[0])
    down = gather_step(down, down_order[0])
    early_all = early[0]
    w_pair = early_all[:, :shard_rows, :head].reshape(width, head)
    w_query = early_all[:, :shard_rows, 2 * head :].reshape(width, query_width)
    segment_all = early_all[:, : segment_piece.shape[0], head : 2 * head].reshape(
        lax.axis_size("fsdp"), lax.axis_size("ctx"), micro, length
    )

    mine = lax.dynamic_index_in_dim(segment_all, lax.axis_index("fsdp"), 0, keepdims=False)
    reached = jnp.concatenate([jnp.zeros((reach,) + mine.shape[1:], low), mine])
    seen = lax.dynamic_slice_in_dim(reached, lax.axis_index("ctx"), reach + 1)
    seen = jnp.transpose(seen, (1, 0, 2)).reshape(micro, window).astype(jnp.int32)
    local = segments[:, 0] + 1
    start = jnp.sum((seen[:, None, :] < local[:, :, None]).astype(jnp.int32), axis=2).reshape(count)
    index = before + jnp.arange(length, dtype=jnp.int32)
    positions = jnp.tile(index, micro) - start
    freqs = jnp.exp(
        jnp.arange(ROT // 2, dtype=jnp.float32) * (-2.0 * math.log(10000.0) / ROT)
    )
    angle = freqs[:, None] * positions.reshape(1, count).astype(jnp.float32)
    cosine, sine = jnp.cos(angle), jnp.sin(angle)
    pair_cosine = jnp.where(first_half, cosine, 1.0)
    pair_sine = jnp.where(first_half, sine, 0.0)

    wide = jax.ShapeDtypeStruct((count, width), low)
    attend_in, dense_in = by_rows(
        norm_kernel,
        "norms",
        128,
        [(norm_inputs, 0)],
        [attend_gain, attend_bias, dense_gain, dense_bias],
        [(wide, 0), (wide, 0)],
        grant=56,
    )

    def by_micro(values):
        return jnp.transpose(values.reshape(head, micro, length), (1, 0, 2)).reshape(-1, length)

    def by_token(values):
        return jnp.transpose(values.reshape(micro, head, length), (1, 0, 2)).reshape(head, count)

    pair_lin = dot(w_pair, attend_in, 0, 1) + jnp.where(first_half, key_bias, value_bias)[:, None]
    pair_mine = by_micro(rotate(pair_lin, pair_cosine, pair_sine).astype(low))
    context = lax.axis_size("ctx")
    for i in range(1, len(stages) - 2):
        up = gather_step(up, up_order[i])
        down = gather_step(down, down_order[i])

    def forward(values, d):
        return lax.ppermute(values, "ctx", [(i, i + d) for i in range(context - d)])

    farthest = forward(pair_mine, reach)
    held = pair_mine
    while held.shape[1] < before:
        held = jnp.concatenate([forward(held, held.shape[1] // length), held], axis=1)
    pair_half = jnp.concatenate([farthest, held], axis=1)
    up = gather_step(up, up_order[-2])
    down = gather_step(down, down_order[-2])
    pair_other = partner(pair_half, ("tp", 1))
    pair = jnp.concatenate(
        [side_half.reshape(micro, head, window) for side_half in halves(pair_half, pair_other)],
        axis=1,
    )

    query_lin = dot(w_query, attend_in, 0, 1) + query_bias[:, None]
    query = (
        rotate(query_lin.reshape(heads, head, count), cosine, sine)
        .astype(low)
        .reshape(query_width, count)
    )
    attended, attended_low, logsum = attend_forward(start, query, pair, before, heads, head)
    w_upward = gather_step(up, up_order[-1])[0].reshape(width, hidden_width)
    w_down = gather_step(down, down_order[-1])[0].reshape(width, hidden_width + query_width)
    w_down, w_output = w_down[:, :hidden_width], w_down[:, hidden_width:]

    grad_low = cotangent.reshape(count, width)
    hidden_pre = dot(dense_in, w_upward, 1, 0) + upward_bias
    normal_cdf = 0.5 * (1.0 + lax.erf(hidden_pre * (1.0 / math.sqrt(2.0))))
    normal_pdf = jnp.exp(-0.5 * hidden_pre * hidden_pre) * (1.0 / math.sqrt(2.0 * math.pi))
    hidden = (hidden_pre * normal_cdf).astype(low)
    slope = normal_cdf + hidden_pre * normal_pdf
    hidden, slope = together(hidden, slope.astype(low))
    pre_grad = (dot(grad_low, w_down, 1, 0) * slope.astype(jnp.float32)).astype(low)

    def by_device(values):
        return values.astype(low).reshape(devices, shard_rows, values.shape[1])

    up_order = side + near + deep[::-1]
    down_order = near + side + deep[::-1]
    up = (by_device(dot(dense_in, pre_grad, 0, 0)), stages)
    row_major = Layout(major_to_minor=(0, 1))

    def term(left, right):
        return with_layout_constraint(dot(left, right, 0, 0).astype(low), row_major)

    cut = hidden_width // 2
    down_terms = term(grad_low, hidden)
    third = jnp.concatenate([down_terms[:, :cut], term(grad_low, attended_low)], axis=1)
    third = by_device(third)
    shape = (lax.axis_size("fsdp"), context // 2, 2) + third.shape[1:]
    third_own, third_gots = deep_send(third.reshape(shape), 1)
    down = (by_device(down_terms[:, cut:]), stages)
    attended_grad = dot(w_output, grad_low, 0, 1).astype(low)
    down, down_got = scatter_send(down, down_order[0])
    attended_grad, up_held = together(attended_grad, up[0])
    up, up_got = scatter_send((up_held, up[1]), up_order[0])
    query_grad, pair_back = attend_backward(
        start, query, pair, attended_grad, attended, logsum, cosine, sine, before, heads, head
    )
    query_grad, pair_back, hidden, pre_grad, grad_late, up_got, down_got, *third_gots = together(
        query_grad, pair_back, hidden, pre_grad, grad_low, up_got, down_got, *third_gots
    )
    third = sum_all([third_own] + third_gots).astype(low)
    third = third.reshape((-1,) + third.shape[2:])
    pair_back = pair_back.reshape(micro, 2, head, window)

    keep, send = halves(pair_back[:, 0], pair_back[:, 1])
    pair_other = partner(send, ("tp", 1))
    asked_order = side + near + deep[::-1]
    asked = by_device(dot(attend_in, query_grad, 0, 0))
    pair_other, asked, hidden, pre_grad, grad_late = together(
        pair_other, asked, hidden, pre_grad, grad_late
    )
    up, up_got = scatter_send(scatter_join(up, up_got), up_order[1])
    down, down_got = scatter_send(scatter_join(down, down_got), down_order[1])
    asked, asked_got = scatter_send((asked, stages), asked_order[0])
    branches = (dot(attended_low, w_output, 1, 1) + dot(hidden, w_down, 1, 1)).astype(low)
    dense_part = dot(pre_grad, w_upward, 1, 1).astype(low)
    early_sums = jnp.concatenate(
        [
            jnp.sum(grad_late.astype(jnp.float32), axis=0),
            jnp.sum(pre_grad.astype(jnp.float32), axis=0),
            jnp.sum(query_grad.astype(jnp.float32), axis=0),
        ]
    )
    summed = (keep.astype(jnp.float32) + pair_other.astype(jnp.float32)).astype(low)
    summed = summed.reshape(micro * head, window)

    def backward(values, d):
        return lax.ppermute(values.astype(low), "ctx", [(i + d, i) for i in range(context - d)])

    held = summed.astype(jnp.float32)
    step = reach // 2
    while step > 1:
        got = backward(held[:, : step * length], step)
        if step == reach // 2:
            got, asked_got, branches, dense_part, early_sums, up_got, down_got = together(
                got, asked_got, branches, dense_part, early_sums, up_got, down_got
            )
        held = held[:, step * length :]
        held = jnp.concatenate(
            [held[:, : step * length] + got.astype(jnp.float32), held[:, step * length :]], axis=1
        )
        step //= 2
    asked, asked_got = scatter_send(scatter_join(asked, asked_got), asked_order[1])
    branches_other = partner(branches, ("tp", 1))
    up = scatter_rest(scatter_join(up, up_got), up_order[2 : -len(deep)])
    down = scatter_rest(scatter_join(down, down_got), down_order[2 : -len(deep)])
    bulk, bulk_gots = deep_send(jnp.concatenate([up[0], down[0]], axis=2), 0)
    gots = [backward(held[:, (2 - d) * length : (3 - d) * length], d) for d in (1, 2)]
    third, asked_got, branches_other, *gots = together(third, asked_got, branches_other, *gots)
    third, third_got = scatter_send((third, side + near), side[0])
    pair_sum = held[:, 2 * length :] + gots[0].astype(jnp.float32) + gots[1].astype(jnp.float32)
    asked, asked_got = scatter_send(scatter_join(asked, asked_got), asked_order[2])
    pair_low = rotate(by_token(pair_sum), pair_cosine, -pair_sine).astype(low)

    shared_rows = 4 * width // LANES + 1
    small_rows = shared_rows + early_sums.shape[0] // LANES
    payload_rows = padded_rows(shard_rows) + padded_rows(small_rows)
    norm_part, payload = by_rows(
        functools.partial(part_kernel, shard_rows),
        "parts",
        256,
        [
            (query_grad, 0),
            (pair_low, 1),
            (w_query, None),
            (w_pair, None),
            (dense_part, 0),
            (inputs, 0),
        ],
        [attend_gain, attend_bias, dense_gain, early_sums.reshape(-1, LANES)],
        [(wide, 0), (jax.ShapeDtypeStruct((devices, payload_rows, LANES), low), None)],
        2 * count * width * (query_width + head),
        scratch=[
            pltpu.VMEM((4, width), jnp.float32),
            pltpu.VMEM((head, width), jnp.float32),
            pltpu.VMEM((head, 1), jnp.float32),
        ],
    )
    payload, norm_part, asked_got, third_got, branches_other, *bulk_gots[:-1] = together(
        payload, norm_part, asked_got, third_got, branches_other, *bulk_gots[:-1]
    )
    third = scatter_rest(scatter_join(third, third_got), side[1:])
    third, third_got = scatter_send(third, near[0])
    got = lax.all_to_all(payload, ("fsdp", "ctx"), 0, 0)
    norm_other = partner(norm_part, ("tp", 1))
    asked = scatter_rest(scatter_join(asked, asked_got), asked_order[3:-1])
    asked, asked_got = scatter_send(asked, asked_order[-1])
    tokens_grad, result = by_rows(
        ends_kernel,
        "ends",
        256,
        [
            (norm_part, 0),
            (norm_other, 0),
            (grad_low, 0),
            (inputs, 0),
            (branches, 0),
            (branches_other, 0),
        ],
        [output_bias, down_bias],
        [(wide, 0), (wide, 0)],
        grant=56,
    )
    got, asked_got, third_got, tokens_grad, result, *bulk_gots = together(
        got, asked_got, third_got, tokens_grad, result, *bulk_gots
    )
    def rows_of(count):
        return jax.ShapeDtypeStruct((count, LANES), jnp.float32)

    sizes = [width // LANES, hidden_width // LANES, query_width // LANES, width // LANES]
    own, out_b, up_b, q_b, down_b = pl.pallas_call(
        functools.partial(sum_kernel, shard_rows, shared_rows),
        out_shape=[rows_of(shard_rows + shared_rows)] + [rows_of(size) for size in sizes],
        name="sums",
    )(got)
    other = partner(own, ("tp", 1))
    terms = [bulk] + bulk_gots + [third[0][0], third_got[0], asked[0][0], asked_got[0]]
    grad_query, grad_out, grad_up, grad_down = pl.pallas_call(
        functools.partial(grads_kernel, cut, hidden_width),
        out_shape=[
            jax.ShapeDtypeStruct((shard_rows, columns), jnp.float32)
            for columns in (query_width, query_width, hidden_width, hidden_width)
        ],
        name="grads",
    )(*terms)
    outs = pl.pallas_call(
        functools.partial(last_kernel, shard_rows, head),
        out_shape=[jax.ShapeDtypeStruct((shard_rows, head), jnp.float32)] * 2
        + [jax.ShapeDtypeStruct((1, head), jnp.float32)] * 2
        + [rows_of(width // LANES)] * 4,
        in_specs=[pl.BlockSpec(memory_space=pltpu.SMEM)] + [pl.BlockSpec(memory_space=pltpu.VMEM)] * 2,
        name="last",
    )(core.astype(jnp.int32).reshape(1), own, other)
    grad_key, grad_value, k_b, v_b = outs[0], outs[1], outs[2].reshape(-1), outs[3].reshape(-1)
    g_gain, g_shift, d_gain, d_shift = [values.reshape(-1) for values in outs[4:]]
    out_b, up_b, q_b, down_b = [values.reshape(-1) for values in (out_b, up_b, q_b, down_b)]
    shape = (micro, 1, length, width)
    return (
        result.reshape(shape),
        tokens_grad.reshape(shape),
        grad_query,
        q_b,
        grad_key,
        k_b,
        grad_value,
        v_b,
        grad_out.T,
        out_b,
        grad_up,
        up_b,
        grad_down.T,
        down_b,
        g_gain,
        g_shift,
        d_gain,
        d_shift,
    )


def solution(mesh):
    return jax.shard_map(
        shards,
        mesh=mesh,
        in_specs=(
            P(None, "fsdp", "ctx", None),
            P(None, "fsdp", "ctx"),
            P(("fsdp", "ctx"), "tp"),
            P("tp"),
            P(("fsdp", "ctx"), None),
            P(),
            P(("fsdp", "ctx"), None),
            P(),
            P("tp", ("fsdp", "ctx")),
            P(),
            P(("fsdp", "ctx"), "tp"),
            P("tp"),
            P("tp", ("fsdp", "ctx")),
            P(),
            P(),
            P(),
            P(),
            P(),
            P(None, "fsdp", "ctx", None),
        ),
        out_specs=(
            P(None, "fsdp", "ctx", None),
            P(None, "fsdp", "ctx", None),
            P(("fsdp", "ctx"), "tp"),
            P("tp"),
            P(("fsdp", "ctx"), None),
            P(),
            P(("fsdp", "ctx"), None),
            P(),
            P("tp", ("fsdp", "ctx")),
            P(),
            P(("fsdp", "ctx"), "tp"),
            P("tp"),
            P("tp", ("fsdp", "ctx")),
            P(),
            P(),
            P(),
            P(),
            P(),
        ),
        check_vma=False,
    )
```
